32 devices in a mesh: rep: 8 (over y, x, core), shard: 4 (over z).
Axes of the slice: x: 2, y: 2, z: 4, core: 2. Of those that a mesh axis runs over, the one named last changes fastest.
Arguments:
- block_input: bfloat16 [32, 384, 576], P(('rep', 'shard')), may hold values from -6 to 6
- segment_ids: int32 [32, 384], P(('rep', 'shard')), may hold values from 0 to 383, as said below
- positions: int32 [32, 384], P(('rep', 'shard')), may hold values from 0 to 383, as said below
- query_weight: bfloat16 [576, 576], P('shard'), may hold values from -0.25 to 0.25
- key_weight: bfloat16 [576, 192], P('shard'), may hold values from -0.25 to 0.25
- value_weight: bfloat16 [576, 192], P('shard'), may hold values from -0.25 to 0.25
- output_weight: bfloat16 [576, 576], P('shard'), may hold values from -0.75 to 0.75
- gate_weight: bfloat16 [576, 1536], P('shard'), may hold values from -0.25 to 0.25
- up_weight: bfloat16 [576, 1536], P('shard'), may hold values from -0.25 to 0.25
- down_weight: bfloat16 [1536, 576], P('shard'), may hold values from -0.15625 to 0.15625
- gain_attn: bfloat16 [576], P('shard'), may hold values from 0.5 to 1.5
- gain_mlp: bfloat16 [576], P('shard'), may hold values from 0.5 to 1.5
- layer_output_cotangent: bfloat16 [32, 384, 576], P(('rep', 'shard')), may hold values from -6 to 6
Outputs:
- block_output: bfloat16 [32, 384, 576], P(('rep', 'shard'))
- input_grad: float32 [32, 384, 576], P(('rep', 'shard'))
- grad_query: float32 [576, 576], P('shard')
- grad_key: float32 [576, 192], P('shard')
- grad_value: float32 [576, 192], P('shard')
- grad_output: float32 [576, 576], P('shard')
- grad_gate: float32 [576, 1536], P('shard')
- grad_up: float32 [576, 1536], P('shard')
- grad_down: float32 [1536, 576], P('shard')
- grad_gain_attn: float32 [576], P('shard')
- grad_gain_mlp: float32 [576], P('shard')
The draws below stay inside these ranges and needn't reach their ends.
Inputs may be any that keep to these rules, and one draw needn't show every extreme that they name: `segment_ids`: in each row the ids start at 0, never fall and rise by at most one from token to token. `positions`: 0 at the first token of a segment, rising by one within it.
All inputs are finite; a program needn't handle non-finite values.
Results may differ from the reference program's by a relative error of at most 0.012.
The reference program's roundings to bfloat16 on the way count: a program that leaves them out, or rounds other values in their place, can miss the bound.
Values may be sent and summed in bfloat16 or wider, within the bound.
No kernel may reach another device: no remote copies, remote signals or barrier semaphores. Data moves between devices by JAX's collectives and lax.ppermute only.
A program may use at most 128 MiB of HBM per device.

```python
import jax
import jax.numpy as jnp
from jax import lax

D = 576
QUERY_HEADS = 9
KEY_VALUE_HEADS = 3
HEAD_WIDTH = 64
FF = 1536
LEN = 384
QW = 576
KVW = 192
SEQS = 32


def packing(key):
    indices = jnp.arange(LEN, dtype=jnp.int32)[None, :]
    row_index = jnp.arange(SEQS, dtype=jnp.int32)[:, None]
    starts = jax.random.randint(jax.random.fold_in(key, 21), (SEQS, LEN), 0, 128) == 0
    starts = jnp.where(row_index == 0, False, starts)
    starts = jnp.where(row_index == SEQS - 1, True, starts)
    starts = jnp.where(indices == 0, True, starts)
    segment = jnp.cumsum(starts.astype(jnp.int32), axis=1) - 1
    first = lax.cummax(jnp.where(starts, indices, 0), axis=1)
    return (segment.astype(jnp.int32), (indices - first).astype(jnp.int32))


def draw_segment_ids(key, part):
    return packing(key)[0]


def draw_positions(key, part):
    return packing(key)[1]


def steps_of(own_key, extent, shards, least, top_value):
    loudness = 1.0
    for dim, parts in shards:
        heights = jax.random.uniform(jax.random.fold_in(jax.random.fold_in(own_key, 6), dim), (parts,), jnp.float32, least / len(shards), top_value / len(shards))
        loudness = loudness * jnp.repeat(jnp.exp(heights), extent[dim] // parts).reshape((-1,) + (1,) * (len(extent) - 1 - dim))
    return loudness


def gaussian(key, extent, spread, limit, shards=(), kind=jnp.bfloat16):
    factor_of = steps_of(key, extent, shards, -0.22, 0.18) if shards else 1.0
    drawn = jax.random.normal(key, extent, jnp.float32) * spread * factor_of
    return jnp.minimum(jnp.maximum(drawn, -limit), limit).astype(kind)


def setup_inputs(seed: int = 0) -> dict:
    streams_of = jax.random.split(jax.random.key(seed), 14)
    block_input = gaussian(streams_of[0], (SEQS, LEN, D), 1.0, 6.0, ((0, 32),))
    segment_ids = draw_segment_ids(jax.random.fold_in(streams_of[13], 71), 0)
    positions = draw_positions(jax.random.fold_in(streams_of[13], 71), 0)
    query_weight = gaussian(streams_of[3], (D, QW), D ** -0.5, 0.25, ((0, 4),))
    key_weight = gaussian(streams_of[4], (D, KVW), D ** -0.5, 0.25, ((0, 4),))
    value_weight = gaussian(streams_of[5], (D, KVW), D ** -0.5, 0.25, ((0, 4),))
    output_weight = gaussian(streams_of[6], (QW, D), HEAD_WIDTH ** -0.5, 0.75, ((0, 4),))
    gate_weight = gaussian(streams_of[7], (D, FF), D ** -0.5, 0.25, ((0, 4),))
    up_weight = gaussian(streams_of[8], (D, FF), D ** -0.5, 0.25, ((0, 4),))
    down_weight = gaussian(streams_of[9], (FF, D), FF ** -0.5, 0.15625, ((0, 4),))
    gain_attn = jnp.clip(1.0 + 0.1 * jax.random.normal(streams_of[10], (D,), jnp.float32), 0.5, 1.5).astype(jnp.bfloat16)
    gain_mlp = jnp.clip(1.0 + 0.1 * jax.random.normal(streams_of[11], (D,), jnp.float32), 0.5, 1.5).astype(jnp.bfloat16)
    layer_output_cotangent = gaussian(streams_of[12], (SEQS, LEN, D), 1.0, 6.0, ((0, 32),))
    return dict(block_input=block_input, segment_ids=segment_ids, positions=positions, query_weight=query_weight, key_weight=key_weight, value_weight=value_weight, output_weight=output_weight, gate_weight=gate_weight, up_weight=up_weight, down_weight=down_weight, gain_attn=gain_attn, gain_mlp=gain_mlp, layer_output_cotangent=layer_output_cotangent)


EPSILON = 1e-05
ROPE_BASE = 100000.0

def product_term(pattern, left_op, right_op):
    return jnp.einsum(pattern, left_op.astype(jnp.float32), right_op.astype(jnp.float32), precision=lax.Precision.HIGHEST)

def norm_stats(values):
    inverse = lax.rsqrt(lax.optimization_barrier(jnp.mean(values * values, axis=-1, keepdims=True)) + EPSILON)
    return (inverse, values * inverse)

def rope_tables(positions):
    half_dim = HEAD_WIDTH // 2
    frequency = ROPE_BASE ** (-(jnp.arange(half_dim, dtype=jnp.float32) * 2.0 / HEAD_WIDTH))
    angles = positions.astype(jnp.float32)[:, :, None] * frequency
    return (jnp.cos(angles)[:, :, None, :], jnp.sin(angles)[:, :, None, :])

def rotate(tensor, cosine_table, sine_table, direction):
    half_dim = HEAD_WIDTH // 2
    first_half = tensor[..., :half_dim]
    second_half = tensor[..., half_dim:]
    return jnp.concatenate([first_half * cosine_table - direction * second_half * sine_table, second_half * cosine_table + direction * first_half * sine_table], axis=-1)

def attention_mask(segment_ids):
    indices = jnp.arange(segment_ids.shape[1])
    causal = indices[:, None] >= indices[None, :]
    same_doc = segment_ids[:, :, None] == segment_ids[:, None, :]
    return (causal[None] & same_doc)[:, None, None]

def score_block(q_rot, k_rot, allowed):
    scores = product_term('sqgrh,skgh->sgrqk', q_rot, k_rot) * HEAD_WIDTH ** (-0.5)
    return jnp.where(allowed, scores, -1e+30)

def forward_pass(weights, block_input, segment_ids, positions):
    query_weight, key_weight, value_weight, output_weight, gate_weight, up_weight, down_weight, gain_attn, gain_mlp = weights
    sequence_count, sequence_length, width = block_input.shape
    group_size = QUERY_HEADS // KEY_VALUE_HEADS
    residual_input = block_input.astype(jnp.float32)
    inv_attn, unit_attn = norm_stats(residual_input)
    attention_normalized = (unit_attn * gain_attn.astype(jnp.float32)).astype(jnp.bfloat16)
    cosine_table, sine_table = rope_tables(positions)
    query_projected = product_term('ifw,wq->ifq', attention_normalized, query_weight).reshape(sequence_count, sequence_length, QUERY_HEADS, HEAD_WIDTH)
    key_projected = product_term('ifw,wq->ifq', attention_normalized, key_weight).reshape(sequence_count, sequence_length, KEY_VALUE_HEADS, HEAD_WIDTH)
    value_projected = product_term('ifw,wq->ifq', attention_normalized, value_weight).reshape(sequence_count, sequence_length, KEY_VALUE_HEADS, HEAD_WIDTH)
    q_rot = rotate(query_projected, cosine_table, sine_table, 1.0).astype(jnp.bfloat16)
    q_rot = q_rot.reshape(sequence_count, sequence_length, KEY_VALUE_HEADS, group_size, HEAD_WIDTH)
    k_rot = rotate(key_projected, cosine_table, sine_table, 1.0).astype(jnp.bfloat16)
    value_b = value_projected.astype(jnp.bfloat16)
    allowed = attention_mask(segment_ids)
    scores = score_block(q_rot, k_rot, allowed)
    row_max = lax.optimization_barrier(jnp.max(scores, axis=-1, keepdims=True))
    log_total = row_max + jnp.log(lax.optimization_barrier(jnp.sum(jnp.exp(scores - row_max), axis=-1, keepdims=True)))
    attn_probs = jnp.exp(scores - log_total).astype(jnp.bfloat16)
    attention_merged = product_term('sgrqk,skgh->sqgrh', attn_probs, value_b).reshape(sequence_count, sequence_length, QW).astype(jnp.bfloat16)
    residual_middle = residual_input + product_term('gwb,ba->gwa', attention_merged, output_weight)
    inv_mlp, unit_mlp = norm_stats(residual_middle)
    feedforward_normalized = (unit_mlp * gain_mlp.astype(jnp.float32)).astype(jnp.bfloat16)
    gate_projected = product_term('qbg,gh->qbh', feedforward_normalized, gate_weight)
    up_projected = product_term('qbg,gh->qbh', feedforward_normalized, up_weight)
    hidden_state = (jax.nn.silu(gate_projected) * up_projected).astype(jnp.bfloat16)
    layer_result = residual_middle + product_term('jbw,wg->jbg', hidden_state, down_weight)
    stored = (inv_attn, unit_attn, attention_normalized, q_rot, k_rot, value_b, log_total, attention_merged, inv_mlp, unit_mlp, feedforward_normalized, gate_projected, up_projected, hidden_state)
    return (layer_result, stored)

def backward_mlp(weights, layer_output_cotangent, stored):
    query_weight, key_weight, value_weight, output_weight, gate_weight, up_weight, down_weight, gain_attn, gain_mlp = weights
    inv_mlp, unit_mlp, feedforward_normalized, gate_projected, up_projected, hidden_state = stored[8:]
    grad_out = layer_output_cotangent.astype(jnp.float32)
    activation_cotangent = product_term('zeo,ho->zeh', layer_output_cotangent, down_weight)
    down_weight_gradient = product_term('bue,bux->ex', hidden_state, layer_output_cotangent)
    gate_sigmoid = jax.nn.sigmoid(gate_projected)
    gate_cotangent = (activation_cotangent * up_projected * gate_sigmoid * (1.0 + gate_projected * (1.0 - gate_sigmoid))).astype(jnp.bfloat16)
    up_cotangent = (activation_cotangent * gate_projected * gate_sigmoid).astype(jnp.bfloat16)
    gate_weight_gradient = product_term('avq,avc->qc', feedforward_normalized, gate_cotangent)
    up_weight_gradient = product_term('avq,avc->qc', feedforward_normalized, up_cotangent)
    normalized_cotangent = product_term('abo,mo->abm', gate_cotangent, gate_weight) + product_term('abo,mo->abm', up_cotangent, up_weight)
    g_gain = lax.optimization_barrier(jnp.sum(normalized_cotangent * unit_mlp, axis=(0, 1)))
    d_unit = normalized_cotangent * gain_mlp.astype(jnp.float32)
    grad_mid = grad_out + inv_mlp * (d_unit - unit_mlp * lax.optimization_barrier(jnp.mean(d_unit * unit_mlp, axis=-1, keepdims=True)))
    return (grad_mid, (gate_weight_gradient, up_weight_gradient, down_weight_gradient, g_gain))

def backward_attention(weights, segment_ids, positions, stored, grad_mid):
    query_weight, key_weight, value_weight, output_weight, gate_weight, up_weight, down_weight, gain_attn, gain_mlp = weights
    inv_attn, unit_attn, attention_normalized, q_rot, k_rot, value_b, log_total, attention_merged = stored[:8]
    sequence_count, sequence_length, width = grad_mid.shape
    group_size = QUERY_HEADS // KEY_VALUE_HEADS
    block_gradient = grad_mid.astype(jnp.bfloat16)
    output_weight_gradient = product_term('uvc,uvn->cn', attention_merged, block_gradient)
    merged_cotangent = product_term('nuw,vw->nuv', block_gradient, output_weight).astype(jnp.bfloat16)
    merged_cotangent = merged_cotangent.reshape(sequence_count, sequence_length, KEY_VALUE_HEADS, group_size, HEAD_WIDTH)
    allowed = attention_mask(segment_ids)
    scores = score_block(q_rot, k_rot, allowed)
    attn_probs = jnp.exp(scores - log_total)
    d_value = product_term('sgrqk,sqgrh->skgh', attn_probs.astype(jnp.bfloat16), merged_cotangent)
    d_prob = product_term('sqgrh,skgh->sgrqk', merged_cotangent, value_b)
    mixed_heads = attention_merged.reshape(sequence_count, sequence_length, KEY_VALUE_HEADS, group_size, HEAD_WIDTH)
    row_delta = lax.optimization_barrier(jnp.sum(merged_cotangent.astype(jnp.float32) * mixed_heads.astype(jnp.float32), axis=-1))
    row_delta = jnp.transpose(row_delta, (0, 2, 3, 1))[..., None]
    d_score = (attn_probs * (d_prob - row_delta) * HEAD_WIDTH ** (-0.5)).astype(jnp.bfloat16)
    d_query = product_term('sgrqk,skgh->sqgrh', d_score, k_rot).reshape(sequence_count, sequence_length, QUERY_HEADS, HEAD_WIDTH)
    d_key = product_term('sgrqk,sqgrh->skgh', d_score, q_rot)
    cosine_table, sine_table = rope_tables(positions)
    query_block_cotangent = rotate(d_query, cosine_table, sine_table, -1.0).astype(jnp.bfloat16).reshape(sequence_count, sequence_length, QW)
    key_block_cotangent = rotate(d_key, cosine_table, sine_table, -1.0).astype(jnp.bfloat16).reshape(sequence_count, sequence_length, KVW)
    value_block_cotangent = d_value.astype(jnp.bfloat16).reshape(sequence_count, sequence_length, KVW)
    query_weight_gradient = product_term('uxj,uxc->jc', attention_normalized, query_block_cotangent)
    key_weight_gradient = product_term('uxj,uxc->jc', attention_normalized, key_block_cotangent)
    value_weight_gradient = product_term('uxj,uxc->jc', attention_normalized, value_block_cotangent)
    normalized_cotangent = product_term('vcm,tm->vct', query_block_cotangent, query_weight) + product_term('vcm,tm->vct', key_block_cotangent, key_weight) + product_term('vcm,tm->vct', value_block_cotangent, value_weight)
    g_gain = lax.optimization_barrier(jnp.sum(normalized_cotangent * unit_attn, axis=(0, 1)))
    d_unit = normalized_cotangent * gain_attn.astype(jnp.float32)
    grad_in = grad_mid + inv_attn * (d_unit - unit_attn * lax.optimization_barrier(jnp.mean(d_unit * unit_attn, axis=-1, keepdims=True)))
    return (grad_in, (query_weight_gradient, key_weight_gradient, value_weight_gradient, output_weight_gradient, g_gain))

def reference(block_input, segment_ids, positions, query_weight, key_weight, value_weight, output_weight, gate_weight, up_weight, down_weight, gain_attn, gain_mlp, layer_output_cotangent):
    weights = (query_weight, key_weight, value_weight, output_weight, gate_weight, up_weight, down_weight, gain_attn, gain_mlp)

    def one_step(totals, step_items):
        one_row, one_segment, one_position, cotangent = step_items
        one_row = one_row[None]
        one_segment = one_segment[None]
        one_position = one_position[None]
        cotangent = cotangent[None]
        layer_result, stored = forward_pass(weights, one_row, one_segment, one_position)
        grad_mid, mlp_grads = backward_mlp(weights, cotangent, stored)
        grad_in, attn_grads = backward_attention(weights, one_segment, one_position, stored, grad_mid)
        grad_terms = attn_grads[:4] + mlp_grads[:3] + (attn_grads[4], mlp_grads[3])
        totals = tuple((total + term for total, term in zip(totals, grad_terms)))
        return (totals, (layer_result[0].astype(jnp.bfloat16), grad_in[0]))
    zeros_init = tuple((jnp.zeros(weight.shape, jnp.float32) for weight in weights))
    totals, (outputs, grads) = lax.scan(one_step, zeros_init, (block_input, segment_ids, positions, layer_output_cotangent))
    return (outputs, grads, totals[0], totals[1], totals[2], totals[3], totals[4], totals[5], totals[6], totals[7], totals[8])
```

```python
import jax
import jax.numpy as jnp
from jax import lax
from jax.sharding import PartitionSpec as P

QUERY_HEADS = 9
KEY_VALUE_HEADS = 3
HEAD_WIDTH = 64


EPSILON = 1e-05
ROPE_BASE = 100000.0


def product_term(pattern, left_op, right_op):
    return jnp.einsum(pattern, left_op, right_op, preferred_element_type=jnp.float32)


def norm_stats(values):
    inverse = lax.rsqrt(jnp.mean(values * values, axis=-1, keepdims=True) + EPSILON)
    return (inverse, values * inverse)


def rope_tables(positions):
    half_dim = HEAD_WIDTH // 2
    frequency = ROPE_BASE ** (-(jnp.arange(half_dim, dtype=jnp.float32) * 2.0 / HEAD_WIDTH))
    angles = positions.astype(jnp.float32)[:, :, None] * frequency
    return (jnp.cos(angles)[:, :, None, :], jnp.sin(angles)[:, :, None, :])


def rotate(tensor, cosine_table, sine_table, direction):
    half_dim = HEAD_WIDTH // 2
    first_half = tensor[..., :half_dim]
    second_half = tensor[..., half_dim:]
    return jnp.concatenate(
        [
            first_half * cosine_table - direction * second_half * sine_table,
            second_half * cosine_table + direction * first_half * sine_table,
        ],
        axis=-1,
    )


def attention_mask(segment_ids):
    indices = jnp.arange(segment_ids.shape[1])
    causal = indices[:, None] >= indices[None, :]
    same_doc = segment_ids[:, :, None] == segment_ids[:, None, :]
    return (causal[None] & same_doc)[:, None, None]


def score_block(q_rot, k_rot, allowed):
    scores = product_term("sqgrh,skgh->sgrqk", q_rot, k_rot) * HEAD_WIDTH ** (-0.5)
    return jnp.where(allowed, scores, -1e30)


def forward_pass(weights, block_input, segment_ids, positions):
    (
        query_weight,
        key_weight,
        value_weight,
        output_weight,
        gate_weight,
        up_weight,
        down_weight,
        gain_attn,
        gain_mlp,
    ) = weights
    sequence_count, sequence_length, width = block_input.shape
    group_size = QUERY_HEADS // KEY_VALUE_HEADS
    q_width = QUERY_HEADS * HEAD_WIDTH
    residual_input = block_input.astype(jnp.float32)
    inv_attn, unit_attn = norm_stats(residual_input)
    attention_normalized = (unit_attn * gain_attn.astype(jnp.float32)).astype(jnp.bfloat16)
    cosine_table, sine_table = rope_tables(positions)
    query_projected = product_term("ifw,wq->ifq", attention_normalized, query_weight).reshape(
        sequence_count, sequence_length, QUERY_HEADS, HEAD_WIDTH
    )
    key_projected = product_term("ifw,wq->ifq", attention_normalized, key_weight).reshape(
        sequence_count, sequence_length, KEY_VALUE_HEADS, HEAD_WIDTH
    )
    value_projected = product_term("ifw,wq->ifq", attention_normalized, value_weight).reshape(
        sequence_count, sequence_length, KEY_VALUE_HEADS, HEAD_WIDTH
    )
    q_rot = rotate(query_projected, cosine_table, sine_table, 1.0).astype(jnp.bfloat16)
    q_rot = q_rot.reshape(sequence_count, sequence_length, KEY_VALUE_HEADS, group_size, HEAD_WIDTH)
    k_rot = rotate(key_projected, cosine_table, sine_table, 1.0).astype(jnp.bfloat16)
    value_b = value_projected.astype(jnp.bfloat16)
    allowed = attention_mask(segment_ids)
    scores = score_block(q_rot, k_rot, allowed)
    row_max = jnp.max(scores, axis=-1, keepdims=True)
    log_total = row_max + jnp.log(jnp.sum(jnp.exp(scores - row_max), axis=-1, keepdims=True))
    attn_probs = jnp.exp(scores - log_total).astype(jnp.bfloat16)
    attention_merged = (
        product_term("sgrqk,skgh->sqgrh", attn_probs, value_b)
        .reshape(sequence_count, sequence_length, q_width)
        .astype(jnp.bfloat16)
    )
    residual_middle = residual_input + product_term("gwb,ba->gwa", attention_merged, output_weight)
    inv_mlp, unit_mlp = norm_stats(residual_middle)
    feedforward_normalized = (unit_mlp * gain_mlp.astype(jnp.float32)).astype(jnp.bfloat16)
    gate_projected = product_term("qbg,gh->qbh", feedforward_normalized, gate_weight)
    up_projected = product_term("qbg,gh->qbh", feedforward_normalized, up_weight)
    hidden_state = (jax.nn.silu(gate_projected) * up_projected).astype(jnp.bfloat16)
    layer_result = residual_middle + product_term("jbw,wg->jbg", hidden_state, down_weight)
    stored = (
        inv_attn,
        unit_attn,
        attention_normalized,
        q_rot,
        k_rot,
        value_b,
        log_total,
        attention_merged,
        inv_mlp,
        unit_mlp,
        feedforward_normalized,
        gate_projected,
        up_projected,
        hidden_state,
    )
    return (layer_result, stored)


def backward_mlp(weights, layer_output_cotangent, stored):
    (
        query_weight,
        key_weight,
        value_weight,
        output_weight,
        gate_weight,
        up_weight,
        down_weight,
        gain_attn,
        gain_mlp,
    ) = weights
    inv_mlp, unit_mlp, feedforward_normalized, gate_projected, up_projected, hidden_state = stored[
        8:
    ]
    grad_out = layer_output_cotangent.astype(jnp.float32)
    activation_cotangent = product_term("zeo,ho->zeh", layer_output_cotangent, down_weight)
    down_weight_gradient = product_term("bux,bue->xe", layer_output_cotangent, hidden_state)
    gate_sigmoid = jax.nn.sigmoid(gate_projected)
    gate_cotangent = (
        activation_cotangent
        * up_projected
        * gate_sigmoid
        * (1.0 + gate_projected * (1.0 - gate_sigmoid))
    ).astype(jnp.bfloat16)
    up_cotangent = (activation_cotangent * gate_projected * gate_sigmoid).astype(jnp.bfloat16)
    gate_weight_gradient = product_term("avq,avc->qc", feedforward_normalized, gate_cotangent)
    up_weight_gradient = product_term("avq,avc->qc", feedforward_normalized, up_cotangent)
    normalized_cotangent = product_term("abo,mo->abm", gate_cotangent, gate_weight) + product_term(
        "abo,mo->abm", up_cotangent, up_weight
    )
    g_gain = jnp.sum(normalized_cotangent * unit_mlp, axis=(0, 1))
    d_unit = normalized_cotangent * gain_mlp.astype(jnp.float32)
    grad_mid = grad_out + inv_mlp * (
        d_unit - unit_mlp * jnp.mean(d_unit * unit_mlp, axis=-1, keepdims=True)
    )
    return (grad_mid, (gate_weight_gradient, up_weight_gradient, down_weight_gradient, g_gain))


def backward_attention(weights, segment_ids, positions, stored, grad_mid):
    (
        query_weight,
        key_weight,
        value_weight,
        output_weight,
        gate_weight,
        up_weight,
        down_weight,
        gain_attn,
        gain_mlp,
    ) = weights
    (
        inv_attn,
        unit_attn,
        attention_normalized,
        q_rot,
        k_rot,
        value_b,
        log_total,
        attention_merged,
    ) = stored[:8]
    sequence_count, sequence_length, width = grad_mid.shape
    group_size = QUERY_HEADS // KEY_VALUE_HEADS
    q_width = QUERY_HEADS * HEAD_WIDTH
    kv_width = KEY_VALUE_HEADS * HEAD_WIDTH
    block_gradient = grad_mid.astype(jnp.bfloat16)
    output_weight_gradient = product_term("uvc,uvn->cn", attention_merged, block_gradient)
    merged_cotangent = product_term("nuw,vw->nuv", block_gradient, output_weight).astype(
        jnp.bfloat16
    )
    merged_cotangent = merged_cotangent.reshape(
        sequence_count, sequence_length, KEY_VALUE_HEADS, group_size, HEAD_WIDTH
    )
    allowed = attention_mask(segment_ids)
    scores = score_block(q_rot, k_rot, allowed)
    attn_probs = jnp.exp(scores - log_total)
    d_value = product_term("sgrqk,sqgrh->skgh", attn_probs.astype(jnp.bfloat16), merged_cotangent)
    d_prob = product_term("sqgrh,skgh->sgrqk", merged_cotangent, value_b)
    mixed_heads = attention_merged.reshape(
        sequence_count, sequence_length, KEY_VALUE_HEADS, group_size, HEAD_WIDTH
    )
    row_delta = jnp.sum(
        merged_cotangent.astype(jnp.float32) * mixed_heads.astype(jnp.float32), axis=-1
    )
    row_delta = jnp.transpose(row_delta, (0, 2, 3, 1))[..., None]
    d_score = (attn_probs * (d_prob - row_delta) * HEAD_WIDTH ** (-0.5)).astype(jnp.bfloat16)
    d_query = product_term("sgrqk,skgh->sqgrh", d_score, k_rot).reshape(
        sequence_count, sequence_length, QUERY_HEADS, HEAD_WIDTH
    )
    d_key = product_term("sgrqk,sqgrh->skgh", d_score, q_rot)
    cosine_table, sine_table = rope_tables(positions)
    query_block_cotangent = (
        rotate(d_query, cosine_table, sine_table, -1.0)
        .astype(jnp.bfloat16)
        .reshape(sequence_count, sequence_length, q_width)
    )
    key_block_cotangent = (
        rotate(d_key, cosine_table, sine_table, -1.0)
        .astype(jnp.bfloat16)
        .reshape(sequence_count, sequence_length, kv_width)
    )
    value_block_cotangent = d_value.astype(jnp.bfloat16).reshape(
        sequence_count, sequence_length, kv_width
    )
    query_weight_gradient = product_term("uxj,uxc->jc", attention_normalized, query_block_cotangent)
    key_weight_gradient = product_term("uxj,uxc->jc", attention_normalized, key_block_cotangent)
    value_weight_gradient = product_term("uxj,uxc->jc", attention_normalized, value_block_cotangent)
    normalized_cotangent = (
        product_term("vcm,tm->vct", query_block_cotangent, query_weight)
        + product_term("vcm,tm->vct", key_block_cotangent, key_weight)
        + product_term("vcm,tm->vct", value_block_cotangent, value_weight)
    )
    g_gain = jnp.sum(normalized_cotangent * unit_attn, axis=(0, 1))
    d_unit = normalized_cotangent * gain_attn.astype(jnp.float32)
    grad_in = grad_mid + inv_attn * (
        d_unit - unit_attn * jnp.mean(d_unit * unit_attn, axis=-1, keepdims=True)
    )
    return (
        grad_in,
        (
            query_weight_gradient,
            key_weight_gradient,
            value_weight_gradient,
            output_weight_gradient,
            g_gain,
        ),
    )


def shifted(values, steps):
    size = lax.axis_size("shard")
    return lax.ppermute(values, "shard", [(i, (i + steps) % size) for i in range(size)])


def piece_of(block):
    copies = lax.axis_size("rep")
    me = lax.axis_index("rep")
    rows, columns = block.shape[0] // 2, block.shape[1] // (copies // 2)
    return lax.dynamic_slice(block, ((me % 2) * rows, (me // 2) * columns), (rows, columns))


def row_piece_of(block):
    copies = lax.axis_size("rep")
    rows = block.shape[0] // copies
    return lax.dynamic_slice_in_dim(block, lax.axis_index("rep") * rows, rows, 0)


def fetch_others(piece):
    size = lax.axis_size("shard")
    return jnp.stack([shifted(piece, k) for k in range(1, size)])


def place_blocks(own, others):
    size = lax.axis_size("shard")
    me = lax.axis_index("shard")
    full = jnp.zeros((size,) + own.shape, own.dtype)
    full = lax.dynamic_update_index_in_dim(full, own, me, 0)
    for k in range(1, size):
        full = lax.dynamic_update_index_in_dim(full, others[k - 1], (me - k) % size, 0)
    return full.reshape((size * own.shape[0],) + own.shape[1:])


def join_pieces(gathered):
    copies = gathered.shape[0]
    lead, rows, columns = gathered.shape[1:]
    parts = gathered.reshape(copies // 2, 2, lead, rows, columns)
    return jnp.transpose(parts, (2, 1, 3, 0, 4)).reshape(lead, 2 * rows, copies // 2 * columns)


def split_pieces(full):
    size = lax.axis_size("shard")
    copies = lax.axis_size("rep")
    rows, columns = full.shape[0] // size // 2, full.shape[1] // (copies // 2)
    parts = full.astype(jnp.bfloat16).reshape(size, 2, rows, copies // 2, columns)
    return jnp.transpose(parts, (3, 1, 0, 2, 4)).reshape(copies, size, rows, columns)


def sum_over_shard(parts):
    size = lax.axis_size("shard")
    me = lax.axis_index("shard")
    total = lax.dynamic_index_in_dim(parts, me, 0, keepdims=False).astype(jnp.float32)
    for k in range(1, size):
        block = lax.dynamic_index_in_dim(parts, (me + k) % size, 0, keepdims=False)
        total = total + shifted(block, k).astype(jnp.float32)
    return total


def gather_weights(q, k, v, o, gate, up, down, gain_attn, gain_mlp):
    rows = q.shape[0]
    attn = jnp.concatenate([q, k, v, o], axis=1)
    attn_piece = piece_of(attn)
    gains = jnp.stack([gain_attn, gain_mlp])
    gains_pad = jnp.pad(gains, ((0, 6), (0, attn_piece.shape[1] - rows)))
    attn_others = fetch_others(jnp.concatenate([attn_piece, gains_pad]))
    half = attn_piece.shape[0]
    gains_full = place_blocks(gains, attn_others[:, half : half + 2, :rows])
    size = lax.axis_size("shard")
    gains_full = jnp.transpose(gains_full.reshape(size, 2, rows), (1, 0, 2)).reshape(2, size * rows)
    attn_gathered = lax.all_gather(attn_others[:, :half], "rep")
    attn_full = place_blocks(attn, join_pieces(attn_gathered))
    gate_piece = piece_of(gate)
    tall = jnp.transpose(down)
    tall_piece = row_piece_of(tall).reshape(gate_piece.shape)
    wide = jnp.stack([gate_piece, piece_of(up), tall_piece])
    wide_gathered = lax.all_gather(fetch_others(wide), "rep")
    gate_full = place_blocks(gate, join_pieces(wide_gathered[:, :, 0]))
    up_full = place_blocks(up, join_pieces(wide_gathered[:, :, 1]))
    tall_rows = jnp.transpose(wide_gathered[:, :, 2], (1, 0, 2, 3)).reshape((-1,) + tall.shape)
    down_full = jnp.transpose(place_blocks(down, jnp.transpose(tall_rows, (0, 2, 1))), (0, 1))
    a, b, c = q.shape[1], k.shape[1], v.shape[1]
    return (
        attn_full[:, :a],
        attn_full[:, a : a + b],
        attn_full[:, a + b : a + b + c],
        attn_full[:, a + b + c :],
        gate_full,
        up_full,
        down_full,
        gains_full[0],
        gains_full[1],
    )


def spread_pieces(piece):
    gathered = lax.all_gather(piece.astype(jnp.bfloat16), "rep")
    return join_pieces(gathered[:, None])[0].astype(jnp.float32)


def reduce_mlp(gate, up, tall):
    size = lax.axis_size("shard")
    copies = lax.axis_size("rep")
    gate_parts = split_pieces(gate)
    tall_parts = tall.astype(jnp.bfloat16).reshape(copies, tall.shape[0] // copies, size, -1)
    tall_parts = jnp.transpose(tall_parts, (0, 2, 1, 3))
    rows, columns = tall_parts.shape[2:]
    wide = jnp.stack([gate_parts, split_pieces(up), tall_parts.reshape(gate_parts.shape)], axis=2)
    shape = wide.shape[1:]
    wide = lax.psum_scatter(wide.reshape(-1, columns), "rep", scatter_dimension=0, tiled=True)
    wide = wide.reshape(shape)
    wide = sum_over_shard(wide).astype(jnp.bfloat16)
    wide = lax.all_gather(wide, "rep").astype(jnp.float32)
    tall_total = wide[:, 2].reshape(copies * rows, columns)
    return (
        join_pieces(wide[:, None, 0])[0],
        join_pieces(wide[:, None, 1])[0],
        jnp.transpose(tall_total),
    )


def reduce_attn(q, k, v, o, gain_attn, gain_mlp):
    size = lax.axis_size("shard")
    copies = lax.axis_size("rep")
    parts = split_pieces(jnp.concatenate([q, k, v, o], axis=1))
    half, columns = parts.shape[2:]
    gains = jnp.stack([gain_attn, gain_mlp]).reshape(2, size, -1).astype(jnp.bfloat16)
    rows = gains.shape[2]
    gains = jnp.pad(jnp.transpose(gains, (1, 0, 2)), ((0, 0), (0, 6), (0, columns - rows)))
    gains = jnp.broadcast_to(gains[None], (copies,) + gains.shape)
    parts = lax.psum_scatter(jnp.concatenate([parts, gains], axis=2), "rep", scatter_dimension=0)
    total = sum_over_shard(parts)
    full = spread_pieces(total[:half])
    a, b, c = q.shape[1], k.shape[1], v.shape[1]
    return (
        full[:, :a],
        full[:, a : a + b],
        full[:, a + b : a + b + c],
        full[:, a + b + c :],
        total[half, :rows],
        total[half + 1, :rows],
    )


def on_device(
    block_input,
    segment_ids,
    positions,
    query_weight,
    key_weight,
    value_weight,
    output_weight,
    gate_weight,
    up_weight,
    down_weight,
    gain_attn,
    gain_mlp,
    layer_output_cotangent,
):
    weights = gather_weights(
        query_weight,
        key_weight,
        value_weight,
        output_weight,
        gate_weight,
        up_weight,
        down_weight,
        gain_attn,
        gain_mlp,
    )
    layer_result, stored = forward_pass(weights, block_input, segment_ids, positions)
    grad_mid, mlp_grads = backward_mlp(weights, layer_output_cotangent, stored)
    gate_total, up_total, down_total = reduce_mlp(*mlp_grads[:3])
    grad_in, attn_grads = backward_attention(weights, segment_ids, positions, stored, grad_mid)
    q_total, k_total, v_total, o_total, gain_attn_total, gain_mlp_total = reduce_attn(
        *attn_grads, mlp_grads[3]
    )
    return (
        layer_result.astype(jnp.bfloat16),
        grad_in,
        q_total,
        k_total,
        v_total,
        o_total,
        gate_total,
        up_total,
        down_total,
        gain_attn_total,
        gain_mlp_total,
    )


def solution(mesh):
    placed = (
        P(("rep", "shard"), None, None),
        P(("rep", "shard"), None),
        P(("rep", "shard"), None),
        P("shard", None),
        P("shard", None),
        P("shard", None),
        P("shard", None),
        P("shard", None),
        P("shard", None),
        P("shard", None),
        P("shard"),
        P("shard"),
        P(("rep", "shard"), None, None),
    )
    return jax.shard_map(
        on_device,
        mesh=mesh,
        in_specs=placed,
        out_specs=(
            P(("rep", "shard"), None, None),
            P(("rep", "shard"), None, None),
            P("shard", None),
            P("shard", None),
            P("shard", None),
            P("shard", None),
            P("shard", None),
            P("shard", None),
            P("shard", None),
            P("shard"),
            P("shard"),
        ),
        check_vma=False,
    )
```

```python
import jax
import jax.numpy as jnp
from jax import lax
from jax.experimental import pallas as pl
from jax.experimental.pallas import tpu as pltpu
from jax.sharding import PartitionSpec as P

QUERY_HEADS = 9
KEY_VALUE_HEADS = 3
HEAD_WIDTH = 64


EPSILON = 1e-05
ROPE_BASE = 100000.0


def product_term(pattern, left_op, right_op):
    return jnp.einsum(pattern, left_op, right_op, preferred_element_type=jnp.float32)


def norm_stats(values):
    inverse = lax.rsqrt(jnp.mean(values * values, axis=-1, keepdims=True) + EPSILON)
    return (inverse, values * inverse)


def rope_tables(positions):
    half_dim = HEAD_WIDTH // 2
    frequency = ROPE_BASE ** (-(jnp.arange(half_dim, dtype=jnp.float32) * 2.0 / HEAD_WIDTH))
    angles = positions.astype(jnp.float32)[:, :, None] * frequency
    return (jnp.cos(angles)[:, :, None, :], jnp.sin(angles)[:, :, None, :])


def rotate(tensor, cosine_table, sine_table, direction):
    half_dim = HEAD_WIDTH // 2
    first_half = tensor[..., :half_dim]
    second_half = tensor[..., half_dim:]
    return jnp.concatenate(
        [
            first_half * cosine_table - direction * second_half * sine_table,
            second_half * cosine_table + direction * first_half * sine_table,
        ],
        axis=-1,
    )


def attention_mask(segment_ids):
    indices = jnp.arange(segment_ids.shape[1])
    causal = indices[:, None] >= indices[None, :]
    same_doc = segment_ids[:, :, None] == segment_ids[:, None, :]
    return (causal[None] & same_doc)[:, None, None]


def score_block(q_rot, k_rot, allowed):
    scores = product_term("sqgrh,skgh->sgrqk", q_rot, k_rot) * HEAD_WIDTH ** (-0.5)
    return jnp.where(allowed, scores, -1e30)


def forward_pass(weights, block_input, segment_ids, positions):
    (
        query_weight,
        key_weight,
        value_weight,
        output_weight,
        gate_weight,
        up_weight,
        down_weight,
        gain_attn,
        gain_mlp,
    ) = weights
    sequence_count, sequence_length, width = block_input.shape
    group_size = QUERY_HEADS // KEY_VALUE_HEADS
    q_width = QUERY_HEADS * HEAD_WIDTH
    residual_input = block_input.astype(jnp.float32)
    inv_attn, unit_attn = norm_stats(residual_input)
    attention_normalized = (unit_attn * gain_attn.astype(jnp.float32)).astype(jnp.bfloat16)
    cosine_table, sine_table = rope_tables(positions)
    query_projected = product_term("ifw,wq->ifq", attention_normalized, query_weight).reshape(
        sequence_count, sequence_length, QUERY_HEADS, HEAD_WIDTH
    )
    key_projected = product_term("ifw,wq->ifq", attention_normalized, key_weight).reshape(
        sequence_count, sequence_length, KEY_VALUE_HEADS, HEAD_WIDTH
    )
    value_projected = product_term("ifw,wq->ifq", attention_normalized, value_weight).reshape(
        sequence_count, sequence_length, KEY_VALUE_HEADS, HEAD_WIDTH
    )
    q_rot = rotate(query_projected, cosine_table, sine_table, 1.0).astype(jnp.bfloat16)
    q_rot = q_rot.reshape(sequence_count, sequence_length, KEY_VALUE_HEADS, group_size, HEAD_WIDTH)
    k_rot = rotate(key_projected, cosine_table, sine_table, 1.0).astype(jnp.bfloat16)
    value_b = value_projected.astype(jnp.bfloat16)
    allowed = attention_mask(segment_ids)
    scores = score_block(q_rot, k_rot, allowed)
    row_max = jnp.max(scores, axis=-1, keepdims=True)
    log_total = row_max + jnp.log(jnp.sum(jnp.exp(scores - row_max), axis=-1, keepdims=True))
    attn_probs = jnp.exp(scores - log_total).astype(jnp.bfloat16)
    attention_merged = (
        product_term("sgrqk,skgh->sqgrh", attn_probs, value_b)
        .reshape(sequence_count, sequence_length, q_width)
        .astype(jnp.bfloat16)
    )
    residual_middle = residual_input + product_term("gwb,ba->gwa", attention_merged, output_weight)
    inv_mlp, unit_mlp = norm_stats(residual_middle)
    feedforward_normalized = (unit_mlp * gain_mlp.astype(jnp.float32)).astype(jnp.bfloat16)
    gate_projected = product_term("qbg,gh->qbh", feedforward_normalized, gate_weight)
    up_projected = product_term("qbg,gh->qbh", feedforward_normalized, up_weight)
    hidden_state = (jax.nn.silu(gate_projected) * up_projected).astype(jnp.bfloat16)
    layer_result = residual_middle + product_term("jbw,wg->jbg", hidden_state, down_weight)
    stored = (
        inv_attn,
        unit_attn,
        attention_normalized,
        q_rot,
        k_rot,
        value_b,
        log_total,
        attention_merged,
        inv_mlp,
        unit_mlp,
        feedforward_normalized,
        gate_projected,
        up_projected,
        hidden_state,
    )
    return (layer_result, stored)


def backward_mlp(weights, layer_output_cotangent, stored):
    (
        query_weight,
        key_weight,
        value_weight,
        output_weight,
        gate_weight,
        up_weight,
        down_weight,
        gain_attn,
        gain_mlp,
    ) = weights
    inv_mlp, unit_mlp, feedforward_normalized, gate_projected, up_projected, hidden_state = stored[
        8:
    ]
    grad_out = layer_output_cotangent.astype(jnp.float32)
    activation_cotangent = product_term("zeo,ho->zeh", layer_output_cotangent, down_weight)
    down_weight_gradient = product_term("bux,bue->xe", layer_output_cotangent, hidden_state)
    gate_sigmoid = jax.nn.sigmoid(gate_projected)
    gate_cotangent = (
        activation_cotangent
        * up_projected
        * gate_sigmoid
        * (1.0 + gate_projected * (1.0 - gate_sigmoid))
    ).astype(jnp.bfloat16)
    up_cotangent = (activation_cotangent * gate_projected * gate_sigmoid).astype(jnp.bfloat16)
    gate_weight_gradient = product_term("avq,avc->qc", feedforward_normalized, gate_cotangent)
    up_weight_gradient = product_term("avq,avc->qc", feedforward_normalized, up_cotangent)
    normalized_cotangent = product_term("abo,mo->abm", gate_cotangent, gate_weight) + product_term(
        "abo,mo->abm", up_cotangent, up_weight
    )
    g_gain = jnp.sum(normalized_cotangent * unit_mlp, axis=(0, 1))
    d_unit = normalized_cotangent * gain_mlp.astype(jnp.float32)
    grad_mid = grad_out + inv_mlp * (
        d_unit - unit_mlp * jnp.mean(d_unit * unit_mlp, axis=-1, keepdims=True)
    )
    return (grad_mid, (gate_weight_gradient, up_weight_gradient, down_weight_gradient, g_gain))


def backward_attention(weights, segment_ids, positions, stored, grad_mid):
    (
        query_weight,
        key_weight,
        value_weight,
        output_weight,
        gate_weight,
        up_weight,
        down_weight,
        gain_attn,
        gain_mlp,
    ) = weights
    (
        inv_attn,
        unit_attn,
        attention_normalized,
        q_rot,
        k_rot,
        value_b,
        log_total,
        attention_merged,
    ) = stored[:8]
    sequence_count, sequence_length, width = grad_mid.shape
    group_size = QUERY_HEADS // KEY_VALUE_HEADS
    q_width = QUERY_HEADS * HEAD_WIDTH
    kv_width = KEY_VALUE_HEADS * HEAD_WIDTH
    block_gradient = grad_mid.astype(jnp.bfloat16)
    output_weight_gradient = product_term("uvc,uvn->cn", attention_merged, block_gradient)
    merged_cotangent = product_term("nuw,vw->nuv", block_gradient, output_weight).astype(
        jnp.bfloat16
    )
    merged_cotangent = merged_cotangent.reshape(
        sequence_count, sequence_length, KEY_VALUE_HEADS, group_size, HEAD_WIDTH
    )
    allowed = attention_mask(segment_ids)
    scores = score_block(q_rot, k_rot, allowed)
    attn_probs = jnp.exp(scores - log_total)
    d_value = product_term("sgrqk,sqgrh->skgh", attn_probs.astype(jnp.bfloat16), merged_cotangent)
    d_prob = product_term("sqgrh,skgh->sgrqk", merged_cotangent, value_b)
    mixed_heads = attention_merged.reshape(
        sequence_count, sequence_length, KEY_VALUE_HEADS, group_size, HEAD_WIDTH
    )
    row_delta = jnp.sum(
        merged_cotangent.astype(jnp.float32) * mixed_heads.astype(jnp.float32), axis=-1
    )
    row_delta = jnp.transpose(row_delta, (0, 2, 3, 1))[..., None]
    d_score = (attn_probs * (d_prob - row_delta) * HEAD_WIDTH ** (-0.5)).astype(jnp.bfloat16)
    d_query = product_term("sgrqk,skgh->sqgrh", d_score, k_rot).reshape(
        sequence_count, sequence_length, QUERY_HEADS, HEAD_WIDTH
    )
    d_key = product_term("sgrqk,sqgrh->skgh", d_score, q_rot)
    cosine_table, sine_table = rope_tables(positions)
    query_block_cotangent = (
        rotate(d_query, cosine_table, sine_table, -1.0)
        .astype(jnp.bfloat16)
        .reshape(sequence_count, sequence_length, q_width)
    )
    key_block_cotangent = (
        rotate(d_key, cosine_table, sine_table, -1.0)
        .astype(jnp.bfloat16)
        .reshape(sequence_count, sequence_length, kv_width)
    )
    value_block_cotangent = d_value.astype(jnp.bfloat16).reshape(
        sequence_count, sequence_length, kv_width
    )
    query_weight_gradient = product_term("uxj,uxc->jc", attention_normalized, query_block_cotangent)
    key_weight_gradient = product_term("uxj,uxc->jc", attention_normalized, key_block_cotangent)
    value_weight_gradient = product_term("uxj,uxc->jc", attention_normalized, value_block_cotangent)
    normalized_cotangent = (
        product_term("vcm,tm->vct", query_block_cotangent, query_weight)
        + product_term("vcm,tm->vct", key_block_cotangent, key_weight)
        + product_term("vcm,tm->vct", value_block_cotangent, value_weight)
    )
    g_gain = jnp.sum(normalized_cotangent * unit_attn, axis=(0, 1))
    d_unit = normalized_cotangent * gain_attn.astype(jnp.float32)
    grad_in = grad_mid + inv_attn * (
        d_unit - unit_attn * jnp.mean(d_unit * unit_attn, axis=-1, keepdims=True)
    )
    return (
        grad_in,
        (
            query_weight_gradient,
            key_weight_gradient,
            value_weight_gradient,
            output_weight_gradient,
            g_gain,
        ),
    )


def shifted(values, steps):
    size = lax.axis_size("shard")
    return lax.ppermute(values, "shard", [(i, (i + steps) % size) for i in range(size)])


def piece_of(block):
    copies = lax.axis_size("rep")
    me = lax.axis_index("rep")
    rows, columns = block.shape[0] // 2, block.shape[1] // (copies // 2)
    return lax.dynamic_slice(block, ((me % 2) * rows, (me // 2) * columns), (rows, columns))


def row_piece_of(block):
    copies = lax.axis_size("rep")
    rows = block.shape[0] // copies
    return lax.dynamic_slice_in_dim(block, lax.axis_index("rep") * rows, rows, 0)


def fetch_others(piece):
    size = lax.axis_size("shard")
    return jnp.stack([shifted(piece, k) for k in range(1, size)])


def place_blocks(own, others):
    size = lax.axis_size("shard")
    me = lax.axis_index("shard")
    full = jnp.zeros((size,) + own.shape, own.dtype)
    full = lax.dynamic_update_index_in_dim(full, own, me, 0)
    for k in range(1, size):
        full = lax.dynamic_update_index_in_dim(full, others[k - 1], (me - k) % size, 0)
    return full.reshape((size * own.shape[0],) + own.shape[1:])


def join_pieces(gathered):
    copies = gathered.shape[0]
    lead, rows, columns = gathered.shape[1:]
    parts = gathered.reshape(copies // 2, 2, lead, rows, columns)
    return jnp.transpose(parts, (2, 1, 3, 0, 4)).reshape(lead, 2 * rows, copies // 2 * columns)


def split_pieces(full):
    size = lax.axis_size("shard")
    copies = lax.axis_size("rep")
    rows, columns = full.shape[0] // size // 2, full.shape[1] // (copies // 2)
    parts = full.astype(jnp.bfloat16).reshape(size, 2, rows, copies // 2, columns)
    return jnp.transpose(parts, (3, 1, 0, 2, 4)).reshape(copies, size, rows, columns)


def sum_over_shard(parts):
    size = lax.axis_size("shard")
    me = lax.axis_index("shard")
    total = lax.dynamic_index_in_dim(parts, me, 0, keepdims=False).astype(jnp.float32)
    for k in range(1, size):
        block = lax.dynamic_index_in_dim(parts, (me + k) % size, 0, keepdims=False)
        total = total + shifted(block, k).astype(jnp.float32)
    return total


def gather_weights(q, k, v, o, gate, up, down, gain_attn, gain_mlp):
    rows = q.shape[0]
    attn = jnp.concatenate([q, k, v, o], axis=1)
    attn_piece = piece_of(attn)
    gains = jnp.stack([gain_attn, gain_mlp])
    gains_pad = jnp.pad(gains, ((0, 6), (0, attn_piece.shape[1] - rows)))
    attn_others = fetch_others(jnp.concatenate([attn_piece, gains_pad]))
    half = attn_piece.shape[0]
    gains_full = place_blocks(gains, attn_others[:, half : half + 2, :rows])
    size = lax.axis_size("shard")
    gains_full = jnp.transpose(gains_full.reshape(size, 2, rows), (1, 0, 2)).reshape(2, size * rows)
    attn_gathered = lax.all_gather(attn_others[:, :half], "rep")
    attn_full = place_blocks(attn, join_pieces(attn_gathered))
    gate_piece = piece_of(gate)
    tall = jnp.transpose(down)
    tall_piece = row_piece_of(tall).reshape(gate_piece.shape)
    wide = jnp.stack([gate_piece, piece_of(up), tall_piece])
    wide_gathered = lax.all_gather(fetch_others(wide), "rep")
    gate_full = place_blocks(gate, join_pieces(wide_gathered[:, :, 0]))
    up_full = place_blocks(up, join_pieces(wide_gathered[:, :, 1]))
    tall_rows = jnp.transpose(wide_gathered[:, :, 2], (1, 0, 2, 3)).reshape((-1,) + tall.shape)
    down_full = jnp.transpose(place_blocks(down, jnp.transpose(tall_rows, (0, 2, 1))), (0, 1))
    a, b, c = q.shape[1], k.shape[1], v.shape[1]
    return (
        attn_full[:, :a],
        attn_full[:, a : a + b],
        attn_full[:, a + b : a + b + c],
        attn_full[:, a + b + c :],
        gate_full,
        up_full,
        down_full,
        gains_full[0],
        gains_full[1],
    )


def spread_pieces(piece):
    gathered = lax.all_gather(piece.astype(jnp.bfloat16), "rep")
    return join_pieces(gathered[:, None])[0].astype(jnp.float32)


def reduce_mlp(gate, up, tall):
    size = lax.axis_size("shard")
    copies = lax.axis_size("rep")
    gate_parts = split_pieces(gate)
    tall_parts = tall.astype(jnp.bfloat16).reshape(copies, tall.shape[0] // copies, size, -1)
    tall_parts = jnp.transpose(tall_parts, (0, 2, 1, 3))
    rows, columns = tall_parts.shape[2:]
    wide = jnp.stack([gate_parts, split_pieces(up), tall_parts.reshape(gate_parts.shape)], axis=2)
    shape = wide.shape[1:]
    wide = lax.psum_scatter(wide.reshape(-1, columns), "rep", scatter_dimension=0, tiled=True)
    wide = wide.reshape(shape)
    wide = sum_over_shard(wide).astype(jnp.bfloat16)
    wide = lax.all_gather(wide, "rep").astype(jnp.float32)
    tall_total = wide[:, 2].reshape(copies * rows, columns)
    return (
        join_pieces(wide[:, None, 0])[0],
        join_pieces(wide[:, None, 1])[0],
        jnp.transpose(tall_total),
    )


def reduce_attn(q, k, v, o, gain_attn, gain_mlp):
    size = lax.axis_size("shard")
    copies = lax.axis_size("rep")
    parts = split_pieces(jnp.concatenate([q, k, v, o], axis=1))
    half, columns = parts.shape[2:]
    gains = jnp.stack([gain_attn, gain_mlp]).reshape(2, size, -1).astype(jnp.bfloat16)
    rows = gains.shape[2]
    gains = jnp.pad(jnp.transpose(gains, (1, 0, 2)), ((0, 0), (0, 6), (0, columns - rows)))
    gains = jnp.broadcast_to(gains[None], (copies,) + gains.shape)
    parts = lax.psum_scatter(jnp.concatenate([parts, gains], axis=2), "rep", scatter_dimension=0)
    total = sum_over_shard(parts)
    full = spread_pieces(total[:half])
    a, b, c = q.shape[1], k.shape[1], v.shape[1]
    return (
        full[:, :a],
        full[:, a : a + b],
        full[:, a + b : a + b + c],
        full[:, a + b + c :],
        total[half, :rows],
        total[half + 1, :rows],
    )


def on_device_generic(
    block_input,
    segment_ids,
    positions,
    query_weight,
    key_weight,
    value_weight,
    output_weight,
    gate_weight,
    up_weight,
    down_weight,
    gain_attn,
    gain_mlp,
    layer_output_cotangent,
):
    weights = gather_weights(
        query_weight,
        key_weight,
        value_weight,
        output_weight,
        gate_weight,
        up_weight,
        down_weight,
        gain_attn,
        gain_mlp,
    )
    layer_result, stored = forward_pass(weights, block_input, segment_ids, positions)
    grad_mid, mlp_grads = backward_mlp(weights, layer_output_cotangent, stored)
    gate_total, up_total, down_total = reduce_mlp(*mlp_grads[:3])
    grad_in, attn_grads = backward_attention(weights, segment_ids, positions, stored, grad_mid)
    q_total, k_total, v_total, o_total, gain_attn_total, gain_mlp_total = reduce_attn(
        *attn_grads, mlp_grads[3]
    )
    return (
        layer_result.astype(jnp.bfloat16),
        grad_in,
        q_total,
        k_total,
        v_total,
        o_total,
        gate_total,
        up_total,
        down_total,
        gain_attn_total,
        gain_mlp_total,
    )


TOKENS = 384
CHUNK = 384
GROUPS = KEY_VALUE_HEADS
SHARE = QUERY_HEADS // KEY_VALUE_HEADS
VMEM_LIMIT = 56 * 1024 * 1024


def dot(left, right, left_dim=1, right_dim=0):
    return lax.dot_general(
        left, right, (((left_dim,), (right_dim,)), ((), ())), preferred_element_type=jnp.float32
    )


def widen(values):
    return values.astype(jnp.float32)


def narrow(values):
    return values.astype(jnp.bfloat16)


def mask_bias(seg_col, seg_row):
    shape = (TOKENS, TOKENS)
    key_at = lax.broadcasted_iota(jnp.int32, shape, 0)
    query_at = lax.broadcasted_iota(jnp.int32, shape, 1)
    allowed = (key_at <= query_at) & (seg_col == seg_row)
    return jnp.where(allowed, 0.0, -1e30)


def turn(values, cosine, sine):
    half = HEAD_WIDTH // 2
    first, second = values[:half], values[half:]
    return jnp.concatenate(
        [first * cosine - second * sine, second * cosine + first * sine], axis=0
    )


def attention_forward_kernel(
    shards, z_ref, x_ref, col_ref, row_ref, cos_ref, sin_ref, own_ref, gain_own_ref, others_ref,
    w_ref, gain_ref, x2_ref, q_ref, k_ref, v_ref, o_ref, lse_ref, bias_ref,
):
    z = z_ref[0]
    rows = own_ref.shape[0]
    half = rows // 2
    width = x_ref.shape[1]
    own_at = pl.multiple_of(z * rows, 16)
    w_ref[pl.ds(own_at, rows), :] = own_ref[...]
    gains = widen(gain_own_ref[...])
    for k in range(1, shards):
        at = pl.multiple_of(lax.rem(z + shards - k, shards) * rows, 16)
        gains = gains + widen(others_ref[0, k - 1, half:])
        for c in range(own_ref.shape[1] // CHUNK):
            pieces = [widen(others_ref[2 * c + h, k - 1, :half]) for h in range(2)]
            w_ref[pl.ds(at, rows), c * CHUNK : (c + 1) * CHUNK] = narrow(
                jnp.concatenate(pieces, axis=0)
            )
    tail = width - CHUNK
    gain_attn = jnp.concatenate([gains[0:1], gains[1:2, :tail]], axis=1)
    gain_mlp = jnp.concatenate([gains[2:3], gains[3:4, :tail]], axis=1)
    gain_ref[0:1, :] = gain_attn
    gain_ref[1:2, :] = gain_mlp
    x = widen(x_ref[...])
    inverse = lax.rsqrt(jnp.mean(x * x, axis=-1, keepdims=True) + EPSILON)
    h1 = narrow(x * inverse * gain_attn)
    kv = jnp.transpose(dot(h1, w_ref[:, :CHUNK]))
    q = jnp.transpose(dot(h1, w_ref[:, 896:]))[HEAD_WIDTH:]
    cosine, sine = cos_ref[...], sin_ref[...]
    bias_ref[...] = mask_bias(col_ref[...], row_ref[...])
    for g in range(GROUPS):
        at = g * HEAD_WIDTH
        k_ref[g] = narrow(turn(kv[at : at + HEAD_WIDTH], cosine, sine))
        at = (GROUPS + g) * HEAD_WIDTH
        v_ref[g] = narrow(kv[at : at + HEAD_WIDTH])
        for r in range(SHARE):
            at = (g * SHARE + r) * HEAD_WIDTH
            q_ref[g, :, r * TOKENS : (r + 1) * TOKENS] = narrow(
                turn(q[at : at + HEAD_WIDTH], cosine, sine)
            )

    def one_group(g, carry):
        scores = dot(k_ref[g], q_ref[g], 0, 0) * HEAD_WIDTH ** (-0.5)
        bias = bias_ref[...]
        scores = scores + jnp.concatenate([bias] * SHARE, axis=1)
        top = jnp.max(scores, axis=0, keepdims=True)
        weight = jnp.exp(scores - top)
        total = jnp.sum(weight, axis=0, keepdims=True)
        lse_ref[g] = top + jnp.log(total)
        probs = narrow(weight * (1.0 / total))
        o_ref[g] = narrow(dot(v_ref[g], probs))
        return carry

    lax.fori_loop(0, GROUPS, one_group, 0)
    x2_ref[...] = x + dot(joined_heads(o_ref), w_ref[:, CHUNK : CHUNK + width], 0, 0)


def joined_heads(ref):
    return jnp.concatenate(
        [
            ref[g, :, r * TOKENS : (r + 1) * TOKENS]
            for g in range(GROUPS)
            for r in range(SHARE)
        ],
        axis=0,
    )


def attention_forward(z, x, col, row, cosine, sine, own, gain_own, others, shards):
    width = x.shape[1]
    cells = SHARE * TOKENS
    bf16, f32 = jnp.bfloat16, jnp.float32

    def kernel(*refs):
        attention_forward_kernel(shards, *refs)

    return pl.pallas_call(
        kernel,
        grid_spec=pltpu.PrefetchScalarGridSpec(
            num_scalar_prefetch=1,
            grid=(),
            in_specs=[pl.BlockSpec(memory_space=pltpu.VMEM)] * 8,
            out_specs=[pl.BlockSpec(memory_space=pltpu.VMEM)] * 8,
            scratch_shapes=[pltpu.VMEM((TOKENS, TOKENS), f32)],
        ),
        out_shape=[
            jax.ShapeDtypeStruct((shards * own.shape[0], own.shape[1]), bf16),
            jax.ShapeDtypeStruct((8, width), f32),
            jax.ShapeDtypeStruct((TOKENS, width), f32),
            jax.ShapeDtypeStruct((GROUPS, HEAD_WIDTH, cells), bf16),
            jax.ShapeDtypeStruct((GROUPS, HEAD_WIDTH, TOKENS), bf16),
            jax.ShapeDtypeStruct((GROUPS, HEAD_WIDTH, TOKENS), bf16),
            jax.ShapeDtypeStruct((GROUPS, HEAD_WIDTH, cells), bf16),
            jax.ShapeDtypeStruct((GROUPS, 1, cells), f32),
        ],
        compiler_params=pltpu.CompilerParams(vmem_limit_bytes=VMEM_LIMIT),
        cost_estimate=pl.CostEstimate(
            flops=int(1.5e9), bytes_accessed=8000000, transcendentals=2000000
        ),
        name="attention_forward",
    )(z, x, col, row, cosine, sine, own, gain_own, others)


def mlp_kernel(
    shards, z_ref, x2_ref, ct_ref, gain_ref, gate_ref, up_ref, tall_ref, wide_ref, tall_other_ref,
    out_ref, dx2_ref, gain_grad_ref, grad_ref,
    u2_ref, h2_ref, h2t_ref, ctt_ref, acc_ref, dh2_ref, wg_ref, wu_ref, wd_ref,
):
    z = z_ref[0]
    j = pl.program_id(0)
    rows = gate_ref.shape[0]
    half = rows // 2

    @pl.when(j == 0)
    def _():
        x2 = x2_ref[...]
        inverse = lax.rsqrt(jnp.mean(x2 * x2, axis=-1, keepdims=True) + EPSILON)
        u2 = x2 * inverse
        u2_ref[...] = u2
        h2 = narrow(u2 * gain_ref[1:2, :])
        h2_ref[...] = h2
        h2t_ref[...] = narrow(jnp.transpose(widen(h2)))
        ctt_ref[...] = narrow(jnp.transpose(widen(ct_ref[...])))
        acc_ref[...] = x2
        dh2_ref[...] = jnp.zeros_like(dh2_ref)

    own_at = pl.multiple_of(z * rows, 16)
    wg_ref[pl.ds(own_at, rows), :] = gate_ref[...]
    wu_ref[pl.ds(own_at, rows), :] = up_ref[...]
    for k in range(1, shards):
        at = pl.multiple_of(lax.rem(z + shards - k, shards) * rows, 16)
        for m, ref in ((0, wg_ref), (1, wu_ref)):
            pieces = [widen(wide_ref[h, k - 1, m]) for h in range(2)]
            ref[pl.ds(at, rows), :] = narrow(jnp.concatenate(pieces, axis=0))

    @pl.when(j == z)
    def _():
        wd_ref[...] = tall_ref[...]

    @pl.when(j != z)
    def _():
        pieces = [widen(tall_other_ref[r, 0, 0]) for r in range(tall_other_ref.shape[0])]
        wd_ref[...] = narrow(jnp.concatenate(pieces, axis=0))

    h2, ct = h2_ref[...], ct_ref[...]
    wg, wu, wd = wg_ref[...], wu_ref[...], wd_ref[...]
    gate, up = dot(h2, wg), dot(h2, wu)
    da = dot(ct, wd)
    sigmoid = 1.0 / (1.0 + jnp.exp(-gate))
    silu = gate * sigmoid
    act = narrow(silu * up)
    dg = narrow(da * up * sigmoid * (1.0 + gate * (1.0 - sigmoid)))
    du = narrow(da * silu)
    acc_ref[...] += dot(act, wd, 1, 1)
    dh2_ref[...] += dot(dg, wg, 1, 1) + dot(du, wu, 1, 1)
    for m, grad in ((0, dot(h2t_ref[...], dg)), (1, dot(h2t_ref[...], du))):
        for b in range(shards):
            for h in range(2):
                at = b * rows + h * half
                grad_ref[2 * j + h, b, m] = narrow(grad[at : at + half])
    grad = dot(ctt_ref[...], act)
    for r in range(2 * shards):
        grad_ref[r, j, 2] = narrow(grad[r * half : (r + 1) * half])

    @pl.when(j == pl.num_programs(0) - 1)
    def _():
        out_ref[...] = narrow(acc_ref[...])
        dh2, u2, x2 = dh2_ref[...], u2_ref[...], x2_ref[...]
        inverse = lax.rsqrt(jnp.mean(x2 * x2, axis=-1, keepdims=True) + EPSILON)
        gain_grad_ref[0:1, :] = jnp.sum(dh2 * u2, axis=0, keepdims=True)
        n2 = dh2 * gain_ref[1:2, :]
        mean = jnp.mean(n2 * u2, axis=-1, keepdims=True)
        dx2_ref[...] = widen(ct_ref[...]) + inverse * (n2 - u2 * mean)


def mlp(z, x2, ct, gains, gate, up, tall, gathered, shards):
    width = x2.shape[1]
    copies = gathered.shape[0]
    rows, ff = gate.shape
    half = rows // 2
    bf16, f32 = jnp.bfloat16, jnp.float32

    def kernel(*refs):
        mlp_kernel(shards, *refs)

    def tall_block(j, z_ref):
        return (0, jnp.maximum(lax.rem(z_ref[0] + shards - j, shards) - 1, 0), 2, 0, 0)

    whole = lambda shape: pl.BlockSpec(shape, lambda j, z_ref: (0,) * len(shape))
    return pl.pallas_call(
        kernel,
        grid_spec=pltpu.PrefetchScalarGridSpec(
            num_scalar_prefetch=1,
            grid=(ff // CHUNK,),
            in_specs=[
                whole((TOKENS, width)),
                whole((TOKENS, width)),
                whole((8, width)),
                pl.BlockSpec((rows, CHUNK), lambda j, z_ref: (0, j)),
                pl.BlockSpec((rows, CHUNK), lambda j, z_ref: (0, j)),
                whole((width, CHUNK)),
                pl.BlockSpec((2, shards - 1, 2, half, CHUNK), lambda j, z_ref: (j, 0, 0, 0, 0)),
                pl.BlockSpec((copies, 1, 1, half, CHUNK), tall_block),
            ],
            out_specs=[
                whole((TOKENS, width)),
                whole((TOKENS, width)),
                whole((8, width)),
                whole((copies, shards, 3, half, CHUNK)),
            ],
            scratch_shapes=[
                pltpu.VMEM((TOKENS, width), f32),
                pltpu.VMEM((TOKENS, width), bf16),
                pltpu.VMEM((width, TOKENS), bf16),
                pltpu.VMEM((width, TOKENS), bf16),
                pltpu.VMEM((TOKENS, width), f32),
                pltpu.VMEM((TOKENS, width), f32),
                pltpu.VMEM((width, CHUNK), bf16),
                pltpu.VMEM((width, CHUNK), bf16),
                pltpu.VMEM((width, CHUNK), bf16),
            ],
        ),
        out_shape=[
            jax.ShapeDtypeStruct((TOKENS, width), bf16),
            jax.ShapeDtypeStruct((TOKENS, width), f32),
            jax.ShapeDtypeStruct((8, width), f32),
            jax.ShapeDtypeStruct((copies, shards, 3, half, CHUNK), bf16),
        ],
        compiler_params=pltpu.CompilerParams(
            vmem_limit_bytes=VMEM_LIMIT, dimension_semantics=("arbitrary",)
        ),
        cost_estimate=pl.CostEstimate(
            flops=int(6.2e9), bytes_accessed=14000000, transcendentals=1200000
        ),
        name="mlp",
    )(z, x2, ct, gains, gate, up, tall, gathered, gathered)


def attention_backward_kernel(
    shards, x_ref, dx2_ref, col_ref, row_ref, cos_ref, sin_ref, w_ref, gain_ref, q_ref, k_ref,
    v_ref, o_ref, lse_ref, gain_grad_ref,
    dx_ref, grad_ref,
    bias_ref, do_ref, dq_ref, dk_ref, dv_ref,
):
    width = x_ref.shape[1]
    rows = width // shards
    half = rows // 2
    x = widen(x_ref[...])
    inverse = lax.rsqrt(jnp.mean(x * x, axis=-1, keepdims=True) + EPSILON)
    u1 = x * inverse
    gain_attn = gain_ref[0:1, :]
    h1t = narrow(jnp.transpose(u1 * gain_attn))
    gx = narrow(dx2_ref[...])
    cosine, sine = cos_ref[...], sin_ref[...]
    bias_ref[...] = mask_bias(col_ref[...], row_ref[...])
    do = narrow(dot(w_ref[:, CHUNK : CHUNK + width], gx, 1, 1))
    for g in range(GROUPS):
        for r in range(SHARE):
            at = (g * SHARE + r) * HEAD_WIDTH
            do_ref[g, :, r * TOKENS : (r + 1) * TOKENS] = do[at : at + HEAD_WIDTH]

    def one_group(g, carry):
        bias = bias_ref[...]
        scores = dot(k_ref[g], q_ref[g], 0, 0) * HEAD_WIDTH ** (-0.5)
        scores = scores + jnp.concatenate([bias] * SHARE, axis=1)
        probs = jnp.exp(scores - lse_ref[g])
        do_g = do_ref[g]
        dv_ref[g] = jnp.transpose(dot(narrow(probs), do_g, 1, 1))
        delta = jnp.sum(widen(do_g) * widen(o_ref[g]), axis=0, keepdims=True)
        dp = dot(v_ref[g], do_g, 0, 0)
        ds = narrow(probs * (dp - delta) * HEAD_WIDTH ** (-0.5))
        dq_ref[g] = dot(k_ref[g], ds)
        dk_ref[g] = jnp.transpose(dot(ds, q_ref[g], 1, 1))
        return carry

    lax.fori_loop(0, GROUPS, one_group, 0)
    dkv = [narrow(turn(dk_ref[g], cosine, -sine)) for g in range(GROUPS)]
    dkv = jnp.concatenate(dkv + [narrow(dv_ref[g]) for g in range(GROUPS)], axis=0)
    dq = [
        narrow(turn(dq_ref[g, :, r * TOKENS : (r + 1) * TOKENS], cosine, -sine))
        for g in range(GROUPS)
        for r in range(SHARE)
    ]
    zeros = jnp.zeros((HEAD_WIDTH, TOKENS), jnp.bfloat16)
    dq_padded = jnp.concatenate([zeros] + dq, axis=0)
    dq = jnp.concatenate(dq, axis=0)
    dh1 = jnp.transpose(dot(w_ref[:, :CHUNK], dkv) + dot(w_ref[:, 896:], dq_padded))
    gain_grad = jnp.sum(dh1 * u1, axis=0, keepdims=True)
    n1 = dh1 * gain_attn
    mean = jnp.mean(n1 * u1, axis=-1, keepdims=True)
    dx_ref[...] = dx2_ref[...] + inverse * (n1 - u1 * mean)
    gain_mlp_grad = gain_grad_ref[0:1, :]
    tail = width - CHUNK
    blank = jnp.zeros((1, CHUNK - tail), jnp.float32)
    extra = jnp.concatenate(
        [
            gain_grad[:, :CHUNK],
            jnp.concatenate([gain_grad[:, CHUNK:], blank], axis=1),
            gain_mlp_grad[:, :CHUNK],
            jnp.concatenate([gain_mlp_grad[:, CHUNK:], blank], axis=1),
            jnp.zeros((4, CHUNK), jnp.float32),
        ],
        axis=0,
    )
    o = joined_heads(o_ref)
    for c in range(4):
        if c == 0:
            grad = dot(h1t, dkv, 1, 1)
        elif c == 1:
            grad = dot(o, gx[:, :CHUNK])
        elif c == 2:
            grad = jnp.concatenate(
                [dot(o, gx[:, CHUNK:]), dot(h1t, dq[: CHUNK - tail], 1, 1)], axis=1
            )
        else:
            grad = dot(h1t, dq[CHUNK - tail :], 1, 1)
        for b in range(shards):
            for h in range(2):
                at = b * rows + h * half
                grad_ref[2 * c + h, b] = narrow(
                    jnp.concatenate([grad[at : at + half], extra], axis=0)
                )


def attention_backward(args, shards, copies):
    x = args[0]
    width = x.shape[1]
    half = width // shards // 2
    cells = SHARE * TOKENS
    bf16, f32 = jnp.bfloat16, jnp.float32

    def kernel(*refs):
        attention_backward_kernel(shards, *refs)

    return pl.pallas_call(
        kernel,
        in_specs=[pl.BlockSpec(memory_space=pltpu.VMEM)] * len(args),
        out_specs=[pl.BlockSpec(memory_space=pltpu.VMEM)] * 2,
        out_shape=[
            jax.ShapeDtypeStruct((TOKENS, width), f32),
            jax.ShapeDtypeStruct((copies, shards, half + 8, CHUNK), bf16),
        ],
        scratch_shapes=[
            pltpu.VMEM((TOKENS, TOKENS), f32),
            pltpu.VMEM((GROUPS, HEAD_WIDTH, cells), bf16),
            pltpu.VMEM((GROUPS, HEAD_WIDTH, cells), f32),
            pltpu.VMEM((GROUPS, HEAD_WIDTH, TOKENS), f32),
            pltpu.VMEM((GROUPS, HEAD_WIDTH, TOKENS), f32),
        ],
        compiler_params=pltpu.CompilerParams(vmem_limit_bytes=VMEM_LIMIT),
        cost_estimate=pl.CostEstimate(
            flops=int(3e9), bytes_accessed=9000000, transcendentals=1400000
        ),
        name="attention_backward",
    )(*args)


def unpack_attn_kernel(piece_ref, q_ref, k_ref, v_ref, o_ref):
    half = piece_ref.shape[1]
    columns = []
    for c in range(piece_ref.shape[0] // 2):
        columns.append(
            jnp.concatenate([widen(piece_ref[2 * c]), widen(piece_ref[2 * c + 1])], axis=0)
        )
    full = jnp.concatenate(columns, axis=1)
    kvw, width = k_ref.shape[1], o_ref.shape[1]
    k_ref[...] = full[:, :kvw]
    v_ref[...] = full[:, kvw : 2 * kvw]
    o_ref[...] = full[:, 2 * kvw : 2 * kvw + width]
    q_ref[...] = full[:, 2 * kvw + width :]


def unpack_attn(pieces, shapes):
    return pl.pallas_call(
        unpack_attn_kernel,
        out_shape=[jax.ShapeDtypeStruct(shape, jnp.float32) for shape in shapes],
        name="unpack_attn",
    )(pieces)


def unpack_mlp_kernel(piece_ref, gate_ref, up_ref, down_ref):
    half = piece_ref.shape[2]
    for c in range(piece_ref.shape[0] // 2):
        for h in range(2):
            for m, ref in ((0, gate_ref), (1, up_ref)):
                ref[h * half : (h + 1) * half, c * CHUNK : (c + 1) * CHUNK] = widen(
                    piece_ref[2 * c + h, m]
                )
    tall = [widen(piece_ref[r, 2]) for r in range(piece_ref.shape[0])]
    down_ref[...] = jnp.transpose(jnp.concatenate(tall, axis=0))


def unpack_mlp(pieces, shapes):
    return pl.pallas_call(
        unpack_mlp_kernel,
        out_shape=[jax.ShapeDtypeStruct(shape, jnp.float32) for shape in shapes],
        name="unpack_mlp",
    )(pieces)


def fits_kernels(block_input, query_weight, key_weight, gate_weight, down_weight):
    return (
        lax.axis_size("rep") == 8
        and lax.axis_size("shard") == 4
        and block_input.shape == (1, TOKENS, 576)
        and query_weight.shape == (144, 576)
        and key_weight.shape == (144, 192)
        and gate_weight.shape == (144, 1536)
        and down_weight.shape == (384, 576)
    )


def gain_rows(gain_attn, gain_mlp):
    rows = gain_attn.shape[0]
    size = lax.axis_size("shard")
    both = jnp.zeros((2, 2 * CHUNK), jnp.bfloat16)
    both = lax.dynamic_update_slice(
        both, jnp.stack([gain_attn, gain_mlp]), (0, lax.axis_index("shard") * rows)
    )
    return jnp.pad(both.reshape(4, CHUNK), ((0, 4), (0, 0)))


def on_device(
    block_input,
    segment_ids,
    positions,
    query_weight,
    key_weight,
    value_weight,
    output_weight,
    gate_weight,
    up_weight,
    down_weight,
    gain_attn,
    gain_mlp,
    layer_output_cotangent,
):
    if not fits_kernels(block_input, query_weight, key_weight, gate_weight, down_weight):
        return on_device_generic(
            block_input,
            segment_ids,
            positions,
            query_weight,
            key_weight,
            value_weight,
            output_weight,
            gate_weight,
            up_weight,
            down_weight,
            gain_attn,
            gain_mlp,
            layer_output_cotangent,
        )
    shards, copies = lax.axis_size("shard"), lax.axis_size("rep")
    z = lax.axis_index("shard").astype(jnp.int32).reshape(1)
    own = jnp.concatenate([key_weight, value_weight, output_weight, query_weight], axis=1)
    gains_own = gain_rows(gain_attn, gain_mlp)
    attn_others = fetch_others(jnp.concatenate([piece_of(own), gains_own]))
    attn_pieces = lax.all_gather(attn_others, "rep")
    tall = jnp.transpose(down_weight)
    wide = jnp.stack([piece_of(gate_weight), piece_of(up_weight), row_piece_of(tall)])
    wide_pieces = lax.all_gather(fetch_others(wide), "rep")

    half_dim = HEAD_WIDTH // 2
    frequency = ROPE_BASE ** (-(jnp.arange(half_dim, dtype=jnp.float32) * 2.0 / HEAD_WIDTH))
    angles = frequency[:, None] * positions.astype(jnp.float32)
    cosine, sine = jnp.cos(angles), jnp.sin(angles)
    row = segment_ids
    col = segment_ids.reshape(-1, 1)
    x = block_input[0]
    ct = layer_output_cotangent[0]

    w, gains, x2, q, k, v, o, lse = attention_forward(
        z, x, col, row, cosine, sine, own, gains_own, attn_pieces, shards
    )
    out, dx2, gain_mlp_grad, wide_grad = mlp(
        z, x2, ct, gains, gate_weight, up_weight, tall, wide_pieces, shards
    )
    half = gate_weight.shape[0] // 2
    wide_part = lax.psum_scatter(
        wide_grad.reshape(-1, CHUNK), "rep", scatter_dimension=0, tiled=True
    ).reshape(shards, 3, half, CHUNK)
    dx, attn_grad = attention_backward(
        (x, dx2, col, row, cosine, sine, w, gains, q, k, v, o, lse, gain_mlp_grad),
        shards,
        copies,
    )
    attn_part = lax.psum_scatter(
        attn_grad.reshape(-1, CHUNK), "rep", scatter_dimension=0, tiled=True
    ).reshape(shards, half + 8, CHUNK)
    wide_total = narrow(sum_over_shard(wide_part))
    gate_grad, up_grad, down_grad = unpack_mlp(
        lax.all_gather(wide_total, "rep"),
        (gate_weight.shape, up_weight.shape, down_weight.shape),
    )
    attn_total = sum_over_shard(attn_part)
    q_grad, k_grad, v_grad, o_grad = unpack_attn(
        lax.all_gather(narrow(attn_total[:half]), "rep"),
        (query_weight.shape, key_weight.shape, value_weight.shape, output_weight.shape),
    )
    both = attn_total[half : half + 4].reshape(2, 2 * CHUNK)
    rows = gain_attn.shape[0]
    both = lax.dynamic_slice(both, (0, lax.axis_index("shard") * rows), (2, rows))
    return (
        out[None],
        dx[None],
        q_grad,
        k_grad,
        v_grad,
        o_grad,
        gate_grad,
        up_grad,
        down_grad,
        both[0],
        both[1],
    )


def solution(mesh):
    placed = (
        P(("rep", "shard"), None, None),
        P(("rep", "shard"), None),
        P(("rep", "shard"), None),
        P("shard", None),
        P("shard", None),
        P("shard", None),
        P("shard", None),
        P("shard", None),
        P("shard", None),
        P("shard", None),
        P("shard"),
        P("shard"),
        P(("rep", "shard"), None, None),
    )
    return jax.shard_map(
        on_device,
        mesh=mesh,
        in_specs=placed,
        out_specs=(
            P(("rep", "shard"), None, None),
            P(("rep", "shard"), None, None),
            P("shard", None),
            P("shard", None),
            P("shard", None),
            P("shard", None),
            P("shard", None),
            P("shard", None),
            P("shard", None),
            P("shard"),
            P("shard"),
        ),
        check_vma=False,
    )
```

```python
import jax
import jax.numpy as jnp
from jax import lax
from jax.experimental import pallas as pl
from jax.experimental.pallas import tpu as pltpu
from jax.sharding import PartitionSpec as P

QUERY_HEADS = 9
KEY_VALUE_HEADS = 3
HEAD_WIDTH = 64


EPSILON = 1e-05
ROPE_BASE = 100000.0


def product_term(pattern, left_op, right_op):
    return jnp.einsum(pattern, left_op, right_op, preferred_element_type=jnp.float32)


def norm_stats(values):
    inverse = lax.rsqrt(jnp.mean(values * values, axis=-1, keepdims=True) + EPSILON)
    return (inverse, values * inverse)


def rope_tables(positions):
    half_dim = HEAD_WIDTH // 2
    frequency = ROPE_BASE ** (-(jnp.arange(half_dim, dtype=jnp.float32) * 2.0 / HEAD_WIDTH))
    angles = positions.astype(jnp.float32)[:, :, None] * frequency
    return (jnp.cos(angles)[:, :, None, :], jnp.sin(angles)[:, :, None, :])


def rotate(tensor, cosine_table, sine_table, direction):
    half_dim = HEAD_WIDTH // 2
    first_half = tensor[..., :half_dim]
    second_half = tensor[..., half_dim:]
    return jnp.concatenate(
        [
            first_half * cosine_table - direction * second_half * sine_table,
            second_half * cosine_table + direction * first_half * sine_table,
        ],
        axis=-1,
    )


def attention_mask(segment_ids):
    indices = jnp.arange(segment_ids.shape[1])
    causal = indices[:, None] >= indices[None, :]
    same_doc = segment_ids[:, :, None] == segment_ids[:, None, :]
    return (causal[None] & same_doc)[:, None, None]


def score_block(q_rot, k_rot, allowed):
    scores = product_term("sqgrh,skgh->sgrqk", q_rot, k_rot) * HEAD_WIDTH ** (-0.5)
    return jnp.where(allowed, scores, -1e30)


def forward_pass(weights, block_input, segment_ids, positions):
    (
        query_weight,
        key_weight,
        value_weight,
        output_weight,
        gate_weight,
        up_weight,
        down_weight,
        gain_attn,
        gain_mlp,
    ) = weights
    sequence_count, sequence_length, width = block_input.shape
    group_size = QUERY_HEADS // KEY_VALUE_HEADS
    q_width = QUERY_HEADS * HEAD_WIDTH
    residual_input = block_input.astype(jnp.float32)
    inv_attn, unit_attn = norm_stats(residual_input)
    attention_normalized = (unit_attn * gain_attn.astype(jnp.float32)).astype(jnp.bfloat16)
    cosine_table, sine_table = rope_tables(positions)
    query_projected = product_term("ifw,wq->ifq", attention_normalized, query_weight).reshape(
        sequence_count, sequence_length, QUERY_HEADS, HEAD_WIDTH
    )
    key_projected = product_term("ifw,wq->ifq", attention_normalized, key_weight).reshape(
        sequence_count, sequence_length, KEY_VALUE_HEADS, HEAD_WIDTH
    )
    value_projected = product_term("ifw,wq->ifq", attention_normalized, value_weight).reshape(
        sequence_count, sequence_length, KEY_VALUE_HEADS, HEAD_WIDTH
    )
    q_rot = rotate(query_projected, cosine_table, sine_table, 1.0).astype(jnp.bfloat16)
    q_rot = q_rot.reshape(sequence_count, sequence_length, KEY_VALUE_HEADS, group_size, HEAD_WIDTH)
    k_rot = rotate(key_projected, cosine_table, sine_table, 1.0).astype(jnp.bfloat16)
    value_b = value_projected.astype(jnp.bfloat16)
    allowed = attention_mask(segment_ids)
    scores = score_block(q_rot, k_rot, allowed)
    row_max = jnp.max(scores, axis=-1, keepdims=True)
    log_total = row_max + jnp.log(jnp.sum(jnp.exp(scores - row_max), axis=-1, keepdims=True))
    attn_probs = jnp.exp(scores - log_total).astype(jnp.bfloat16)
    attention_merged = (
        product_term("sgrqk,skgh->sqgrh", attn_probs, value_b)
        .reshape(sequence_count, sequence_length, q_width)
        .astype(jnp.bfloat16)
    )
    residual_middle = residual_input + product_term("gwb,ba->gwa", attention_merged, output_weight)
    inv_mlp, unit_mlp = norm_stats(residual_middle)
    feedforward_normalized = (unit_mlp * gain_mlp.astype(jnp.float32)).astype(jnp.bfloat16)
    gate_projected = product_term("qbg,gh->qbh", feedforward_normalized, gate_weight)
    up_projected = product_term("qbg,gh->qbh", feedforward_normalized, up_weight)
    hidden_state = (jax.nn.silu(gate_projected) * up_projected).astype(jnp.bfloat16)
    layer_result = residual_middle + product_term("jbw,wg->jbg", hidden_state, down_weight)
    stored = (
        inv_attn,
        unit_attn,
        attention_normalized,
        q_rot,
        k_rot,
        value_b,
        log_total,
        attention_merged,
        inv_mlp,
        unit_mlp,
        feedforward_normalized,
        gate_projected,
        up_projected,
        hidden_state,
    )
    return (layer_result, stored)


def backward_mlp(weights, layer_output_cotangent, stored):
    (
        query_weight,
        key_weight,
        value_weight,
        output_weight,
        gate_weight,
        up_weight,
        down_weight,
        gain_attn,
        gain_mlp,
    ) = weights
    inv_mlp, unit_mlp, feedforward_normalized, gate_projected, up_projected, hidden_state = stored[
        8:
    ]
    grad_out = layer_output_cotangent.astype(jnp.float32)
    activation_cotangent = product_term("zeo,ho->zeh", layer_output_cotangent, down_weight)
    down_weight_gradient = product_term("bux,bue->xe", layer_output_cotangent, hidden_state)
    gate_sigmoid = jax.nn.sigmoid(gate_projected)
    gate_cotangent = (
        activation_cotangent
        * up_projected
        * gate_sigmoid
        * (1.0 + gate_projected * (1.0 - gate_sigmoid))
    ).astype(jnp.bfloat16)
    up_cotangent = (activation_cotangent * gate_projected * gate_sigmoid).astype(jnp.bfloat16)
    gate_weight_gradient = product_term("avq,avc->qc", feedforward_normalized, gate_cotangent)
    up_weight_gradient = product_term("avq,avc->qc", feedforward_normalized, up_cotangent)
    normalized_cotangent = product_term("abo,mo->abm", gate_cotangent, gate_weight) + product_term(
        "abo,mo->abm", up_cotangent, up_weight
    )
    g_gain = jnp.sum(normalized_cotangent * unit_mlp, axis=(0, 1))
    d_unit = normalized_cotangent * gain_mlp.astype(jnp.float32)
    grad_mid = grad_out + inv_mlp * (
        d_unit - unit_mlp * jnp.mean(d_unit * unit_mlp, axis=-1, keepdims=True)
    )
    return (grad_mid, (gate_weight_gradient, up_weight_gradient, down_weight_gradient, g_gain))


def backward_attention(weights, segment_ids, positions, stored, grad_mid):
    (
        query_weight,
        key_weight,
        value_weight,
        output_weight,
        gate_weight,
        up_weight,
        down_weight,
        gain_attn,
        gain_mlp,
    ) = weights
    (
        inv_attn,
        unit_attn,
        attention_normalized,
        q_rot,
        k_rot,
        value_b,
        log_total,
        attention_merged,
    ) = stored[:8]
    sequence_count, sequence_length, width = grad_mid.shape
    group_size = QUERY_HEADS // KEY_VALUE_HEADS
    q_width = QUERY_HEADS * HEAD_WIDTH
    kv_width = KEY_VALUE_HEADS * HEAD_WIDTH
    block_gradient = grad_mid.astype(jnp.bfloat16)
    output_weight_gradient = product_term("uvc,uvn->cn", attention_merged, block_gradient)
    merged_cotangent = product_term("nuw,vw->nuv", block_gradient, output_weight).astype(
        jnp.bfloat16
    )
    merged_cotangent = merged_cotangent.reshape(
        sequence_count, sequence_length, KEY_VALUE_HEADS, group_size, HEAD_WIDTH
    )
    allowed = attention_mask(segment_ids)
    scores = score_block(q_rot, k_rot, allowed)
    attn_probs = jnp.exp(scores - log_total)
    d_value = product_term("sgrqk,sqgrh->skgh", attn_probs.astype(jnp.bfloat16), merged_cotangent)
    d_prob = product_term("sqgrh,skgh->sgrqk", merged_cotangent, value_b)
    mixed_heads = attention_merged.reshape(
        sequence_count, sequence_length, KEY_VALUE_HEADS, group_size, HEAD_WIDTH
    )
    row_delta = jnp.sum(
        merged_cotangent.astype(jnp.float32) * mixed_heads.astype(jnp.float32), axis=-1
    )
    row_delta = jnp.transpose(row_delta, (0, 2, 3, 1))[..., None]
    d_score = (attn_probs * (d_prob - row_delta) * HEAD_WIDTH ** (-0.5)).astype(jnp.bfloat16)
    d_query = product_term("sgrqk,skgh->sqgrh", d_score, k_rot).reshape(
        sequence_count, sequence_length, QUERY_HEADS, HEAD_WIDTH
    )
    d_key = product_term("sgrqk,sqgrh->skgh", d_score, q_rot)
    cosine_table, sine_table = rope_tables(positions)
    query_block_cotangent = (
        rotate(d_query, cosine_table, sine_table, -1.0)
        .astype(jnp.bfloat16)
        .reshape(sequence_count, sequence_length, q_width)
    )
    key_block_cotangent = (
        rotate(d_key, cosine_table, sine_table, -1.0)
        .astype(jnp.bfloat16)
        .reshape(sequence_count, sequence_length, kv_width)
    )
    value_block_cotangent = d_value.astype(jnp.bfloat16).reshape(
        sequence_count, sequence_length, kv_width
    )
    query_weight_gradient = product_term("uxj,uxc->jc", attention_normalized, query_block_cotangent)
    key_weight_gradient = product_term("uxj,uxc->jc", attention_normalized, key_block_cotangent)
    value_weight_gradient = product_term("uxj,uxc->jc", attention_normalized, value_block_cotangent)
    normalized_cotangent = (
        product_term("vcm,tm->vct", query_block_cotangent, query_weight)
        + product_term("vcm,tm->vct", key_block_cotangent, key_weight)
        + product_term("vcm,tm->vct", value_block_cotangent, value_weight)
    )
    g_gain = jnp.sum(normalized_cotangent * unit_attn, axis=(0, 1))
    d_unit = normalized_cotangent * gain_attn.astype(jnp.float32)
    grad_in = grad_mid + inv_attn * (
        d_unit - unit_attn * jnp.mean(d_unit * unit_attn, axis=-1, keepdims=True)
    )
    return (
        grad_in,
        (
            query_weight_gradient,
            key_weight_gradient,
            value_weight_gradient,
            output_weight_gradient,
            g_gain,
        ),
    )


def shifted(values, steps):
    size = lax.axis_size("shard")
    return lax.ppermute(values, "shard", [(i, (i + steps) % size) for i in range(size)])


def piece_of(block):
    copies = lax.axis_size("rep")
    me = lax.axis_index("rep")
    rows, columns = block.shape[0] // 2, block.shape[1] // (copies // 2)
    return lax.dynamic_slice(block, ((me % 2) * rows, (me // 2) * columns), (rows, columns))


def row_piece_of(block):
    copies = lax.axis_size("rep")
    rows = block.shape[0] // copies
    return lax.dynamic_slice_in_dim(block, lax.axis_index("rep") * rows, rows, 0)


def fetch_others(piece):
    size = lax.axis_size("shard")
    return jnp.stack([shifted(piece, k) for k in range(1, size)])


def place_blocks(own, others):
    size = lax.axis_size("shard")
    me = lax.axis_index("shard")
    full = jnp.zeros((size,) + own.shape, own.dtype)
    full = lax.dynamic_update_index_in_dim(full, own, me, 0)
    for k in range(1, size):
        full = lax.dynamic_update_index_in_dim(full, others[k - 1], (me - k) % size, 0)
    return full.reshape((size * own.shape[0],) + own.shape[1:])


def join_pieces(gathered):
    copies = gathered.shape[0]
    lead, rows, columns = gathered.shape[1:]
    parts = gathered.reshape(copies // 2, 2, lead, rows, columns)
    return jnp.transpose(parts, (2, 1, 3, 0, 4)).reshape(lead, 2 * rows, copies // 2 * columns)


def split_pieces(full):
    size = lax.axis_size("shard")
    copies = lax.axis_size("rep")
    rows, columns = full.shape[0] // size // 2, full.shape[1] // (copies // 2)
    parts = full.astype(jnp.bfloat16).reshape(size, 2, rows, copies // 2, columns)
    return jnp.transpose(parts, (3, 1, 0, 2, 4)).reshape(copies, size, rows, columns)


def sum_over_shard(parts):
    size = lax.axis_size("shard")
    me = lax.axis_index("shard")
    total = lax.dynamic_index_in_dim(parts, me, 0, keepdims=False).astype(jnp.float32)
    for k in range(1, size):
        block = lax.dynamic_index_in_dim(parts, (me + k) % size, 0, keepdims=False)
        total = total + shifted(block, k).astype(jnp.float32)
    return total


def gather_weights(q, k, v, o, gate, up, down, gain_attn, gain_mlp):
    rows = q.shape[0]
    attn = jnp.concatenate([q, k, v, o], axis=1)
    attn_piece = piece_of(attn)
    gains = jnp.stack([gain_attn, gain_mlp])
    gains_pad = jnp.pad(gains, ((0, 6), (0, attn_piece.shape[1] - rows)))
    attn_others = fetch_others(jnp.concatenate([attn_piece, gains_pad]))
    half = attn_piece.shape[0]
    gains_full = place_blocks(gains, attn_others[:, half : half + 2, :rows])
    size = lax.axis_size("shard")
    gains_full = jnp.transpose(gains_full.reshape(size, 2, rows), (1, 0, 2)).reshape(2, size * rows)
    attn_gathered = lax.all_gather(attn_others[:, :half], "rep")
    attn_full = place_blocks(attn, join_pieces(attn_gathered))
    gate_piece = piece_of(gate)
    tall = jnp.transpose(down)
    tall_piece = row_piece_of(tall).reshape(gate_piece.shape)
    wide = jnp.stack([gate_piece, piece_of(up), tall_piece])
    wide_gathered = lax.all_gather(fetch_others(wide), "rep")
    gate_full = place_blocks(gate, join_pieces(wide_gathered[:, :, 0]))
    up_full = place_blocks(up, join_pieces(wide_gathered[:, :, 1]))
    tall_rows = jnp.transpose(wide_gathered[:, :, 2], (1, 0, 2, 3)).reshape((-1,) + tall.shape)
    down_full = jnp.transpose(place_blocks(down, jnp.transpose(tall_rows, (0, 2, 1))), (0, 1))
    a, b, c = q.shape[1], k.shape[1], v.shape[1]
    return (
        attn_full[:, :a],
        attn_full[:, a : a + b],
        attn_full[:, a + b : a + b + c],
        attn_full[:, a + b + c :],
        gate_full,
        up_full,
        down_full,
        gains_full[0],
        gains_full[1],
    )


def spread_pieces(piece):
    gathered = lax.all_gather(piece.astype(jnp.bfloat16), "rep")
    return join_pieces(gathered[:, None])[0].astype(jnp.float32)


def reduce_mlp(gate, up, tall):
    size = lax.axis_size("shard")
    copies = lax.axis_size("rep")
    gate_parts = split_pieces(gate)
    tall_parts = tall.astype(jnp.bfloat16).reshape(copies, tall.shape[0] // copies, size, -1)
    tall_parts = jnp.transpose(tall_parts, (0, 2, 1, 3))
    rows, columns = tall_parts.shape[2:]
    wide = jnp.stack([gate_parts, split_pieces(up), tall_parts.reshape(gate_parts.shape)], axis=2)
    shape = wide.shape[1:]
    wide = lax.psum_scatter(wide.reshape(-1, columns), "rep", scatter_dimension=0, tiled=True)
    wide = wide.reshape(shape)
    wide = sum_over_shard(wide).astype(jnp.bfloat16)
    wide = lax.all_gather(wide, "rep").astype(jnp.float32)
    tall_total = wide[:, 2].reshape(copies * rows, columns)
    return (
        join_pieces(wide[:, None, 0])[0],
        join_pieces(wide[:, None, 1])[0],
        jnp.transpose(tall_total),
    )


def reduce_attn(q, k, v, o, gain_attn, gain_mlp):
    size = lax.axis_size("shard")
    copies = lax.axis_size("rep")
    parts = split_pieces(jnp.concatenate([q, k, v, o], axis=1))
    half, columns = parts.shape[2:]
    gains = jnp.stack([gain_attn, gain_mlp]).reshape(2, size, -1).astype(jnp.bfloat16)
    rows = gains.shape[2]
    gains = jnp.pad(jnp.transpose(gains, (1, 0, 2)), ((0, 0), (0, 6), (0, columns - rows)))
    gains = jnp.broadcast_to(gains[None], (copies,) + gains.shape)
    parts = lax.psum_scatter(jnp.concatenate([parts, gains], axis=2), "rep", scatter_dimension=0)
    total = sum_over_shard(parts)
    full = spread_pieces(total[:half])
    a, b, c = q.shape[1], k.shape[1], v.shape[1]
    return (
        full[:, :a],
        full[:, a : a + b],
        full[:, a + b : a + b + c],
        full[:, a + b + c :],
        total[half, :rows],
        total[half + 1, :rows],
    )


def on_device_generic(
    block_input,
    segment_ids,
    positions,
    query_weight,
    key_weight,
    value_weight,
    output_weight,
    gate_weight,
    up_weight,
    down_weight,
    gain_attn,
    gain_mlp,
    layer_output_cotangent,
):
    weights = gather_weights(
        query_weight,
        key_weight,
        value_weight,
        output_weight,
        gate_weight,
        up_weight,
        down_weight,
        gain_attn,
        gain_mlp,
    )
    layer_result, stored = forward_pass(weights, block_input, segment_ids, positions)
    grad_mid, mlp_grads = backward_mlp(weights, layer_output_cotangent, stored)
    gate_total, up_total, down_total = reduce_mlp(*mlp_grads[:3])
    grad_in, attn_grads = backward_attention(weights, segment_ids, positions, stored, grad_mid)
    q_total, k_total, v_total, o_total, gain_attn_total, gain_mlp_total = reduce_attn(
        *attn_grads, mlp_grads[3]
    )
    return (
        layer_result.astype(jnp.bfloat16),
        grad_in,
        q_total,
        k_total,
        v_total,
        o_total,
        gate_total,
        up_total,
        down_total,
        gain_attn_total,
        gain_mlp_total,
    )


TOKENS = 384
CHUNK = 384
GROUPS = KEY_VALUE_HEADS
SHARE = QUERY_HEADS // KEY_VALUE_HEADS
VMEM_LIMIT = 56 * 1024 * 1024


def dot(left, right, left_dim=1, right_dim=0):
    return lax.dot_general(
        left, right, (((left_dim,), (right_dim,)), ((), ())), preferred_element_type=jnp.float32
    )


def widen(values):
    return values.astype(jnp.float32)


def narrow(values):
    return values.astype(jnp.bfloat16)


def mask_bias(seg_col, seg_row):
    shape = (TOKENS, TOKENS)
    key_at = lax.broadcasted_iota(jnp.int32, shape, 0)
    query_at = lax.broadcasted_iota(jnp.int32, shape, 1)
    allowed = (key_at <= query_at) & (seg_col == seg_row)
    return jnp.where(allowed, 0.0, -1e30)


def turn(values, cosine, sine):
    half = HEAD_WIDTH // 2
    first, second = values[:half], values[half:]
    return jnp.concatenate(
        [first * cosine - second * sine, second * cosine + first * sine], axis=0
    )


def attention_forward_kernel(
    shards, at_ref, x_ref, col_ref, row_ref, cos_ref, sin_ref, own_ref, gain_own_ref, mine_ref,
    pair_ref, w_ref, gain_ref, x2_ref, q_ref, k_ref, v_ref, o_ref, lse_ref, bias_ref,
):
    z = at_ref[0]
    first_core = at_ref[2] == 0
    rows = own_ref.shape[0]
    half = rows // 2
    width = x_ref.shape[1]
    own_at = pl.multiple_of(z * rows, 16)
    w_ref[pl.ds(own_at, rows), :] = own_ref[...]
    gains = widen(gain_own_ref[...])
    for k in range(1, shards):
        at = pl.multiple_of(lax.rem(z + shards - k, shards) * rows, 16)
        gains = gains + widen(mine_ref[k - 1, half:])
        mine, pair = widen(mine_ref[k - 1, :half]), widen(pair_ref[k - 1, :half])
        upper = jnp.where(first_core, mine, pair)
        lower = jnp.where(first_core, pair, mine)
        w_ref[pl.ds(at, rows), :] = narrow(jnp.concatenate([upper, lower], axis=0))
    gain_attn = gains[0:1, :width]
    gain_mlp = gains[1:2, :width]
    gain_ref[0:1, :] = gain_attn
    gain_ref[1:2, :] = gain_mlp
    x = widen(x_ref[...])
    inverse = lax.rsqrt(jnp.mean(x * x, axis=-1, keepdims=True) + EPSILON)
    h1 = narrow(x * inverse * gain_attn)
    kv = jnp.transpose(dot(h1, w_ref[:, :CHUNK]))
    q = jnp.transpose(dot(h1, w_ref[:, 896:]))[HEAD_WIDTH:]
    cosine, sine = cos_ref[...], sin_ref[...]
    bias_ref[...] = mask_bias(col_ref[...], row_ref[...])
    for g in range(GROUPS):
        at = g * HEAD_WIDTH
        k_ref[g] = narrow(turn(kv[at : at + HEAD_WIDTH], cosine, sine))
        at = (GROUPS + g) * HEAD_WIDTH
        v_ref[g] = narrow(kv[at : at + HEAD_WIDTH])
        for r in range(SHARE):
            at = (g * SHARE + r) * HEAD_WIDTH
            q_ref[g, :, r * TOKENS : (r + 1) * TOKENS] = narrow(
                turn(q[at : at + HEAD_WIDTH], cosine, sine)
            )

    def one_group(g, carry):
        scores = dot(k_ref[g], q_ref[g], 0, 0) * HEAD_WIDTH ** (-0.5)
        bias = bias_ref[...]
        scores = scores + jnp.concatenate([bias] * SHARE, axis=1)
        top = jnp.max(scores, axis=0, keepdims=True)
        weight = jnp.exp(scores - top)
        total = jnp.sum(weight, axis=0, keepdims=True)
        lse_ref[g] = top + jnp.log(total)
        probs = narrow(weight * (1.0 / total))
        o_ref[g] = narrow(dot(v_ref[g], probs))
        return carry

    lax.fori_loop(0, GROUPS, one_group, 0)
    x2_ref[...] = x + dot(joined_heads(o_ref), w_ref[:, CHUNK : CHUNK + width], 0, 0)


def joined_heads(ref):
    return jnp.concatenate(
        [
            ref[g, :, r * TOKENS : (r + 1) * TOKENS]
            for g in range(GROUPS)
            for r in range(SHARE)
        ],
        axis=0,
    )


def attention_forward(at, x, col, row, cosine, sine, own, gain_own, mine, pair, shards):
    width = x.shape[1]
    cells = SHARE * TOKENS
    bf16, f32 = jnp.bfloat16, jnp.float32

    def kernel(*refs):
        attention_forward_kernel(shards, *refs)

    return pl.pallas_call(
        kernel,
        grid_spec=pltpu.PrefetchScalarGridSpec(
            num_scalar_prefetch=1,
            grid=(),
            in_specs=[pl.BlockSpec(memory_space=pltpu.VMEM)] * 9,
            out_specs=[pl.BlockSpec(memory_space=pltpu.VMEM)] * 8,
            scratch_shapes=[pltpu.VMEM((TOKENS, TOKENS), f32)],
        ),
        out_shape=[
            jax.ShapeDtypeStruct((shards * own.shape[0], own.shape[1]), bf16),
            jax.ShapeDtypeStruct((8, width), f32),
            jax.ShapeDtypeStruct((TOKENS, width), f32),
            jax.ShapeDtypeStruct((GROUPS, HEAD_WIDTH, cells), bf16),
            jax.ShapeDtypeStruct((GROUPS, HEAD_WIDTH, TOKENS), bf16),
            jax.ShapeDtypeStruct((GROUPS, HEAD_WIDTH, TOKENS), bf16),
            jax.ShapeDtypeStruct((GROUPS, HEAD_WIDTH, cells), bf16),
            jax.ShapeDtypeStruct((GROUPS, 1, cells), f32),
        ],
        compiler_params=pltpu.CompilerParams(vmem_limit_bytes=VMEM_LIMIT),
        cost_estimate=pl.CostEstimate(
            flops=int(1.5e9), bytes_accessed=8000000, transcendentals=2000000
        ),
        name="attention_forward",
    )(at, x, col, row, cosine, sine, own, gain_own, mine, pair)


def mlp_kernel(
    shards, at_ref, x2_ref, ct_ref, gain_ref, gate_ref, up_ref, tall_ref, wide_ref, tall_other_ref,
    out_ref, dx2_ref, gain_grad_ref, keep_ref, send_ref,
    u2_ref, h2_ref, h2t_ref, ctt_ref, acc_ref, dh2_ref, wg_ref, wu_ref, wd_ref,
    gg_ref, gu_ref, gd_ref,
):
    z, chip, core = at_ref[0], at_ref[1], at_ref[2]
    j = pl.program_id(0)
    rows = gate_ref.shape[0]
    half = rows // 2

    @pl.when(j == 0)
    def _():
        x2 = x2_ref[...]
        inverse = lax.rsqrt(jnp.mean(x2 * x2, axis=-1, keepdims=True) + EPSILON)
        u2 = x2 * inverse
        u2_ref[...] = u2
        h2 = narrow(u2 * gain_ref[1:2, :])
        h2_ref[...] = h2
        h2t_ref[...] = narrow(jnp.transpose(widen(h2)))
        ctt_ref[...] = narrow(jnp.transpose(widen(ct_ref[...])))
        acc_ref[...] = x2
        dh2_ref[...] = jnp.zeros_like(dh2_ref)

    own_at = pl.multiple_of(z * rows, 16)
    wg_ref[pl.ds(own_at, rows), :] = gate_ref[...]
    wu_ref[pl.ds(own_at, rows), :] = up_ref[...]
    for k in range(1, shards):
        at = pl.multiple_of(lax.rem(z + shards - k, shards) * rows, 16)
        for m, ref in ((0, wg_ref), (1, wu_ref)):
            pieces = [widen(wide_ref[h, k - 1, m]) for h in range(2)]
            ref[pl.ds(at, rows), :] = narrow(jnp.concatenate(pieces, axis=0))

    @pl.when(j == z)
    def _():
        wd_ref[...] = tall_ref[...]

    @pl.when(j != z)
    def _():
        pieces = [widen(tall_other_ref[r, 0, 0]) for r in range(tall_other_ref.shape[0])]
        wd_ref[...] = narrow(jnp.concatenate(pieces, axis=0))

    h2, ct = h2_ref[...], ct_ref[...]
    wg, wu, wd = wg_ref[...], wu_ref[...], wd_ref[...]
    gate, up = dot(h2, wg), dot(h2, wu)
    da = dot(ct, wd)
    sigmoid = 1.0 / (1.0 + jnp.exp(-gate))
    silu = gate * sigmoid
    act = narrow(silu * up)
    dg = narrow(da * up * sigmoid * (1.0 + gate * (1.0 - sigmoid)))
    du = narrow(da * silu)
    acc_ref[...] += dot(act, wd, 1, 1)
    dh2_ref[...] += dot(dg, wg, 1, 1) + dot(du, wu, 1, 1)
    gg_ref[...] = dot(h2t_ref[...], dg)
    gu_ref[...] = dot(h2t_ref[...], du)
    gd_ref[...] = dot(ctt_ref[...], act)
    to_chip = lax.bitwise_xor(j, chip)
    to_shard = lax.rem(j + shards - z, shards)
    for rel, ref in ((0, keep_ref), (1, send_ref)):
        to_core = lax.bitwise_xor(core, rel)
        for k in range(shards):
            at = lax.rem(z + k, shards) * rows + to_core * half
            at = pl.multiple_of(at, 8)
            ref[to_chip, k, 0] = narrow(gg_ref[pl.ds(at, half), :])
            ref[to_chip, k, 1] = narrow(gu_ref[pl.ds(at, half), :])
        for c in range(4):
            at = (2 * lax.bitwise_xor(chip, c) + to_core) * half
            at = pl.multiple_of(at, 8)
            ref[c, to_shard, 2] = narrow(gd_ref[pl.ds(at, half), :])

    @pl.when(j == pl.num_programs(0) - 1)
    def _():
        out_ref[...] = narrow(acc_ref[...])
        dh2, u2, x2 = dh2_ref[...], u2_ref[...], x2_ref[...]
        inverse = lax.rsqrt(jnp.mean(x2 * x2, axis=-1, keepdims=True) + EPSILON)
        gain_grad_ref[0:1, :] = jnp.sum(dh2 * u2, axis=0, keepdims=True)
        n2 = dh2 * gain_ref[1:2, :]
        mean = jnp.mean(n2 * u2, axis=-1, keepdims=True)
        dx2_ref[...] = widen(ct_ref[...]) + inverse * (n2 - u2 * mean)


def mlp(at, x2, ct, gains, gate, up, tall, gathered, shards):
    width = x2.shape[1]
    copies = gathered.shape[0]
    rows, ff = gate.shape
    half = rows // 2
    bf16, f32 = jnp.bfloat16, jnp.float32

    def kernel(*refs):
        mlp_kernel(shards, *refs)

    def tall_block(j, at_ref):
        return (0, jnp.maximum(lax.rem(at_ref[0] + shards - j, shards) - 1, 0), 2, 0, 0)

    whole = lambda shape: pl.BlockSpec(shape, lambda j, at_ref: (0,) * len(shape))
    return pl.pallas_call(
        kernel,
        grid_spec=pltpu.PrefetchScalarGridSpec(
            num_scalar_prefetch=1,
            grid=(ff // CHUNK,),
            in_specs=[
                whole((TOKENS, width)),
                whole((TOKENS, width)),
                whole((8, width)),
                pl.BlockSpec((rows, CHUNK), lambda j, at_ref: (0, j)),
                pl.BlockSpec((rows, CHUNK), lambda j, at_ref: (0, j)),
                whole((width, CHUNK)),
                pl.BlockSpec((2, shards - 1, 2, half, CHUNK), lambda j, at_ref: (j, 0, 0, 0, 0)),
                pl.BlockSpec((copies, 1, 1, half, CHUNK), tall_block),
            ],
            out_specs=[
                whole((TOKENS, width)),
                whole((TOKENS, width)),
                whole((8, width)),
                whole((copies // 2, shards, 3, half, CHUNK)),
                whole((copies // 2, shards, 3, half, CHUNK)),
            ],
            scratch_shapes=[
                pltpu.VMEM((TOKENS, width), f32),
                pltpu.VMEM((TOKENS, width), bf16),
                pltpu.VMEM((width, TOKENS), bf16),
                pltpu.VMEM((width, TOKENS), bf16),
                pltpu.VMEM((TOKENS, width), f32),
                pltpu.VMEM((TOKENS, width), f32),
                pltpu.VMEM((width, CHUNK), bf16),
                pltpu.VMEM((width, CHUNK), bf16),
                pltpu.VMEM((width, CHUNK), bf16),
                pltpu.VMEM((width, CHUNK), f32),
                pltpu.VMEM((width, CHUNK), f32),
                pltpu.VMEM((width, CHUNK), f32),
            ],
        ),
        out_shape=[
            jax.ShapeDtypeStruct((TOKENS, width), bf16),
            jax.ShapeDtypeStruct((TOKENS, width), f32),
            jax.ShapeDtypeStruct((8, width), f32),
            jax.ShapeDtypeStruct((copies // 2, shards, 3, half, CHUNK), bf16),
            jax.ShapeDtypeStruct((copies // 2, shards, 3, half, CHUNK), bf16),
        ],
        compiler_params=pltpu.CompilerParams(
            vmem_limit_bytes=VMEM_LIMIT, dimension_semantics=("arbitrary",)
        ),
        cost_estimate=pl.CostEstimate(
            flops=int(6.2e9), bytes_accessed=14000000, transcendentals=1200000
        ),
        name="mlp",
    )(at, x2, ct, gains, gate, up, tall, gathered, gathered)


def attention_backward_kernel(
    shards, at_ref, x_ref, dx2_ref, col_ref, row_ref, cos_ref, sin_ref, w_ref, gain_ref, q_ref,
    k_ref, v_ref, o_ref, lse_ref, gain_grad_ref,
    dx_ref, keep_ref, send_ref,
    bias_ref, do_ref, dq_ref, dk_ref, dv_ref, grad_ref,
):
    z, chip, core = at_ref[0], at_ref[1], at_ref[2]
    width = x_ref.shape[1]
    rows = width // shards
    half = rows // 2
    x = widen(x_ref[...])
    inverse = lax.rsqrt(jnp.mean(x * x, axis=-1, keepdims=True) + EPSILON)
    u1 = x * inverse
    gain_attn = gain_ref[0:1, :]
    h1t = narrow(jnp.transpose(u1 * gain_attn))
    gx = narrow(dx2_ref[...])
    cosine, sine = cos_ref[...], sin_ref[...]
    bias_ref[...] = mask_bias(col_ref[...], row_ref[...])
    do = narrow(dot(w_ref[:, CHUNK : CHUNK + width], gx, 1, 1))
    for g in range(GROUPS):
        for r in range(SHARE):
            at = (g * SHARE + r) * HEAD_WIDTH
            do_ref[g, :, r * TOKENS : (r + 1) * TOKENS] = do[at : at + HEAD_WIDTH]

    def one_group(g, carry):
        bias = bias_ref[...]
        scores = dot(k_ref[g], q_ref[g], 0, 0) * HEAD_WIDTH ** (-0.5)
        scores = scores + jnp.concatenate([bias] * SHARE, axis=1)
        probs = jnp.exp(scores - lse_ref[g])
        do_g = do_ref[g]
        dv_ref[g] = jnp.transpose(dot(narrow(probs), do_g, 1, 1))
        delta = jnp.sum(widen(do_g) * widen(o_ref[g]), axis=0, keepdims=True)
        dp = dot(v_ref[g], do_g, 0, 0)
        ds = narrow(probs * (dp - delta) * HEAD_WIDTH ** (-0.5))
        dq_ref[g] = dot(k_ref[g], ds)
        dk_ref[g] = jnp.transpose(dot(ds, q_ref[g], 1, 1))
        return carry

    lax.fori_loop(0, GROUPS, one_group, 0)
    dkv = [narrow(turn(dk_ref[g], cosine, -sine)) for g in range(GROUPS)]
    dkv = jnp.concatenate(dkv + [narrow(dv_ref[g]) for g in range(GROUPS)], axis=0)
    dq = [
        narrow(turn(dq_ref[g, :, r * TOKENS : (r + 1) * TOKENS], cosine, -sine))
        for g in range(GROUPS)
        for r in range(SHARE)
    ]
    zeros = jnp.zeros((HEAD_WIDTH, TOKENS), jnp.bfloat16)
    dq_padded = jnp.concatenate([zeros] + dq, axis=0)
    dq = jnp.concatenate(dq, axis=0)
    dh1 = jnp.transpose(dot(w_ref[:, :CHUNK], dkv) + dot(w_ref[:, 896:], dq_padded))
    gain_grad = jnp.sum(dh1 * u1, axis=0, keepdims=True)
    n1 = dh1 * gain_attn
    mean = jnp.mean(n1 * u1, axis=-1, keepdims=True)
    dx_ref[...] = dx2_ref[...] + inverse * (n1 - u1 * mean)
    gain_mlp_grad = gain_grad_ref[0:1, :]
    tail = width - CHUNK
    blank = jnp.zeros((1, CHUNK - tail), jnp.float32)
    extra = jnp.concatenate(
        [
            gain_grad[:, :CHUNK],
            jnp.concatenate([gain_grad[:, CHUNK:], blank], axis=1),
            gain_mlp_grad[:, :CHUNK],
            jnp.concatenate([gain_mlp_grad[:, CHUNK:], blank], axis=1),
            jnp.zeros((4, CHUNK), jnp.float32),
        ],
        axis=0,
    )
    o = joined_heads(o_ref)
    for c in range(4):
        if c == 0:
            grad = dot(h1t, dkv, 1, 1)
        elif c == 1:
            grad = dot(o, gx[:, :CHUNK])
        elif c == 2:
            grad = jnp.concatenate(
                [dot(o, gx[:, CHUNK:]), dot(h1t, dq[: CHUNK - tail], 1, 1)], axis=1
            )
        else:
            grad = dot(h1t, dq[CHUNK - tail :], 1, 1)
        grad_ref[...] = grad
        to_chip = lax.bitwise_xor(chip, c)
        for rel, ref in ((0, keep_ref), (1, send_ref)):
            for k in range(shards):
                at = lax.rem(z + k, shards) * rows + lax.bitwise_xor(core, rel) * half
                at = pl.multiple_of(at, 8)
                ref[to_chip, k] = narrow(
                    jnp.concatenate([grad_ref[pl.ds(at, half), :], extra], axis=0)
                )


def attention_backward(at, args, shards, copies):
    x = args[0]
    width = x.shape[1]
    half = width // shards // 2
    cells = SHARE * TOKENS
    bf16, f32 = jnp.bfloat16, jnp.float32

    def kernel(*refs):
        attention_backward_kernel(shards, *refs)

    return pl.pallas_call(
        kernel,
        grid_spec=pltpu.PrefetchScalarGridSpec(
            num_scalar_prefetch=1,
            grid=(),
            in_specs=[pl.BlockSpec(memory_space=pltpu.VMEM)] * len(args),
            out_specs=[pl.BlockSpec(memory_space=pltpu.VMEM)] * 3,
            scratch_shapes=[
                pltpu.VMEM((TOKENS, TOKENS), f32),
                pltpu.VMEM((GROUPS, HEAD_WIDTH, cells), bf16),
                pltpu.VMEM((GROUPS, HEAD_WIDTH, cells), f32),
                pltpu.VMEM((GROUPS, HEAD_WIDTH, TOKENS), f32),
                pltpu.VMEM((GROUPS, HEAD_WIDTH, TOKENS), f32),
                pltpu.VMEM((width, CHUNK), f32),
            ],
        ),
        out_shape=[
            jax.ShapeDtypeStruct((TOKENS, width), f32),
            jax.ShapeDtypeStruct((copies // 2, shards, half + 8, CHUNK), bf16),
            jax.ShapeDtypeStruct((copies // 2, shards, half + 8, CHUNK), bf16),
        ],
        compiler_params=pltpu.CompilerParams(vmem_limit_bytes=VMEM_LIMIT),
        cost_estimate=pl.CostEstimate(
            flops=int(3e9), bytes_accessed=9000000, transcendentals=1400000
        ),
        name="attention_backward",
    )(at, *args)


def unpack_attn_kernel(piece_ref, q_ref, k_ref, v_ref, o_ref):
    half = piece_ref.shape[1]
    columns = []
    for c in range(piece_ref.shape[0] // 2):
        columns.append(
            jnp.concatenate([widen(piece_ref[2 * c]), widen(piece_ref[2 * c + 1])], axis=0)
        )
    full = jnp.concatenate(columns, axis=1)
    kvw, width = k_ref.shape[1], o_ref.shape[1]
    k_ref[...] = full[:, :kvw]
    v_ref[...] = full[:, kvw : 2 * kvw]
    o_ref[...] = full[:, 2 * kvw : 2 * kvw + width]
    q_ref[...] = full[:, 2 * kvw + width :]


def unpack_attn(pieces, shapes):
    return pl.pallas_call(
        unpack_attn_kernel,
        out_shape=[jax.ShapeDtypeStruct(shape, jnp.float32) for shape in shapes],
        name="unpack_attn",
    )(pieces)


def unpack_mlp_kernel(piece_ref, gate_ref, up_ref, down_ref):
    half = piece_ref.shape[2]
    for c in range(piece_ref.shape[0] // 2):
        for h in range(2):
            for m, ref in ((0, gate_ref), (1, up_ref)):
                ref[h * half : (h + 1) * half, c * CHUNK : (c + 1) * CHUNK] = widen(
                    piece_ref[2 * c + h, m]
                )
    tall = [widen(piece_ref[r, 2]) for r in range(piece_ref.shape[0])]
    down_ref[...] = jnp.transpose(jnp.concatenate(tall, axis=0))


def unpack_mlp(pieces, shapes):
    return pl.pallas_call(
        unpack_mlp_kernel,
        out_shape=[jax.ShapeDtypeStruct(shape, jnp.float32) for shape in shapes],
        name="unpack_mlp",
    )(pieces)


def fits_kernels(block_input, query_weight, key_weight, gate_weight, down_weight):
    return (
        lax.axis_size("rep") == 8
        and lax.axis_size("shard") == 4
        and block_input.shape == (1, TOKENS, 576)
        and query_weight.shape == (144, 576)
        and key_weight.shape == (144, 192)
        and gate_weight.shape == (144, 1536)
        and down_weight.shape == (384, 576)
    )


def gain_rows(gain_attn, gain_mlp, columns):
    both = jnp.zeros((8, columns), jnp.bfloat16)
    at = lax.axis_index("shard") * gain_attn.shape[0]
    return lax.dynamic_update_slice(both, jnp.stack([gain_attn, gain_mlp]), (0, at))


def swapped(values, bit):
    size = lax.axis_size("rep")
    return lax.ppermute(values, "rep", [(i, i ^ bit) for i in range(size)])


def plus(left, right):
    return narrow(widen(left) + widen(right))


def sum_in_plane(keep, came):
    tail = keep.shape[1:]
    mid = tail[0] // 2
    keep = keep.reshape((2, 2) + tail)
    came = came.reshape((2, 2) + tail)
    a_came = swapped(plus(keep[:, 1, :mid], came[:, 1, :mid]), 2)
    b_came = swapped(plus(keep[1, :, mid:], came[1, :, mid:]), 4)
    a_keep = plus(keep[:, 0, :mid], came[:, 0, :mid])
    b_keep = plus(keep[0, :, mid:], came[0, :, mid:])
    a_last = swapped(plus(a_keep[1], a_came[1]), 4)
    b_last = swapped(plus(b_keep[1], b_came[1]), 2)
    a = widen(a_keep[0]) + widen(a_came[0]) + widen(a_last)
    b = widen(b_keep[0]) + widen(b_came[0]) + widen(b_last)
    return a, b


def sum_along_shard(a, b):
    blocks = [a[i] for i in range(a.shape[0])] + [b[i] for i in range(b.shape[0])]
    came = [shifted(narrow(blocks[k]), k) for k in range(1, len(blocks))]
    total = blocks[0]
    for value in came:
        total = total + widen(value)
    return total


def on_device(
    block_input,
    segment_ids,
    positions,
    query_weight,
    key_weight,
    value_weight,
    output_weight,
    gate_weight,
    up_weight,
    down_weight,
    gain_attn,
    gain_mlp,
    layer_output_cotangent,
):
    if not fits_kernels(block_input, query_weight, key_weight, gate_weight, down_weight):
        return on_device_generic(
            block_input,
            segment_ids,
            positions,
            query_weight,
            key_weight,
            value_weight,
            output_weight,
            gate_weight,
            up_weight,
            down_weight,
            gain_attn,
            gain_mlp,
            layer_output_cotangent,
        )
    shards, copies = lax.axis_size("shard"), lax.axis_size("rep")
    rank = lax.axis_index("rep")
    at = jnp.stack([lax.axis_index("shard"), rank // 2, rank % 2]).astype(jnp.int32)
    tall = jnp.transpose(down_weight)
    wide = jnp.stack([piece_of(gate_weight), piece_of(up_weight), row_piece_of(tall)])
    wide_others = fetch_others(wide)
    wide_pieces = lax.all_gather(wide_others, "rep")
    own = jnp.concatenate([key_weight, value_weight, output_weight, query_weight], axis=1)
    gains_own = gain_rows(gain_attn, gain_mlp, own.shape[1])
    rows = own.shape[0]
    own_half = lax.dynamic_slice_in_dim(own, (rank % 2) * (rows // 2), rows // 2, 0)
    own_half = jnp.concatenate([own_half, gains_own])
    own_half, _ = lax.optimization_barrier((own_half, wide_others))
    mine = fetch_others(own_half)
    pair = swapped(mine, 1)

    half_dim = HEAD_WIDTH // 2
    frequency = ROPE_BASE ** (-(jnp.arange(half_dim, dtype=jnp.float32) * 2.0 / HEAD_WIDTH))
    angles = frequency[:, None] * positions.astype(jnp.float32)
    cosine, sine = jnp.cos(angles), jnp.sin(angles)
    row = segment_ids
    col = segment_ids.reshape(-1, 1)
    x = block_input[0]
    ct = layer_output_cotangent[0]

    w, gains, x2, q, k, v, o, lse = attention_forward(
        at, x, col, row, cosine, sine, own, gains_own, mine, pair, shards
    )
    out, dx2, gain_mlp_grad, wide_keep, wide_send = mlp(
        at, x2, ct, gains, gate_weight, up_weight, tall, wide_pieces, shards
    )
    wide_came = swapped(wide_send, 1)
    dx, attn_keep, attn_send = attention_backward(
        at,
        (x, dx2, col, row, cosine, sine, w, gains, q, k, v, o, lse, gain_mlp_grad),
        shards,
        copies,
    )
    wide_total = narrow(sum_along_shard(*sum_in_plane(wide_keep, wide_came)))
    gate_grad, up_grad, down_grad = unpack_mlp(
        lax.all_gather(wide_total, "rep"),
        (gate_weight.shape, up_weight.shape, down_weight.shape),
    )
    attn_total = sum_along_shard(*sum_in_plane(attn_keep, swapped(attn_send, 1)))
    half = rows // 2
    q_grad, k_grad, v_grad, o_grad = unpack_attn(
        lax.all_gather(narrow(attn_total[:half]), "rep"),
        (query_weight.shape, key_weight.shape, value_weight.shape, output_weight.shape),
    )
    both = attn_total[half : half + 4].reshape(2, 2 * CHUNK)
    both = lax.dynamic_slice(both, (0, lax.axis_index("shard") * rows), (2, rows))
    return (
        out[None],
        dx[None],
        q_grad,
        k_grad,
        v_grad,
        o_grad,
        gate_grad,
        up_grad,
        down_grad,
        both[0],
        both[1],
    )


def solution(mesh):
    placed = (
        P(("rep", "shard"), None, None),
        P(("rep", "shard"), None),
        P(("rep", "shard"), None),
        P("shard", None),
        P("shard", None),
        P("shard", None),
        P("shard", None),
        P("shard", None),
        P("shard", None),
        P("shard", None),
        P("shard"),
        P("shard"),
        P(("rep", "shard"), None, None),
    )
    return jax.shard_map(
        on_device,
        mesh=mesh,
        in_specs=placed,
        out_specs=(
            P(("rep", "shard"), None, None),
            P(("rep", "shard"), None, None),
            P("shard", None),
            P("shard", None),
            P("shard", None),
            P("shard", None),
            P("shard", None),
            P("shard", None),
            P("shard", None),
            P("shard"),
            P("shard"),
        ),
        check_vma=False,
    )
```

```python
import jax
import jax.numpy as jnp
from jax import lax
from jax.experimental import pallas as pl
from jax.experimental.pallas import tpu as pltpu
from jax.sharding import PartitionSpec as P

QUERY_HEADS = 9
KEY_VALUE_HEADS = 3
HEAD_WIDTH = 64


EPSILON = 1e-05
ROPE_BASE = 100000.0


def product_term(pattern, left_op, right_op):
    return jnp.einsum(pattern, left_op, right_op, preferred_element_type=jnp.float32)


def norm_stats(values):
    inverse = lax.rsqrt(jnp.mean(values * values, axis=-1, keepdims=True) + EPSILON)
    return (inverse, values * inverse)


def rope_tables(positions):
    half_dim = HEAD_WIDTH // 2
    frequency = ROPE_BASE ** (-(jnp.arange(half_dim, dtype=jnp.float32) * 2.0 / HEAD_WIDTH))
    angles = positions.astype(jnp.float32)[:, :, None] * frequency
    return (jnp.cos(angles)[:, :, None, :], jnp.sin(angles)[:, :, None, :])


def rotate(tensor, cosine_table, sine_table, direction):
    half_dim = HEAD_WIDTH // 2
    first_half = tensor[..., :half_dim]
    second_half = tensor[..., half_dim:]
    return jnp.concatenate(
        [
            first_half * cosine_table - direction * second_half * sine_table,
            second_half * cosine_table + direction * first_half * sine_table,
        ],
        axis=-1,
    )


def attention_mask(segment_ids):
    indices = jnp.arange(segment_ids.shape[1])
    causal = indices[:, None] >= indices[None, :]
    same_doc = segment_ids[:, :, None] == segment_ids[:, None, :]
    return (causal[None] & same_doc)[:, None, None]


def score_block(q_rot, k_rot, allowed):
    scores = product_term("sqgrh,skgh->sgrqk", q_rot, k_rot) * HEAD_WIDTH ** (-0.5)
    return jnp.where(allowed, scores, -1e30)


def forward_pass(weights, block_input, segment_ids, positions):
    (
        query_weight,
        key_weight,
        value_weight,
        output_weight,
        gate_weight,
        up_weight,
        down_weight,
        gain_attn,
        gain_mlp,
    ) = weights
    sequence_count, sequence_length, width = block_input.shape
    group_size = QUERY_HEADS // KEY_VALUE_HEADS
    q_width = QUERY_HEADS * HEAD_WIDTH
    residual_input = block_input.astype(jnp.float32)
    inv_attn, unit_attn = norm_stats(residual_input)
    attention_normalized = (unit_attn * gain_attn.astype(jnp.float32)).astype(jnp.bfloat16)
    cosine_table, sine_table = rope_tables(positions)
    query_projected = product_term("ifw,wq->ifq", attention_normalized, query_weight).reshape(
        sequence_count, sequence_length, QUERY_HEADS, HEAD_WIDTH
    )
    key_projected = product_term("ifw,wq->ifq", attention_normalized, key_weight).reshape(
        sequence_count, sequence_length, KEY_VALUE_HEADS, HEAD_WIDTH
    )
    value_projected = product_term("ifw,wq->ifq", attention_normalized, value_weight).reshape(
        sequence_count, sequence_length, KEY_VALUE_HEADS, HEAD_WIDTH
    )
    q_rot = rotate(query_projected, cosine_table, sine_table, 1.0).astype(jnp.bfloat16)
    q_rot = q_rot.reshape(sequence_count, sequence_length, KEY_VALUE_HEADS, group_size, HEAD_WIDTH)
    k_rot = rotate(key_projected, cosine_table, sine_table, 1.0).astype(jnp.bfloat16)
    value_b = value_projected.astype(jnp.bfloat16)
    allowed = attention_mask(segment_ids)
    scores = score_block(q_rot, k_rot, allowed)
    row_max = jnp.max(scores, axis=-1, keepdims=True)
    log_total = row_max + jnp.log(jnp.sum(jnp.exp(scores - row_max), axis=-1, keepdims=True))
    attn_probs = jnp.exp(scores - log_total).astype(jnp.bfloat16)
    attention_merged = (
        product_term("sgrqk,skgh->sqgrh", attn_probs, value_b)
        .reshape(sequence_count, sequence_length, q_width)
        .astype(jnp.bfloat16)
    )
    residual_middle = residual_input + product_term("gwb,ba->gwa", attention_merged, output_weight)
    inv_mlp, unit_mlp = norm_stats(residual_middle)
    feedforward_normalized = (unit_mlp * gain_mlp.astype(jnp.float32)).astype(jnp.bfloat16)
    gate_projected = product_term("qbg,gh->qbh", feedforward_normalized, gate_weight)
    up_projected = product_term("qbg,gh->qbh", feedforward_normalized, up_weight)
    hidden_state = (jax.nn.silu(gate_projected) * up_projected).astype(jnp.bfloat16)
    layer_result = residual_middle + product_term("jbw,wg->jbg", hidden_state, down_weight)
    stored = (
        inv_attn,
        unit_attn,
        attention_normalized,
        q_rot,
        k_rot,
        value_b,
        log_total,
        attention_merged,
        inv_mlp,
        unit_mlp,
        feedforward_normalized,
        gate_projected,
        up_projected,
        hidden_state,
    )
    return (layer_result, stored)


def backward_mlp(weights, layer_output_cotangent, stored):
    (
        query_weight,
        key_weight,
        value_weight,
        output_weight,
        gate_weight,
        up_weight,
        down_weight,
        gain_attn,
        gain_mlp,
    ) = weights
    inv_mlp, unit_mlp, feedforward_normalized, gate_projected, up_projected, hidden_state = stored[
        8:
    ]
    grad_out = layer_output_cotangent.astype(jnp.float32)
    activation_cotangent = product_term("zeo,ho->zeh", layer_output_cotangent, down_weight)
    down_weight_gradient = product_term("bux,bue->xe", layer_output_cotangent, hidden_state)
    gate_sigmoid = jax.nn.sigmoid(gate_projected)
    gate_cotangent = (
        activation_cotangent
        * up_projected
        * gate_sigmoid
        * (1.0 + gate_projected * (1.0 - gate_sigmoid))
    ).astype(jnp.bfloat16)
    up_cotangent = (activation_cotangent * gate_projected * gate_sigmoid).astype(jnp.bfloat16)
    gate_weight_gradient = product_term("avq,avc->qc", feedforward_normalized, gate_cotangent)
    up_weight_gradient = product_term("avq,avc->qc", feedforward_normalized, up_cotangent)
    normalized_cotangent = product_term("abo,mo->abm", gate_cotangent, gate_weight) + product_term(
        "abo,mo->abm", up_cotangent, up_weight
    )
    g_gain = jnp.sum(normalized_cotangent * unit_mlp, axis=(0, 1))
    d_unit = normalized_cotangent * gain_mlp.astype(jnp.float32)
    grad_mid = grad_out + inv_mlp * (
        d_unit - unit_mlp * jnp.mean(d_unit * unit_mlp, axis=-1, keepdims=True)
    )
    return (grad_mid, (gate_weight_gradient, up_weight_gradient, down_weight_gradient, g_gain))


def backward_attention(weights, segment_ids, positions, stored, grad_mid):
    (
        query_weight,
        key_weight,
        value_weight,
        output_weight,
        gate_weight,
        up_weight,
        down_weight,
        gain_attn,
        gain_mlp,
    ) = weights
    (
        inv_attn,
        unit_attn,
        attention_normalized,
        q_rot,
        k_rot,
        value_b,
        log_total,
        attention_merged,
    ) = stored[:8]
    sequence_count, sequence_length, width = grad_mid.shape
    group_size = QUERY_HEADS // KEY_VALUE_HEADS
    q_width = QUERY_HEADS * HEAD_WIDTH
    kv_width = KEY_VALUE_HEADS * HEAD_WIDTH
    block_gradient = grad_mid.astype(jnp.bfloat16)
    output_weight_gradient = product_term("uvc,uvn->cn", attention_merged, block_gradient)
    merged_cotangent = product_term("nuw,vw->nuv", block_gradient, output_weight).astype(
        jnp.bfloat16
    )
    merged_cotangent = merged_cotangent.reshape(
        sequence_count, sequence_length, KEY_VALUE_HEADS, group_size, HEAD_WIDTH
    )
    allowed = attention_mask(segment_ids)
    scores = score_block(q_rot, k_rot, allowed)
    attn_probs = jnp.exp(scores - log_total)
    d_value = product_term("sgrqk,sqgrh->skgh", attn_probs.astype(jnp.bfloat16), merged_cotangent)
    d_prob = product_term("sqgrh,skgh->sgrqk", merged_cotangent, value_b)
    mixed_heads = attention_merged.reshape(
        sequence_count, sequence_length, KEY_VALUE_HEADS, group_size, HEAD_WIDTH
    )
    row_delta = jnp.sum(
        merged_cotangent.astype(jnp.float32) * mixed_heads.astype(jnp.float32), axis=-1
    )
    row_delta = jnp.transpose(row_delta, (0, 2, 3, 1))[..., None]
    d_score = (attn_probs * (d_prob - row_delta) * HEAD_WIDTH ** (-0.5)).astype(jnp.bfloat16)
    d_query = product_term("sgrqk,skgh->sqgrh", d_score, k_rot).reshape(
        sequence_count, sequence_length, QUERY_HEADS, HEAD_WIDTH
    )
    d_key = product_term("sgrqk,sqgrh->skgh", d_score, q_rot)
    cosine_table, sine_table = rope_tables(positions)
    query_block_cotangent = (
        rotate(d_query, cosine_table, sine_table, -1.0)
        .astype(jnp.bfloat16)
        .reshape(sequence_count, sequence_length, q_width)
    )
    key_block_cotangent = (
        rotate(d_key, cosine_table, sine_table, -1.0)
        .astype(jnp.bfloat16)
        .reshape(sequence_count, sequence_length, kv_width)
    )
    value_block_cotangent = d_value.astype(jnp.bfloat16).reshape(
        sequence_count, sequence_length, kv_width
    )
    query_weight_gradient = product_term("uxj,uxc->jc", attention_normalized, query_block_cotangent)
    key_weight_gradient = product_term("uxj,uxc->jc", attention_normalized, key_block_cotangent)
    value_weight_gradient = product_term("uxj,uxc->jc", attention_normalized, value_block_cotangent)
    normalized_cotangent = (
        product_term("vcm,tm->vct", query_block_cotangent, query_weight)
        + product_term("vcm,tm->vct", key_block_cotangent, key_weight)
        + product_term("vcm,tm->vct", value_block_cotangent, value_weight)
    )
    g_gain = jnp.sum(normalized_cotangent * unit_attn, axis=(0, 1))
    d_unit = normalized_cotangent * gain_attn.astype(jnp.float32)
    grad_in = grad_mid + inv_attn * (
        d_unit - unit_attn * jnp.mean(d_unit * unit_attn, axis=-1, keepdims=True)
    )
    return (
        grad_in,
        (
            query_weight_gradient,
            key_weight_gradient,
            value_weight_gradient,
            output_weight_gradient,
            g_gain,
        ),
    )


def shifted(values, steps):
    size = lax.axis_size("shard")
    return lax.ppermute(values, "shard", [(i, (i + steps) % size) for i in range(size)])


def piece_of(block):
    copies = lax.axis_size("rep")
    me = lax.axis_index("rep")
    rows, columns = block.shape[0] // 2, block.shape[1] // (copies // 2)
    return lax.dynamic_slice(block, ((me % 2) * rows, (me // 2) * columns), (rows, columns))


def row_piece_of(block):
    copies = lax.axis_size("rep")
    rows = block.shape[0] // copies
    return lax.dynamic_slice_in_dim(block, lax.axis_index("rep") * rows, rows, 0)


def fetch_others(piece):
    size = lax.axis_size("shard")
    return jnp.stack([shifted(piece, k) for k in range(1, size)])


def place_blocks(own, others):
    size = lax.axis_size("shard")
    me = lax.axis_index("shard")
    full = jnp.zeros((size,) + own.shape, own.dtype)
    full = lax.dynamic_update_index_in_dim(full, own, me, 0)
    for k in range(1, size):
        full = lax.dynamic_update_index_in_dim(full, others[k - 1], (me - k) % size, 0)
    return full.reshape((size * own.shape[0],) + own.shape[1:])


def join_pieces(gathered):
    copies = gathered.shape[0]
    lead, rows, columns = gathered.shape[1:]
    parts = gathered.reshape(copies // 2, 2, lead, rows, columns)
    return jnp.transpose(parts, (2, 1, 3, 0, 4)).reshape(lead, 2 * rows, copies // 2 * columns)


def split_pieces(full):
    size = lax.axis_size("shard")
    copies = lax.axis_size("rep")
    rows, columns = full.shape[0] // size // 2, full.shape[1] // (copies // 2)
    parts = full.astype(jnp.bfloat16).reshape(size, 2, rows, copies // 2, columns)
    return jnp.transpose(parts, (3, 1, 0, 2, 4)).reshape(copies, size, rows, columns)


def sum_over_shard(parts):
    size = lax.axis_size("shard")
    me = lax.axis_index("shard")
    total = lax.dynamic_index_in_dim(parts, me, 0, keepdims=False).astype(jnp.float32)
    for k in range(1, size):
        block = lax.dynamic_index_in_dim(parts, (me + k) % size, 0, keepdims=False)
        total = total + shifted(block, k).astype(jnp.float32)
    return total


def gather_weights(q, k, v, o, gate, up, down, gain_attn, gain_mlp):
    rows = q.shape[0]
    attn = jnp.concatenate([q, k, v, o], axis=1)
    attn_piece = piece_of(attn)
    gains = jnp.stack([gain_attn, gain_mlp])
    gains_pad = jnp.pad(gains, ((0, 6), (0, attn_piece.shape[1] - rows)))
    attn_others = fetch_others(jnp.concatenate([attn_piece, gains_pad]))
    half = attn_piece.shape[0]
    gains_full = place_blocks(gains, attn_others[:, half : half + 2, :rows])
    size = lax.axis_size("shard")
    gains_full = jnp.transpose(gains_full.reshape(size, 2, rows), (1, 0, 2)).reshape(2, size * rows)
    attn_gathered = lax.all_gather(attn_others[:, :half], "rep")
    attn_full = place_blocks(attn, join_pieces(attn_gathered))
    gate_piece = piece_of(gate)
    tall = jnp.transpose(down)
    tall_piece = row_piece_of(tall).reshape(gate_piece.shape)
    wide = jnp.stack([gate_piece, piece_of(up), tall_piece])
    wide_gathered = lax.all_gather(fetch_others(wide), "rep")
    gate_full = place_blocks(gate, join_pieces(wide_gathered[:, :, 0]))
    up_full = place_blocks(up, join_pieces(wide_gathered[:, :, 1]))
    tall_rows = jnp.transpose(wide_gathered[:, :, 2], (1, 0, 2, 3)).reshape((-1,) + tall.shape)
    down_full = jnp.transpose(place_blocks(down, jnp.transpose(tall_rows, (0, 2, 1))), (0, 1))
    a, b, c = q.shape[1], k.shape[1], v.shape[1]
    return (
        attn_full[:, :a],
        attn_full[:, a : a + b],
        attn_full[:, a + b : a + b + c],
        attn_full[:, a + b + c :],
        gate_full,
        up_full,
        down_full,
        gains_full[0],
        gains_full[1],
    )


def spread_pieces(piece):
    gathered = lax.all_gather(piece.astype(jnp.bfloat16), "rep")
    return join_pieces(gathered[:, None])[0].astype(jnp.float32)


def reduce_mlp(gate, up, tall):
    size = lax.axis_size("shard")
    copies = lax.axis_size("rep")
    gate_parts = split_pieces(gate)
    tall_parts = tall.astype(jnp.bfloat16).reshape(copies, tall.shape[0] // copies, size, -1)
    tall_parts = jnp.transpose(tall_parts, (0, 2, 1, 3))
    rows, columns = tall_parts.shape[2:]
    wide = jnp.stack([gate_parts, split_pieces(up), tall_parts.reshape(gate_parts.shape)], axis=2)
    shape = wide.shape[1:]
    wide = lax.psum_scatter(wide.reshape(-1, columns), "rep", scatter_dimension=0, tiled=True)
    wide = wide.reshape(shape)
    wide = sum_over_shard(wide).astype(jnp.bfloat16)
    wide = lax.all_gather(wide, "rep").astype(jnp.float32)
    tall_total = wide[:, 2].reshape(copies * rows, columns)
    return (
        join_pieces(wide[:, None, 0])[0],
        join_pieces(wide[:, None, 1])[0],
        jnp.transpose(tall_total),
    )


def reduce_attn(q, k, v, o, gain_attn, gain_mlp):
    size = lax.axis_size("shard")
    copies = lax.axis_size("rep")
    parts = split_pieces(jnp.concatenate([q, k, v, o], axis=1))
    half, columns = parts.shape[2:]
    gains = jnp.stack([gain_attn, gain_mlp]).reshape(2, size, -1).astype(jnp.bfloat16)
    rows = gains.shape[2]
    gains = jnp.pad(jnp.transpose(gains, (1, 0, 2)), ((0, 0), (0, 6), (0, columns - rows)))
    gains = jnp.broadcast_to(gains[None], (copies,) + gains.shape)
    parts = lax.psum_scatter(jnp.concatenate([parts, gains], axis=2), "rep", scatter_dimension=0)
    total = sum_over_shard(parts)
    full = spread_pieces(total[:half])
    a, b, c = q.shape[1], k.shape[1], v.shape[1]
    return (
        full[:, :a],
        full[:, a : a + b],
        full[:, a + b : a + b + c],
        full[:, a + b + c :],
        total[half, :rows],
        total[half + 1, :rows],
    )


def on_device_generic(
    block_input,
    segment_ids,
    positions,
    query_weight,
    key_weight,
    value_weight,
    output_weight,
    gate_weight,
    up_weight,
    down_weight,
    gain_attn,
    gain_mlp,
    layer_output_cotangent,
):
    weights = gather_weights(
        query_weight,
        key_weight,
        value_weight,
        output_weight,
        gate_weight,
        up_weight,
        down_weight,
        gain_attn,
        gain_mlp,
    )
    layer_result, stored = forward_pass(weights, block_input, segment_ids, positions)
    grad_mid, mlp_grads = backward_mlp(weights, layer_output_cotangent, stored)
    gate_total, up_total, down_total = reduce_mlp(*mlp_grads[:3])
    grad_in, attn_grads = backward_attention(weights, segment_ids, positions, stored, grad_mid)
    q_total, k_total, v_total, o_total, gain_attn_total, gain_mlp_total = reduce_attn(
        *attn_grads, mlp_grads[3]
    )
    return (
        layer_result.astype(jnp.bfloat16),
        grad_in,
        q_total,
        k_total,
        v_total,
        o_total,
        gate_total,
        up_total,
        down_total,
        gain_attn_total,
        gain_mlp_total,
    )


TOKENS = 384
CHUNK = 384
LANES = 128
GROUPS = KEY_VALUE_HEADS
SHARE = QUERY_HEADS // KEY_VALUE_HEADS
VMEM_LIMIT = 56 * 1024 * 1024


def dot(left, right, left_dim=1, right_dim=0):
    return lax.dot_general(
        left, right, (((left_dim,), (right_dim,)), ((), ())), preferred_element_type=jnp.float32
    )


def widen(values):
    return values.astype(jnp.float32)


def narrow(values):
    return values.astype(jnp.bfloat16)


def mask_bias(seg_row):
    shape = (TOKENS, TOKENS)
    seg_col = jnp.transpose(jnp.broadcast_to(seg_row, (LANES, TOKENS)))[:, 0:1]
    key_at = lax.broadcasted_iota(jnp.int32, shape, 0)
    query_at = lax.broadcasted_iota(jnp.int32, shape, 1)
    allowed = (key_at <= query_at) & (seg_col == seg_row)
    return jnp.where(allowed, 0.0, -1e30)


def turn(values, cosine, sine):
    half = HEAD_WIDTH // 2
    first, second = values[:half], values[half:]
    return jnp.concatenate(
        [first * cosine - second * sine, second * cosine + first * sine], axis=0
    )


def attention_forward_kernel(
    shards, at_ref, x_ref, row_ref, cos_ref, sin_ref, own_ref, gain_own_ref, mine_ref,
    pair_ref, w_ref, gain_ref, x2_ref, q_ref, k_ref, v_ref, o_ref, lse_ref, bias_ref,
):
    z = at_ref[0]
    first_core = at_ref[2] == 0
    rows = own_ref.shape[0]
    half = rows // 2
    width = x_ref.shape[0]
    own_at = pl.multiple_of(z * rows, 16)
    w_ref[pl.ds(own_at, rows), :] = own_ref[...]
    gains = widen(gain_own_ref[...])
    for k in range(1, shards):
        at = pl.multiple_of(lax.rem(z + shards - k, shards) * rows, 16)
        gains = gains + widen(mine_ref[k - 1, half:])
        mine, pair = widen(mine_ref[k - 1, :half]), widen(pair_ref[k - 1, :half])
        upper = jnp.where(first_core, mine, pair)
        lower = jnp.where(first_core, pair, mine)
        w_ref[pl.ds(at, rows), :] = narrow(jnp.concatenate([upper, lower], axis=0))
    turned = jnp.transpose(jnp.concatenate([gains[:, : 5 * LANES]] * (LANES // 8), axis=0))
    gain_ref[...] = turned[:width]
    x = widen(x_ref[...])
    inverse = lax.rsqrt(jnp.mean(x * x, axis=0, keepdims=True) + EPSILON)
    h1 = narrow(x * inverse * turned[:width, 0:1])
    kv = dot(w_ref[:, :CHUNK], h1, 0, 0)
    q = dot(w_ref[:, 896:], h1, 0, 0)[HEAD_WIDTH:]
    cosine, sine = cos_ref[...], sin_ref[...]
    bias_ref[...] = mask_bias(row_ref[...])
    for g in range(GROUPS):
        at = g * HEAD_WIDTH
        k_ref[g] = narrow(turn(kv[at : at + HEAD_WIDTH], cosine, sine))
        at = (GROUPS + g) * HEAD_WIDTH
        v_ref[g] = narrow(kv[at : at + HEAD_WIDTH])
        for r in range(SHARE):
            at = (g * SHARE + r) * HEAD_WIDTH
            q_ref[g, :, r * TOKENS : (r + 1) * TOKENS] = narrow(
                turn(q[at : at + HEAD_WIDTH], cosine, sine)
            )

    def one_group(g, carry):
        scores = dot(k_ref[g], q_ref[g], 0, 0) * HEAD_WIDTH ** (-0.5)
        bias = bias_ref[...]
        scores = scores + jnp.concatenate([bias] * SHARE, axis=1)
        top = jnp.max(scores, axis=0, keepdims=True)
        weight = jnp.exp(scores - top)
        total = jnp.sum(weight, axis=0, keepdims=True)
        lse_ref[g] = top + jnp.log(total)
        probs = narrow(weight * (1.0 / total))
        o_ref[g] = narrow(dot(v_ref[g], probs))
        return carry

    lax.fori_loop(0, GROUPS, one_group, 0)
    x2_ref[...] = x + dot(w_ref[:, CHUNK : CHUNK + width], joined_heads(o_ref), 0, 0)


def joined_heads(ref):
    return jnp.concatenate(
        [
            ref[g, :, r * TOKENS : (r + 1) * TOKENS]
            for g in range(GROUPS)
            for r in range(SHARE)
        ],
        axis=0,
    )


def attention_forward(at, x, row, cosine, sine, own, gain_own, mine, pair, shards):
    width = x.shape[0]
    cells = SHARE * TOKENS
    bf16, f32 = jnp.bfloat16, jnp.float32

    def kernel(*refs):
        attention_forward_kernel(shards, *refs)

    return pl.pallas_call(
        kernel,
        grid_spec=pltpu.PrefetchScalarGridSpec(
            num_scalar_prefetch=1,
            grid=(),
            in_specs=[pl.BlockSpec(memory_space=pltpu.VMEM)] * 8,
            out_specs=[pl.BlockSpec(memory_space=pltpu.VMEM)] * 8,
            scratch_shapes=[pltpu.VMEM((TOKENS, TOKENS), f32)],
        ),
        out_shape=[
            jax.ShapeDtypeStruct((shards * own.shape[0], own.shape[1]), bf16),
            jax.ShapeDtypeStruct((width, LANES), f32),
            jax.ShapeDtypeStruct((width, TOKENS), f32),
            jax.ShapeDtypeStruct((GROUPS, HEAD_WIDTH, cells), bf16),
            jax.ShapeDtypeStruct((GROUPS, HEAD_WIDTH, TOKENS), bf16),
            jax.ShapeDtypeStruct((GROUPS, HEAD_WIDTH, TOKENS), bf16),
            jax.ShapeDtypeStruct((GROUPS, HEAD_WIDTH, cells), bf16),
            jax.ShapeDtypeStruct((GROUPS, 1, cells), f32),
        ],
        compiler_params=pltpu.CompilerParams(vmem_limit_bytes=VMEM_LIMIT),
        cost_estimate=pl.CostEstimate(
            flops=int(1.5e9), bytes_accessed=8000000, transcendentals=2000000
        ),
        name="attention_forward",
    )(at, x, row, cosine, sine, own, gain_own, mine, pair)


def mlp_kernel(
    shards, at_ref, x2_ref, ctt_ref, gain_ref, gate_ref, up_ref, tall_ref, wide_ref, tall_other_ref,
    out_ref, dx2_ref, gain_grad_ref, keep_ref, send_ref,
    h2_ref, h2t_ref, ct_ref, acc_ref, dh2_ref, wg_ref, wu_ref, wd_ref,
    gg_ref, gu_ref, gd_ref,
):
    z, chip, core = at_ref[0], at_ref[1], at_ref[2]
    j = pl.program_id(0)
    rows = gate_ref.shape[0]
    half = rows // 2

    @pl.when(j == 0)
    def _():
        x2 = x2_ref[...]
        inverse = lax.rsqrt(jnp.mean(x2 * x2, axis=0, keepdims=True) + EPSILON)
        h2t = x2 * inverse * gain_ref[:, 1:2]
        h2t_ref[...] = narrow(h2t)
        h2_ref[...] = narrow(jnp.transpose(h2t))
        ct_ref[...] = narrow(jnp.transpose(widen(ctt_ref[...])))
        acc_ref[...] = x2
        dh2_ref[...] = jnp.zeros_like(dh2_ref)

    own_at = pl.multiple_of(z * rows, 16)
    wg_ref[pl.ds(own_at, rows), :] = gate_ref[...]
    wu_ref[pl.ds(own_at, rows), :] = up_ref[...]
    for k in range(1, shards):
        at = pl.multiple_of(lax.rem(z + shards - k, shards) * rows, 16)
        for m, ref in ((0, wg_ref), (1, wu_ref)):
            pieces = [widen(wide_ref[h, k - 1, m]) for h in range(2)]
            ref[pl.ds(at, rows), :] = narrow(jnp.concatenate(pieces, axis=0))

    @pl.when(j == z)
    def _():
        wd_ref[...] = tall_ref[...]

    @pl.when(j != z)
    def _():
        pieces = [widen(tall_other_ref[r, 0, 0]) for r in range(tall_other_ref.shape[0])]
        wd_ref[...] = narrow(jnp.concatenate(pieces, axis=0))

    h2, ct = h2_ref[...], ct_ref[...]
    wg, wu, wd = wg_ref[...], wu_ref[...], wd_ref[...]
    gate, up = dot(h2, wg), dot(h2, wu)
    da = dot(ct, wd)
    sigmoid = 1.0 / (1.0 + jnp.exp(-gate))
    silu = gate * sigmoid
    act = narrow(silu * up)
    dg = narrow(da * up * sigmoid * (1.0 + gate * (1.0 - sigmoid)))
    du = narrow(da * silu)
    acc_ref[...] += dot(wd, act, 1, 1)
    dh2_ref[...] += dot(wg, dg, 1, 1) + dot(wu, du, 1, 1)
    gg_ref[...] = dot(h2t_ref[...], dg)
    gu_ref[...] = dot(h2t_ref[...], du)
    gd_ref[...] = dot(ctt_ref[...], act)
    to_chip = lax.bitwise_xor(j, chip)
    to_shard = lax.rem(j + shards - z, shards)
    for rel, ref in ((0, keep_ref), (1, send_ref)):
        to_core = lax.bitwise_xor(core, rel)
        for k in range(shards):
            at = lax.rem(z + k, shards) * rows + to_core * half
            at = pl.multiple_of(at, 8)
            ref[to_chip, k, 0] = narrow(gg_ref[pl.ds(at, half), :])
            ref[to_chip, k, 1] = narrow(gu_ref[pl.ds(at, half), :])
        for c in range(4):
            at = (2 * lax.bitwise_xor(chip, c) + to_core) * half
            at = pl.multiple_of(at, 8)
            ref[c, to_shard, 2] = narrow(gd_ref[pl.ds(at, half), :])

    @pl.when(j == pl.num_programs(0) - 1)
    def _():
        out_ref[...] = narrow(acc_ref[...])
        dh2, x2 = dh2_ref[...], x2_ref[...]
        inverse = lax.rsqrt(jnp.mean(x2 * x2, axis=0, keepdims=True) + EPSILON)
        u2 = x2 * inverse
        gain_grad = jnp.sum(dh2 * u2, axis=1, keepdims=True)
        gain_grad_ref[...] = jnp.broadcast_to(gain_grad, gain_grad_ref.shape)
        n2 = dh2 * gain_ref[:, 1:2]
        mean = jnp.mean(n2 * u2, axis=0, keepdims=True)
        dx2_ref[...] = widen(ctt_ref[...]) + inverse * (n2 - u2 * mean)


def mlp(at, x2, ct, gains, gate, up, tall, gathered, shards):
    width = x2.shape[0]
    copies = gathered.shape[0]
    rows, ff = gate.shape
    half = rows // 2
    bf16, f32 = jnp.bfloat16, jnp.float32

    def kernel(*refs):
        mlp_kernel(shards, *refs)

    def tall_block(j, at_ref):
        return (0, jnp.maximum(lax.rem(at_ref[0] + shards - j, shards) - 1, 0), 2, 0, 0)

    whole = lambda shape: pl.BlockSpec(shape, lambda j, at_ref: (0,) * len(shape))
    return pl.pallas_call(
        kernel,
        grid_spec=pltpu.PrefetchScalarGridSpec(
            num_scalar_prefetch=1,
            grid=(ff // CHUNK,),
            in_specs=[
                whole((width, TOKENS)),
                whole((width, TOKENS)),
                whole((width, LANES)),
                pl.BlockSpec((rows, CHUNK), lambda j, at_ref: (0, j)),
                pl.BlockSpec((rows, CHUNK), lambda j, at_ref: (0, j)),
                whole((width, CHUNK)),
                pl.BlockSpec((2, shards - 1, 2, half, CHUNK), lambda j, at_ref: (j, 0, 0, 0, 0)),
                pl.BlockSpec((copies, 1, 1, half, CHUNK), tall_block),
            ],
            out_specs=[
                whole((width, TOKENS)),
                whole((width, TOKENS)),
                whole((width, LANES)),
                whole((copies // 2, shards, 3, half, CHUNK)),
                whole((copies // 2, shards, 3, half, CHUNK)),
            ],
            scratch_shapes=[
                pltpu.VMEM((TOKENS, width), bf16),
                pltpu.VMEM((width, TOKENS), bf16),
                pltpu.VMEM((TOKENS, width), bf16),
                pltpu.VMEM((width, TOKENS), f32),
                pltpu.VMEM((width, TOKENS), f32),
                pltpu.VMEM((width, CHUNK), bf16),
                pltpu.VMEM((width, CHUNK), bf16),
                pltpu.VMEM((width, CHUNK), bf16),
                pltpu.VMEM((width, CHUNK), f32),
                pltpu.VMEM((width, CHUNK), f32),
                pltpu.VMEM((width, CHUNK), f32),
            ],
        ),
        out_shape=[
            jax.ShapeDtypeStruct((width, TOKENS), bf16),
            jax.ShapeDtypeStruct((width, TOKENS), f32),
            jax.ShapeDtypeStruct((width, LANES), f32),
            jax.ShapeDtypeStruct((copies // 2, shards, 3, half, CHUNK), bf16),
            jax.ShapeDtypeStruct((copies // 2, shards, 3, half, CHUNK), bf16),
        ],
        compiler_params=pltpu.CompilerParams(
            vmem_limit_bytes=VMEM_LIMIT, dimension_semantics=("arbitrary",)
        ),
        cost_estimate=pl.CostEstimate(
            flops=int(6.2e9), bytes_accessed=14000000, transcendentals=1200000
        ),
        name="mlp",
    )(at, x2, ct, gains, gate, up, tall, gathered, gathered)


def attention_backward_kernel(
    shards, at_ref, x_ref, dx2_ref, row_ref, cos_ref, sin_ref, w_ref, gain_ref, q_ref,
    k_ref, v_ref, o_ref, lse_ref, gain_grad_ref,
    dx_ref, keep_ref, send_ref,
    bias_ref, do_ref, dq_ref, dk_ref, dv_ref, grad_ref,
):
    z, chip, core = at_ref[0], at_ref[1], at_ref[2]
    width = x_ref.shape[0]
    rows = width // shards
    half = rows // 2
    x = widen(x_ref[...])
    inverse = lax.rsqrt(jnp.mean(x * x, axis=0, keepdims=True) + EPSILON)
    u1 = x * inverse
    gain_attn = gain_ref[:, 0:1]
    h1t = narrow(u1 * gain_attn)
    gx = narrow(dx2_ref[...])
    cosine, sine = cos_ref[...], sin_ref[...]
    bias_ref[...] = mask_bias(row_ref[...])
    do = narrow(dot(w_ref[:, CHUNK : CHUNK + width], gx))
    for g in range(GROUPS):
        for r in range(SHARE):
            at = (g * SHARE + r) * HEAD_WIDTH
            do_ref[g, :, r * TOKENS : (r + 1) * TOKENS] = do[at : at + HEAD_WIDTH]

    def one_group(g, carry):
        bias = bias_ref[...]
        scores = dot(k_ref[g], q_ref[g], 0, 0) * HEAD_WIDTH ** (-0.5)
        scores = scores + jnp.concatenate([bias] * SHARE, axis=1)
        probs = jnp.exp(scores - lse_ref[g])
        do_g = do_ref[g]
        dv_ref[g] = jnp.transpose(dot(narrow(probs), do_g, 1, 1))
        delta = jnp.sum(widen(do_g) * widen(o_ref[g]), axis=0, keepdims=True)
        dp = dot(v_ref[g], do_g, 0, 0)
        ds = narrow(probs * (dp - delta) * HEAD_WIDTH ** (-0.5))
        dq_ref[g] = dot(k_ref[g], ds)
        dk_ref[g] = jnp.transpose(dot(ds, q_ref[g], 1, 1))
        return carry

    lax.fori_loop(0, GROUPS, one_group, 0)
    dkv = [narrow(turn(dk_ref[g], cosine, -sine)) for g in range(GROUPS)]
    dkv = jnp.concatenate(dkv + [narrow(dv_ref[g]) for g in range(GROUPS)], axis=0)
    dq = [
        narrow(turn(dq_ref[g, :, r * TOKENS : (r + 1) * TOKENS], cosine, -sine))
        for g in range(GROUPS)
        for r in range(SHARE)
    ]
    zeros = jnp.zeros((HEAD_WIDTH, TOKENS), jnp.bfloat16)
    dq_padded = jnp.concatenate([zeros] + dq, axis=0)
    dq = jnp.concatenate(dq, axis=0)
    dh1 = dot(w_ref[:, :CHUNK], dkv) + dot(w_ref[:, 896:], dq_padded)
    gain_grad = jnp.sum(dh1 * u1, axis=1, keepdims=True)
    lane = lax.broadcasted_iota(jnp.int32, gain_grad_ref.shape, 1)
    both = jnp.transpose(jnp.where(lane == 0, gain_grad, gain_grad_ref[...]))
    gain_grad, gain_mlp_grad = both[0:1], both[1:2]
    n1 = dh1 * gain_attn
    mean = jnp.mean(n1 * u1, axis=0, keepdims=True)
    dx_ref[...] = dx2_ref[...] + inverse * (n1 - u1 * mean)
    tail = width - CHUNK
    blank = jnp.zeros((1, CHUNK - tail), jnp.float32)
    extra = jnp.concatenate(
        [
            gain_grad[:, :CHUNK],
            jnp.concatenate([gain_grad[:, CHUNK:], blank], axis=1),
            gain_mlp_grad[:, :CHUNK],
            jnp.concatenate([gain_mlp_grad[:, CHUNK:], blank], axis=1),
            jnp.zeros((4, CHUNK), jnp.float32),
        ],
        axis=0,
    )
    o = joined_heads(o_ref)
    for c in range(4):
        if c == 0:
            grad = dot(h1t, dkv, 1, 1)
        elif c == 1:
            grad = dot(o, gx[:CHUNK], 1, 1)
        elif c == 2:
            grad = jnp.concatenate(
                [dot(o, gx[CHUNK:], 1, 1), dot(h1t, dq[: CHUNK - tail], 1, 1)], axis=1
            )
        else:
            grad = dot(h1t, dq[CHUNK - tail :], 1, 1)
        grad_ref[...] = grad
        to_chip = lax.bitwise_xor(chip, c)
        for rel, ref in ((0, keep_ref), (1, send_ref)):
            for k in range(shards):
                at = lax.rem(z + k, shards) * rows + lax.bitwise_xor(core, rel) * half
                at = pl.multiple_of(at, 8)
                ref[to_chip, k] = narrow(
                    jnp.concatenate([grad_ref[pl.ds(at, half), :], extra], axis=0)
                )


def attention_backward(at, args, shards, copies):
    x = args[0]
    width = x.shape[0]
    half = width // shards // 2
    cells = SHARE * TOKENS
    bf16, f32 = jnp.bfloat16, jnp.float32

    def kernel(*refs):
        attention_backward_kernel(shards, *refs)

    return pl.pallas_call(
        kernel,
        grid_spec=pltpu.PrefetchScalarGridSpec(
            num_scalar_prefetch=1,
            grid=(),
            in_specs=[pl.BlockSpec(memory_space=pltpu.VMEM)] * len(args),
            out_specs=[pl.BlockSpec(memory_space=pltpu.VMEM)] * 3,
            scratch_shapes=[
                pltpu.VMEM((TOKENS, TOKENS), f32),
                pltpu.VMEM((GROUPS, HEAD_WIDTH, cells), bf16),
                pltpu.VMEM((GROUPS, HEAD_WIDTH, cells), f32),
                pltpu.VMEM((GROUPS, HEAD_WIDTH, TOKENS), f32),
                pltpu.VMEM((GROUPS, HEAD_WIDTH, TOKENS), f32),
                pltpu.VMEM((width, CHUNK), f32),
            ],
        ),
        out_shape=[
            jax.ShapeDtypeStruct((width, TOKENS), f32),
            jax.ShapeDtypeStruct((copies // 2, shards, half + 8, CHUNK), bf16),
            jax.ShapeDtypeStruct((copies // 2, shards, half + 8, CHUNK), bf16),
        ],
        compiler_params=pltpu.CompilerParams(vmem_limit_bytes=VMEM_LIMIT),
        cost_estimate=pl.CostEstimate(
            flops=int(3e9), bytes_accessed=9000000, transcendentals=1400000
        ),
        name="attention_backward",
    )(at, *args)


def unpack_attn_kernel(piece_ref, q_ref, k_ref, v_ref, o_ref):
    half = piece_ref.shape[1]
    columns = []
    for c in range(piece_ref.shape[0] // 2):
        columns.append(
            jnp.concatenate([widen(piece_ref[2 * c]), widen(piece_ref[2 * c + 1])], axis=0)
        )
    full = jnp.concatenate(columns, axis=1)
    kvw, width = k_ref.shape[1], o_ref.shape[1]
    k_ref[...] = full[:, :kvw]
    v_ref[...] = full[:, kvw : 2 * kvw]
    o_ref[...] = full[:, 2 * kvw : 2 * kvw + width]
    q_ref[...] = full[:, 2 * kvw + width :]


def unpack_attn(pieces, shapes):
    return pl.pallas_call(
        unpack_attn_kernel,
        out_shape=[jax.ShapeDtypeStruct(shape, jnp.float32) for shape in shapes],
        name="unpack_attn",
    )(pieces)


def unpack_mlp_kernel(piece_ref, gate_ref, up_ref, tall_ref):
    half = piece_ref.shape[2]
    for c in range(piece_ref.shape[0] // 2):
        for h in range(2):
            for m, ref in ((0, gate_ref), (1, up_ref)):
                ref[h * half : (h + 1) * half, c * CHUNK : (c + 1) * CHUNK] = widen(
                    piece_ref[2 * c + h, m]
                )
    for r in range(piece_ref.shape[0]):
        tall_ref[r * half : (r + 1) * half, :] = widen(piece_ref[r, 2])


def unpack_mlp(pieces, shapes):
    return pl.pallas_call(
        unpack_mlp_kernel,
        out_shape=[jax.ShapeDtypeStruct(shape, jnp.float32) for shape in shapes],
        name="unpack_mlp",
    )(pieces)


def fits_kernels(block_input, query_weight, key_weight, gate_weight, down_weight):
    return (
        lax.axis_size("rep") == 8
        and lax.axis_size("shard") == 4
        and block_input.shape == (1, TOKENS, 576)
        and query_weight.shape == (144, 576)
        and key_weight.shape == (144, 192)
        and gate_weight.shape == (144, 1536)
        and down_weight.shape == (384, 576)
    )


def gain_rows(gain_attn, gain_mlp, columns):
    both = jnp.zeros((8, columns), jnp.bfloat16)
    at = lax.axis_index("shard") * gain_attn.shape[0]
    return lax.dynamic_update_slice(both, jnp.stack([gain_attn, gain_mlp]), (0, at))


def swapped(values, bit):
    size = lax.axis_size("rep")
    return lax.ppermute(values, "rep", [(i, i ^ bit) for i in range(size)])


def plus(left, right):
    return narrow(widen(left) + widen(right))


def exchange_one(keep, came):
    tail = keep.shape[1:]
    mid = tail[0] // 2
    keep = keep.reshape((2, 2) + tail)
    came = came.reshape((2, 2) + tail)
    a_came = swapped(plus(keep[:, 1, :mid], came[:, 1, :mid]), 2)
    b_came = swapped(plus(keep[1, :, mid:], came[1, :, mid:]), 4)
    a_keep = plus(keep[:, 0, :mid], came[:, 0, :mid])
    b_keep = plus(keep[0, :, mid:], came[0, :, mid:])
    return a_keep, b_keep, a_came, b_came


def exchange_two(a_keep, b_keep, a_came, b_came):
    a_last = swapped(plus(a_keep[1], a_came[1]), 4)
    b_last = swapped(plus(b_keep[1], b_came[1]), 2)
    return a_last, b_last


def own_blocks(a_keep, b_keep, a_came, b_came, a_last, b_last):
    a = widen(a_keep[0]) + widen(a_came[0]) + widen(a_last)
    b = widen(b_keep[0]) + widen(b_came[0]) + widen(b_last)
    return [a[i] for i in range(a.shape[0])] + [b[i] for i in range(b.shape[0])]


def exchange_shards(blocks):
    return [shifted(narrow(blocks[k]), k) for k in range(1, len(blocks))]


def added(block, came):
    for value in came:
        block = block + widen(value)
    return block


def on_device(
    block_input,
    segment_ids,
    positions,
    query_weight,
    key_weight,
    value_weight,
    output_weight,
    gate_weight,
    up_weight,
    down_weight,
    gain_attn,
    gain_mlp,
    layer_output_cotangent,
):
    if not fits_kernels(block_input, query_weight, key_weight, gate_weight, down_weight):
        return on_device_generic(
            block_input,
            segment_ids,
            positions,
            query_weight,
            key_weight,
            value_weight,
            output_weight,
            gate_weight,
            up_weight,
            down_weight,
            gain_attn,
            gain_mlp,
            layer_output_cotangent,
        )
    shards, copies = lax.axis_size("shard"), lax.axis_size("rep")
    rank = lax.axis_index("rep")
    at = jnp.stack([lax.axis_index("shard"), rank // 2, rank % 2]).astype(jnp.int32)
    tall = jnp.transpose(down_weight)
    wide = jnp.stack([piece_of(gate_weight), piece_of(up_weight), row_piece_of(tall)])
    wide_came = [shifted(wide, k) for k in range(1, shards)]
    wide_pieces = lax.all_gather(jnp.stack(wide_came), "rep")
    half_dim = HEAD_WIDTH // 2
    frequency = ROPE_BASE ** (-(jnp.arange(half_dim, dtype=jnp.float32) * 2.0 / HEAD_WIDTH))
    angles = frequency[:, None] * positions.astype(jnp.float32)
    cosine, sine = jnp.cos(angles), jnp.sin(angles)
    row = segment_ids
    x = jnp.transpose(block_input[0])
    ct = jnp.transpose(layer_output_cotangent[0])
    own = jnp.concatenate([key_weight, value_weight, output_weight, query_weight], axis=1)
    gains_own = gain_rows(gain_attn, gain_mlp, own.shape[1])
    rows = own.shape[0]
    own_half = lax.dynamic_slice_in_dim(own, (rank % 2) * (rows // 2), rows // 2, 0)
    own_half = jnp.concatenate([own_half, gains_own])
    own_half, own, gains_own, cosine, sine, at, _ = lax.optimization_barrier(
        (own_half, own, gains_own, cosine, sine, at, wide_came[0])
    )
    mine = fetch_others(own_half)
    pair = swapped(mine, 1)

    w, gains, x2, q, k, v, o, lse = attention_forward(
        at, x, row, cosine, sine, own, gains_own, mine, pair, shards
    )
    out, dx2, gain_mlp_grad, wide_keep, wide_send = mlp(
        at, x2, ct, gains, gate_weight, up_weight, tall, wide_pieces, shards
    )
    wide_came = swapped(wide_send, 1)
    dx, attn_keep, attn_send = attention_backward(
        at,
        (x, dx2, row, cosine, sine, w, gains, q, k, v, o, lse, gain_mlp_grad),
        shards,
        copies,
    )
    barrier = lax.optimization_barrier
    wide_one = exchange_one(wide_keep, wide_came)
    wide_one, attn_send = barrier((wide_one, attn_send))
    attn_came = swapped(attn_send, 1)
    wide_two = exchange_two(*wide_one)
    wide_two, attn_came = barrier((wide_two, attn_came))
    wide_blocks = own_blocks(*wide_one, *wide_two)
    attn_one = exchange_one(attn_keep, attn_came)
    wide_last = exchange_shards(wide_blocks)
    wide_last, attn_one = barrier((wide_last, attn_one))
    wide_total = narrow(added(wide_blocks[0], wide_last))
    attn_two = exchange_two(*attn_one)
    attn_blocks = own_blocks(*attn_one, *attn_two)
    attn_total = added(attn_blocks[0], exchange_shards(attn_blocks))
    gate_grad, up_grad, tall_grad = unpack_mlp(
        lax.all_gather(wide_total, "rep"),
        (gate_weight.shape, up_weight.shape, tall.shape),
    )
    half = rows // 2
    q_grad, k_grad, v_grad, o_grad = unpack_attn(
        lax.all_gather(narrow(attn_total[:half]), "rep"),
        (query_weight.shape, key_weight.shape, value_weight.shape, output_weight.shape),
    )
    both = attn_total[half : half + 4].reshape(2, 2 * CHUNK)
    both = lax.dynamic_slice(both, (0, lax.axis_index("shard") * rows), (2, rows))
    return (
        jnp.transpose(out)[None],
        jnp.transpose(dx)[None],
        q_grad,
        k_grad,
        v_grad,
        o_grad,
        gate_grad,
        up_grad,
        jnp.transpose(tall_grad),
        both[0],
        both[1],
    )


def solution(mesh):
    placed = (
        P(("rep", "shard"), None, None),
        P(("rep", "shard"), None),
        P(("rep", "shard"), None),
        P("shard", None),
        P("shard", None),
        P("shard", None),
        P("shard", None),
        P("shard", None),
        P("shard", None),
        P("shard", None),
        P("shard"),
        P("shard"),
        P(("rep", "shard"), None, None),
    )
    return jax.shard_map(
        on_device,
        mesh=mesh,
        in_specs=placed,
        out_specs=(
            P(("rep", "shard"), None, None),
            P(("rep", "shard"), None, None),
            P("shard", None),
            P("shard", None),
            P("shard", None),
            P("shard", None),
            P("shard", None),
            P("shard", None),
            P("shard", None),
            P("shard"),
            P("shard"),
        ),
        check_vma=False,
    )
```

```python
import jax
import jax.numpy as jnp
from jax import lax
from jax.experimental import pallas as pl
from jax.experimental.pallas import tpu as pltpu
from jax.sharding import PartitionSpec as P

QUERY_HEADS = 9
KEY_VALUE_HEADS = 3
HEAD_WIDTH = 64


EPSILON = 1e-05
ROPE_BASE = 100000.0


def product_term(pattern, left_op, right_op):
    return jnp.einsum(pattern, left_op, right_op, preferred_element_type=jnp.float32)


def norm_stats(values):
    inverse = lax.rsqrt(jnp.mean(values * values, axis=-1, keepdims=True) + EPSILON)
    return (inverse, values * inverse)


def rope_tables(positions):
    half_dim = HEAD_WIDTH // 2
    frequency = ROPE_BASE ** (-(jnp.arange(half_dim, dtype=jnp.float32) * 2.0 / HEAD_WIDTH))
    angles = positions.astype(jnp.float32)[:, :, None] * frequency
    return (jnp.cos(angles)[:, :, None, :], jnp.sin(angles)[:, :, None, :])


def rotate(tensor, cosine_table, sine_table, direction):
    half_dim = HEAD_WIDTH // 2
    first_half = tensor[..., :half_dim]
    second_half = tensor[..., half_dim:]
    return jnp.concatenate(
        [
            first_half * cosine_table - direction * second_half * sine_table,
            second_half * cosine_table + direction * first_half * sine_table,
        ],
        axis=-1,
    )


def attention_mask(segment_ids):
    indices = jnp.arange(segment_ids.shape[1])
    causal = indices[:, None] >= indices[None, :]
    same_doc = segment_ids[:, :, None] == segment_ids[:, None, :]
    return (causal[None] & same_doc)[:, None, None]


def score_block(q_rot, k_rot, allowed):
    scores = product_term("sqgrh,skgh->sgrqk", q_rot, k_rot) * HEAD_WIDTH ** (-0.5)
    return jnp.where(allowed, scores, -1e30)


def forward_pass(weights, block_input, segment_ids, positions):
    (
        query_weight,
        key_weight,
        value_weight,
        output_weight,
        gate_weight,
        up_weight,
        down_weight,
        gain_attn,
        gain_mlp,
    ) = weights
    sequence_count, sequence_length, width = block_input.shape
    group_size = QUERY_HEADS // KEY_VALUE_HEADS
    q_width = QUERY_HEADS * HEAD_WIDTH
    residual_input = block_input.astype(jnp.float32)
    inv_attn, unit_attn = norm_stats(residual_input)
    attention_normalized = (unit_attn * gain_attn.astype(jnp.float32)).astype(jnp.bfloat16)
    cosine_table, sine_table = rope_tables(positions)
    query_projected = product_term("ifw,wq->ifq", attention_normalized, query_weight).reshape(
        sequence_count, sequence_length, QUERY_HEADS, HEAD_WIDTH
    )
    key_projected = product_term("ifw,wq->ifq", attention_normalized, key_weight).reshape(
        sequence_count, sequence_length, KEY_VALUE_HEADS, HEAD_WIDTH
    )
    value_projected = product_term("ifw,wq->ifq", attention_normalized, value_weight).reshape(
        sequence_count, sequence_length, KEY_VALUE_HEADS, HEAD_WIDTH
    )
    q_rot = rotate(query_projected, cosine_table, sine_table, 1.0).astype(jnp.bfloat16)
    q_rot = q_rot.reshape(sequence_count, sequence_length, KEY_VALUE_HEADS, group_size, HEAD_WIDTH)
    k_rot = rotate(key_projected, cosine_table, sine_table, 1.0).astype(jnp.bfloat16)
    value_b = value_projected.astype(jnp.bfloat16)
    allowed = attention_mask(segment_ids)
    scores = score_block(q_rot, k_rot, allowed)
    row_max = jnp.max(scores, axis=-1, keepdims=True)
    log_total = row_max + jnp.log(jnp.sum(jnp.exp(scores - row_max), axis=-1, keepdims=True))
    attn_probs = jnp.exp(scores - log_total).astype(jnp.bfloat16)
    attention_merged = (
        product_term("sgrqk,skgh->sqgrh", attn_probs, value_b)
        .reshape(sequence_count, sequence_length, q_width)
        .astype(jnp.bfloat16)
    )
    residual_middle = residual_input + product_term("gwb,ba->gwa", attention_merged, output_weight)
    inv_mlp, unit_mlp = norm_stats(residual_middle)
    feedforward_normalized = (unit_mlp * gain_mlp.astype(jnp.float32)).astype(jnp.bfloat16)
    gate_projected = product_term("qbg,gh->qbh", feedforward_normalized, gate_weight)
    up_projected = product_term("qbg,gh->qbh", feedforward_normalized, up_weight)
    hidden_state = (jax.nn.silu(gate_projected) * up_projected).astype(jnp.bfloat16)
    layer_result = residual_middle + product_term("jbw,wg->jbg", hidden_state, down_weight)
    stored = (
        inv_attn,
        unit_attn,
        attention_normalized,
        q_rot,
        k_rot,
        value_b,
        log_total,
        attention_merged,
        inv_mlp,
        unit_mlp,
        feedforward_normalized,
        gate_projected,
        up_projected,
        hidden_state,
    )
    return (layer_result, stored)


def backward_mlp(weights, layer_output_cotangent, stored):
    (
        query_weight,
        key_weight,
        value_weight,
        output_weight,
        gate_weight,
        up_weight,
        down_weight,
        gain_attn,
        gain_mlp,
    ) = weights
    inv_mlp, unit_mlp, feedforward_normalized, gate_projected, up_projected, hidden_state = stored[
        8:
    ]
    grad_out = layer_output_cotangent.astype(jnp.float32)
    activation_cotangent = product_term("zeo,ho->zeh", layer_output_cotangent, down_weight)
    down_weight_gradient = product_term("bux,bue->xe", layer_output_cotangent, hidden_state)
    gate_sigmoid = jax.nn.sigmoid(gate_projected)
    gate_cotangent = (
        activation_cotangent
        * up_projected
        * gate_sigmoid
        * (1.0 + gate_projected * (1.0 - gate_sigmoid))
    ).astype(jnp.bfloat16)
    up_cotangent = (activation_cotangent * gate_projected * gate_sigmoid).astype(jnp.bfloat16)
    gate_weight_gradient = product_term("avq,avc->qc", feedforward_normalized, gate_cotangent)
    up_weight_gradient = product_term("avq,avc->qc", feedforward_normalized, up_cotangent)
    normalized_cotangent = product_term("abo,mo->abm", gate_cotangent, gate_weight) + product_term(
        "abo,mo->abm", up_cotangent, up_weight
    )
    g_gain = jnp.sum(normalized_cotangent * unit_mlp, axis=(0, 1))
    d_unit = normalized_cotangent * gain_mlp.astype(jnp.float32)
    grad_mid = grad_out + inv_mlp * (
        d_unit - unit_mlp * jnp.mean(d_unit * unit_mlp, axis=-1, keepdims=True)
    )
    return (grad_mid, (gate_weight_gradient, up_weight_gradient, down_weight_gradient, g_gain))


def backward_attention(weights, segment_ids, positions, stored, grad_mid):
    (
        query_weight,
        key_weight,
        value_weight,
        output_weight,
        gate_weight,
        up_weight,
        down_weight,
        gain_attn,
        gain_mlp,
    ) = weights
    (
        inv_attn,
        unit_attn,
        attention_normalized,
        q_rot,
        k_rot,
        value_b,
        log_total,
        attention_merged,
    ) = stored[:8]
    sequence_count, sequence_length, width = grad_mid.shape
    group_size = QUERY_HEADS // KEY_VALUE_HEADS
    q_width = QUERY_HEADS * HEAD_WIDTH
    kv_width = KEY_VALUE_HEADS * HEAD_WIDTH
    block_gradient = grad_mid.astype(jnp.bfloat16)
    output_weight_gradient = product_term("uvc,uvn->cn", attention_merged, block_gradient)
    merged_cotangent = product_term("nuw,vw->nuv", block_gradient, output_weight).astype(
        jnp.bfloat16
    )
    merged_cotangent = merged_cotangent.reshape(
        sequence_count, sequence_length, KEY_VALUE_HEADS, group_size, HEAD_WIDTH
    )
    allowed = attention_mask(segment_ids)
    scores = score_block(q_rot, k_rot, allowed)
    attn_probs = jnp.exp(scores - log_total)
    d_value = product_term("sgrqk,sqgrh->skgh", attn_probs.astype(jnp.bfloat16), merged_cotangent)
    d_prob = product_term("sqgrh,skgh->sgrqk", merged_cotangent, value_b)
    mixed_heads = attention_merged.reshape(
        sequence_count, sequence_length, KEY_VALUE_HEADS, group_size, HEAD_WIDTH
    )
    row_delta = jnp.sum(
        merged_cotangent.astype(jnp.float32) * mixed_heads.astype(jnp.float32), axis=-1
    )
    row_delta = jnp.transpose(row_delta, (0, 2, 3, 1))[..., None]
    d_score = (attn_probs * (d_prob - row_delta) * HEAD_WIDTH ** (-0.5)).astype(jnp.bfloat16)
    d_query = product_term("sgrqk,skgh->sqgrh", d_score, k_rot).reshape(
        sequence_count, sequence_length, QUERY_HEADS, HEAD_WIDTH
    )
    d_key = product_term("sgrqk,sqgrh->skgh", d_score, q_rot)
    cosine_table, sine_table = rope_tables(positions)
    query_block_cotangent = (
        rotate(d_query, cosine_table, sine_table, -1.0)
        .astype(jnp.bfloat16)
        .reshape(sequence_count, sequence_length, q_width)
    )
    key_block_cotangent = (
        rotate(d_key, cosine_table, sine_table, -1.0)
        .astype(jnp.bfloat16)
        .reshape(sequence_count, sequence_length, kv_width)
    )
    value_block_cotangent = d_value.astype(jnp.bfloat16).reshape(
        sequence_count, sequence_length, kv_width
    )
    query_weight_gradient = product_term("uxj,uxc->jc", attention_normalized, query_block_cotangent)
    key_weight_gradient = product_term("uxj,uxc->jc", attention_normalized, key_block_cotangent)
    value_weight_gradient = product_term("uxj,uxc->jc", attention_normalized, value_block_cotangent)
    normalized_cotangent = (
        product_term("vcm,tm->vct", query_block_cotangent, query_weight)
        + product_term("vcm,tm->vct", key_block_cotangent, key_weight)
        + product_term("vcm,tm->vct", value_block_cotangent, value_weight)
    )
    g_gain = jnp.sum(normalized_cotangent * unit_attn, axis=(0, 1))
    d_unit = normalized_cotangent * gain_attn.astype(jnp.float32)
    grad_in = grad_mid + inv_attn * (
        d_unit - unit_attn * jnp.mean(d_unit * unit_attn, axis=-1, keepdims=True)
    )
    return (
        grad_in,
        (
            query_weight_gradient,
            key_weight_gradient,
            value_weight_gradient,
            output_weight_gradient,
            g_gain,
        ),
    )


def shifted(values, steps):
    size = lax.axis_size("shard")
    return lax.ppermute(values, "shard", [(i, (i + steps) % size) for i in range(size)])


def piece_of(block):
    copies = lax.axis_size("rep")
    me = lax.axis_index("rep")
    rows, columns = block.shape[0] // 2, block.shape[1] // (copies // 2)
    return lax.dynamic_slice(block, ((me % 2) * rows, (me // 2) * columns), (rows, columns))


def row_piece_of(block):
    copies = lax.axis_size("rep")
    rows = block.shape[0] // copies
    return lax.dynamic_slice_in_dim(block, lax.axis_index("rep") * rows, rows, 0)


def fetch_others(piece):
    size = lax.axis_size("shard")
    return jnp.stack([shifted(piece, k) for k in range(1, size)])


def place_blocks(own, others):
    size = lax.axis_size("shard")
    me = lax.axis_index("shard")
    full = jnp.zeros((size,) + own.shape, own.dtype)
    full = lax.dynamic_update_index_in_dim(full, own, me, 0)
    for k in range(1, size):
        full = lax.dynamic_update_index_in_dim(full, others[k - 1], (me - k) % size, 0)
    return full.reshape((size * own.shape[0],) + own.shape[1:])


def join_pieces(gathered):
    copies = gathered.shape[0]
    lead, rows, columns = gathered.shape[1:]
    parts = gathered.reshape(copies // 2, 2, lead, rows, columns)
    return jnp.transpose(parts, (2, 1, 3, 0, 4)).reshape(lead, 2 * rows, copies // 2 * columns)


def split_pieces(full):
    size = lax.axis_size("shard")
    copies = lax.axis_size("rep")
    rows, columns = full.shape[0] // size // 2, full.shape[1] // (copies // 2)
    parts = full.astype(jnp.bfloat16).reshape(size, 2, rows, copies // 2, columns)
    return jnp.transpose(parts, (3, 1, 0, 2, 4)).reshape(copies, size, rows, columns)


def sum_over_shard(parts):
    size = lax.axis_size("shard")
    me = lax.axis_index("shard")
    total = lax.dynamic_index_in_dim(parts, me, 0, keepdims=False).astype(jnp.float32)
    for k in range(1, size):
        block = lax.dynamic_index_in_dim(parts, (me + k) % size, 0, keepdims=False)
        total = total + shifted(block, k).astype(jnp.float32)
    return total


def gather_weights(q, k, v, o, gate, up, down, gain_attn, gain_mlp):
    rows = q.shape[0]
    attn = jnp.concatenate([q, k, v, o], axis=1)
    attn_piece = piece_of(attn)
    gains = jnp.stack([gain_attn, gain_mlp])
    gains_pad = jnp.pad(gains, ((0, 6), (0, attn_piece.shape[1] - rows)))
    attn_others = fetch_others(jnp.concatenate([attn_piece, gains_pad]))
    half = attn_piece.shape[0]
    gains_full = place_blocks(gains, attn_others[:, half : half + 2, :rows])
    size = lax.axis_size("shard")
    gains_full = jnp.transpose(gains_full.reshape(size, 2, rows), (1, 0, 2)).reshape(2, size * rows)
    attn_gathered = lax.all_gather(attn_others[:, :half], "rep")
    attn_full = place_blocks(attn, join_pieces(attn_gathered))
    gate_piece = piece_of(gate)
    tall = jnp.transpose(down)
    tall_piece = row_piece_of(tall).reshape(gate_piece.shape)
    wide = jnp.stack([gate_piece, piece_of(up), tall_piece])
    wide_gathered = lax.all_gather(fetch_others(wide), "rep")
    gate_full = place_blocks(gate, join_pieces(wide_gathered[:, :, 0]))
    up_full = place_blocks(up, join_pieces(wide_gathered[:, :, 1]))
    tall_rows = jnp.transpose(wide_gathered[:, :, 2], (1, 0, 2, 3)).reshape((-1,) + tall.shape)
    down_full = jnp.transpose(place_blocks(down, jnp.transpose(tall_rows, (0, 2, 1))), (0, 1))
    a, b, c = q.shape[1], k.shape[1], v.shape[1]
    return (
        attn_full[:, :a],
        attn_full[:, a : a + b],
        attn_full[:, a + b : a + b + c],
        attn_full[:, a + b + c :],
        gate_full,
        up_full,
        down_full,
        gains_full[0],
        gains_full[1],
    )


def spread_pieces(piece):
    gathered = lax.all_gather(piece.astype(jnp.bfloat16), "rep")
    return join_pieces(gathered[:, None])[0].astype(jnp.float32)


def reduce_mlp(gate, up, tall):
    size = lax.axis_size("shard")
    copies = lax.axis_size("rep")
    gate_parts = split_pieces(gate)
    tall_parts = tall.astype(jnp.bfloat16).reshape(copies, tall.shape[0] // copies, size, -1)
    tall_parts = jnp.transpose(tall_parts, (0, 2, 1, 3))
    rows, columns = tall_parts.shape[2:]
    wide = jnp.stack([gate_parts, split_pieces(up), tall_parts.reshape(gate_parts.shape)], axis=2)
    shape = wide.shape[1:]
    wide = lax.psum_scatter(wide.reshape(-1, columns), "rep", scatter_dimension=0, tiled=True)
    wide = wide.reshape(shape)
    wide = sum_over_shard(wide).astype(jnp.bfloat16)
    wide = lax.all_gather(wide, "rep").astype(jnp.float32)
    tall_total = wide[:, 2].reshape(copies * rows, columns)
    return (
        join_pieces(wide[:, None, 0])[0],
        join_pieces(wide[:, None, 1])[0],
        jnp.transpose(tall_total),
    )


def reduce_attn(q, k, v, o, gain_attn, gain_mlp):
    size = lax.axis_size("shard")
    copies = lax.axis_size("rep")
    parts = split_pieces(jnp.concatenate([q, k, v, o], axis=1))
    half, columns = parts.shape[2:]
    gains = jnp.stack([gain_attn, gain_mlp]).reshape(2, size, -1).astype(jnp.bfloat16)
    rows = gains.shape[2]
    gains = jnp.pad(jnp.transpose(gains, (1, 0, 2)), ((0, 0), (0, 6), (0, columns - rows)))
    gains = jnp.broadcast_to(gains[None], (copies,) + gains.shape)
    parts = lax.psum_scatter(jnp.concatenate([parts, gains], axis=2), "rep", scatter_dimension=0)
    total = sum_over_shard(parts)
    full = spread_pieces(total[:half])
    a, b, c = q.shape[1], k.shape[1], v.shape[1]
    return (
        full[:, :a],
        full[:, a : a + b],
        full[:, a + b : a + b + c],
        full[:, a + b + c :],
        total[half, :rows],
        total[half + 1, :rows],
    )


def on_device_generic(
    block_input,
    segment_ids,
    positions,
    query_weight,
    key_weight,
    value_weight,
    output_weight,
    gate_weight,
    up_weight,
    down_weight,
    gain_attn,
    gain_mlp,
    layer_output_cotangent,
):
    weights = gather_weights(
        query_weight,
        key_weight,
        value_weight,
        output_weight,
        gate_weight,
        up_weight,
        down_weight,
        gain_attn,
        gain_mlp,
    )
    layer_result, stored = forward_pass(weights, block_input, segment_ids, positions)
    grad_mid, mlp_grads = backward_mlp(weights, layer_output_cotangent, stored)
    gate_total, up_total, down_total = reduce_mlp(*mlp_grads[:3])
    grad_in, attn_grads = backward_attention(weights, segment_ids, positions, stored, grad_mid)
    q_total, k_total, v_total, o_total, gain_attn_total, gain_mlp_total = reduce_attn(
        *attn_grads, mlp_grads[3]
    )
    return (
        layer_result.astype(jnp.bfloat16),
        grad_in,
        q_total,
        k_total,
        v_total,
        o_total,
        gate_total,
        up_total,
        down_total,
        gain_attn_total,
        gain_mlp_total,
    )


TOKENS = 384
CHUNK = 384
LANES = 128
GROUPS = KEY_VALUE_HEADS
SHARE = QUERY_HEADS // KEY_VALUE_HEADS
VMEM_LIMIT = 56 * 1024 * 1024


def dot(left, right, left_dim=1, right_dim=0):
    return lax.dot_general(
        left, right, (((left_dim,), (right_dim,)), ((), ())), preferred_element_type=jnp.float32
    )


def widen(values):
    return values.astype(jnp.float32)


def narrow(values):
    return values.astype(jnp.bfloat16)


def mask_bias(seg_row):
    shape = (TOKENS, TOKENS)
    seg_col = jnp.transpose(jnp.broadcast_to(seg_row, (LANES, TOKENS)))[:, 0:1]
    key_at = lax.broadcasted_iota(jnp.int32, shape, 0)
    query_at = lax.broadcasted_iota(jnp.int32, shape, 1)
    allowed = (key_at <= query_at) & (seg_col == seg_row)
    return jnp.where(allowed, 0.0, -1e30)


def turn(values, cosine, sine):
    half = HEAD_WIDTH // 2
    first, second = values[:half], values[half:]
    return jnp.concatenate(
        [first * cosine - second * sine, second * cosine + first * sine], axis=0
    )


def in_core_order(core, mine, pair):
    mine, pair = widen(mine), widen(pair)
    upper = jnp.where(core == 0, mine, pair)
    lower = jnp.where(core == 0, pair, mine)
    return narrow(jnp.concatenate([upper, lower], axis=0))


def attention_forward_kernel(
    shards, at_ref, x_ref, row_ref, cos_ref, sin_ref, own_ref, gain_own_ref, mine_ref,
    pair_ref, w_ref, gain_ref, x2_ref, q_ref, k_ref, v_ref, o_ref, lse_ref, bias_ref,
):
    z = at_ref[0]
    rows = own_ref.shape[0]
    half = rows // 2
    width = x_ref.shape[0]
    own_at = pl.multiple_of(z * rows, 16)
    w_ref[pl.ds(own_at, rows), :] = own_ref[...]
    gains = widen(gain_own_ref[...])
    for k in range(1, shards):
        at = pl.multiple_of(lax.rem(z + shards - k, shards) * rows, 16)
        gains = gains + widen(mine_ref[0, k - 1, half:])
        for c in range(mine_ref.shape[0]):
            to = lax.bitwise_xor(at_ref[1], c)
            w_ref[pl.ds(at, rows), c * CHUNK : (c + 1) * CHUNK] = in_core_order(
                at_ref[2], mine_ref[to, k - 1, :half], pair_ref[to, k - 1, :half]
            )
    spare = 5 * LANES - CHUNK
    gains = jnp.concatenate(
        [
            jnp.concatenate([gains[0:1], gains[1:2, :spare]], axis=1),
            jnp.concatenate([gains[2:3], gains[3:4, :spare]], axis=1),
            jnp.zeros((6, 5 * LANES), jnp.float32),
        ],
        axis=0,
    )
    turned = jnp.transpose(jnp.concatenate([gains] * (LANES // 8), axis=0))
    gain_ref[...] = turned[:width]
    x = widen(x_ref[...])
    inverse = lax.rsqrt(jnp.mean(x * x, axis=0, keepdims=True) + EPSILON)
    h1 = narrow(x * inverse * turned[:width, 0:1])
    kv = dot(w_ref[:, :CHUNK], h1, 0, 0)
    q = dot(w_ref[:, 896:], h1, 0, 0)[HEAD_WIDTH:]
    cosine, sine = cos_ref[...], sin_ref[...]
    bias_ref[...] = mask_bias(row_ref[...])
    for g in range(GROUPS):
        at = g * HEAD_WIDTH
        k_ref[g] = narrow(turn(kv[at : at + HEAD_WIDTH], cosine, sine))
        at = (GROUPS + g) * HEAD_WIDTH
        v_ref[g] = narrow(kv[at : at + HEAD_WIDTH])
        for r in range(SHARE):
            at = (g * SHARE + r) * HEAD_WIDTH
            q_ref[g, :, r * TOKENS : (r + 1) * TOKENS] = narrow(
                turn(q[at : at + HEAD_WIDTH], cosine, sine)
            )

    def one_group(g, carry):
        scores = dot(k_ref[g], q_ref[g], 0, 0) * HEAD_WIDTH ** (-0.5)
        bias = bias_ref[...]
        scores = scores + jnp.concatenate([bias] * SHARE, axis=1)
        top = jnp.max(scores, axis=0, keepdims=True)
        weight = jnp.exp(scores - top)
        total = jnp.sum(weight, axis=0, keepdims=True)
        lse_ref[g] = top + jnp.log(total)
        probs = narrow(weight * (1.0 / total))
        o_ref[g] = narrow(dot(v_ref[g], probs))
        return carry

    lax.fori_loop(0, GROUPS, one_group, 0)
    x2_ref[...] = x + dot(w_ref[:, CHUNK : CHUNK + width], joined_heads(o_ref), 0, 0)


def joined_heads(ref):
    return jnp.concatenate(
        [
            ref[g, :, r * TOKENS : (r + 1) * TOKENS]
            for g in range(GROUPS)
            for r in range(SHARE)
        ],
        axis=0,
    )


def attention_forward(at, x, row, cosine, sine, own, gain_own, mine, pair, shards):
    width = x.shape[0]
    cells = SHARE * TOKENS
    bf16, f32 = jnp.bfloat16, jnp.float32

    def kernel(*refs):
        attention_forward_kernel(shards, *refs)

    return pl.pallas_call(
        kernel,
        grid_spec=pltpu.PrefetchScalarGridSpec(
            num_scalar_prefetch=1,
            grid=(),
            in_specs=[pl.BlockSpec(memory_space=pltpu.VMEM)] * 8,
            out_specs=[pl.BlockSpec(memory_space=pltpu.VMEM)] * 8,
            scratch_shapes=[pltpu.VMEM((TOKENS, TOKENS), f32)],
        ),
        out_shape=[
            jax.ShapeDtypeStruct((shards * own.shape[0], own.shape[1]), bf16),
            jax.ShapeDtypeStruct((width, LANES), f32),
            jax.ShapeDtypeStruct((width, TOKENS), f32),
            jax.ShapeDtypeStruct((GROUPS, HEAD_WIDTH, cells), bf16),
            jax.ShapeDtypeStruct((GROUPS, HEAD_WIDTH, TOKENS), bf16),
            jax.ShapeDtypeStruct((GROUPS, HEAD_WIDTH, TOKENS), bf16),
            jax.ShapeDtypeStruct((GROUPS, HEAD_WIDTH, cells), bf16),
            jax.ShapeDtypeStruct((GROUPS, 1, cells), f32),
        ],
        compiler_params=pltpu.CompilerParams(vmem_limit_bytes=VMEM_LIMIT),
        cost_estimate=pl.CostEstimate(
            flops=int(1.5e9), bytes_accessed=8000000, transcendentals=2000000
        ),
        name="attention_forward",
    )(at, x, row, cosine, sine, own, gain_own, mine, pair)


def mlp_kernel(
    shards, at_ref, x2_ref, ctt_ref, gain_ref, gate_ref, up_ref, tall_ref, mine_ref,
    pair_ref, tall_mine_ref, tall_pair_ref,
    out_ref, dx2_ref, gain_grad_ref, keep_ref, send_ref,
    h2_ref, h2t_ref, ct_ref, acc_ref, dh2_ref, wg_ref, wu_ref, wd_ref,
    gg_ref, gu_ref, gd_ref,
):
    z, chip, core = at_ref[0], at_ref[1], at_ref[2]
    j = pl.program_id(0)
    rows = gate_ref.shape[0]
    half = rows // 2

    @pl.when(j == 0)
    def _():
        x2 = x2_ref[...]
        inverse = lax.rsqrt(jnp.mean(x2 * x2, axis=0, keepdims=True) + EPSILON)
        h2t = x2 * inverse * gain_ref[:, 1:2]
        h2t_ref[...] = narrow(h2t)
        h2_ref[...] = narrow(jnp.transpose(h2t))
        ct_ref[...] = narrow(jnp.transpose(widen(ctt_ref[...])))
        acc_ref[...] = x2
        dh2_ref[...] = jnp.zeros_like(dh2_ref)

    own_at = pl.multiple_of(z * rows, 16)
    wg_ref[pl.ds(own_at, rows), :] = gate_ref[...]
    wu_ref[pl.ds(own_at, rows), :] = up_ref[...]
    for k in range(1, shards):
        at = pl.multiple_of(lax.rem(z + shards - k, shards) * rows, 16)
        for m, ref in ((0, wg_ref), (1, wu_ref)):
            ref[pl.ds(at, rows), :] = in_core_order(
                core, mine_ref[0, k - 1, m], pair_ref[0, k - 1, m]
            )

    @pl.when(j == z)
    def _():
        wd_ref[...] = tall_ref[...]

    @pl.when(j != z)
    def _():
        for c in range(tall_mine_ref.shape[0]):
            to = lax.bitwise_xor(chip, c)
            wd_ref[c * rows : (c + 1) * rows, :] = in_core_order(
                core, tall_mine_ref[to, 0, 0], tall_pair_ref[to, 0, 0]
            )

    h2, ct = h2_ref[...], ct_ref[...]
    wg, wu, wd = wg_ref[...], wu_ref[...], wd_ref[...]
    gate, up = dot(h2, wg), dot(h2, wu)
    da = dot(ct, wd)
    sigmoid = 1.0 / (1.0 + jnp.exp(-gate))
    silu = gate * sigmoid
    act = narrow(silu * up)
    dg = narrow(da * up * sigmoid * (1.0 + gate * (1.0 - sigmoid)))
    du = narrow(da * silu)
    acc_ref[...] += dot(wd, act, 1, 1)
    dh2_ref[...] += dot(wg, dg, 1, 1) + dot(wu, du, 1, 1)
    gg_ref[...] = dot(h2t_ref[...], dg)
    gu_ref[...] = dot(h2t_ref[...], du)
    gd_ref[...] = dot(ctt_ref[...], act)
    to_chip = lax.bitwise_xor(j, chip)
    to_shard = lax.rem(j + shards - z, shards)
    for rel, ref in ((0, keep_ref), (1, send_ref)):
        to_core = lax.bitwise_xor(core, rel)
        for k in range(shards):
            at = lax.rem(z + k, shards) * rows + to_core * half
            at = pl.multiple_of(at, 8)
            ref[to_chip, k, 0] = narrow(gg_ref[pl.ds(at, half), :])
            ref[to_chip, k, 1] = narrow(gu_ref[pl.ds(at, half), :])
        for c in range(4):
            at = (2 * lax.bitwise_xor(chip, c) + to_core) * half
            at = pl.multiple_of(at, 8)
            ref[c, to_shard, 2] = narrow(gd_ref[pl.ds(at, half), :])

    @pl.when(j == pl.num_programs(0) - 1)
    def _():
        out_ref[...] = narrow(acc_ref[...])
        dh2, x2 = dh2_ref[...], x2_ref[...]
        inverse = lax.rsqrt(jnp.mean(x2 * x2, axis=0, keepdims=True) + EPSILON)
        u2 = x2 * inverse
        gain_grad = jnp.sum(dh2 * u2, axis=1, keepdims=True)
        gain_grad_ref[...] = jnp.broadcast_to(gain_grad, gain_grad_ref.shape)
        n2 = dh2 * gain_ref[:, 1:2]
        mean = jnp.mean(n2 * u2, axis=0, keepdims=True)
        dx2_ref[...] = widen(ctt_ref[...]) + inverse * (n2 - u2 * mean)


def mlp(at, x2, ct, gains, gate, up, tall, mine, pair, shards):
    width = x2.shape[0]
    copies = 2 * mine.shape[0]
    rows, ff = gate.shape
    half = rows // 2
    bf16, f32 = jnp.bfloat16, jnp.float32

    def kernel(*refs):
        mlp_kernel(shards, *refs)

    def wide_block(j, at_ref):
        return (lax.bitwise_xor(j, at_ref[1]), 0, 0, 0, 0)

    def tall_block(j, at_ref):
        return (0, jnp.maximum(lax.rem(at_ref[0] + shards - j, shards) - 1, 0), 2, 0, 0)

    whole = lambda shape: pl.BlockSpec(shape, lambda j, at_ref: (0,) * len(shape))
    return pl.pallas_call(
        kernel,
        grid_spec=pltpu.PrefetchScalarGridSpec(
            num_scalar_prefetch=1,
            grid=(ff // CHUNK,),
            in_specs=[
                whole((width, TOKENS)),
                whole((width, TOKENS)),
                whole((width, LANES)),
                pl.BlockSpec((rows, CHUNK), lambda j, at_ref: (0, j)),
                pl.BlockSpec((rows, CHUNK), lambda j, at_ref: (0, j)),
                whole((width, CHUNK)),
                pl.BlockSpec((1, shards - 1, 2, half, CHUNK), wide_block),
                pl.BlockSpec((1, shards - 1, 2, half, CHUNK), wide_block),
                pl.BlockSpec((copies // 2, 1, 1, half, CHUNK), tall_block),
                pl.BlockSpec((copies // 2, 1, 1, half, CHUNK), tall_block),
            ],
            out_specs=[
                whole((width, TOKENS)),
                whole((width, TOKENS)),
                whole((width, LANES)),
                whole((copies // 2, shards, 3, half, CHUNK)),
                whole((copies // 2, shards, 3, half, CHUNK)),
            ],
            scratch_shapes=[
                pltpu.VMEM((TOKENS, width), bf16),
                pltpu.VMEM((width, TOKENS), bf16),
                pltpu.VMEM((TOKENS, width), bf16),
                pltpu.VMEM((width, TOKENS), f32),
                pltpu.VMEM((width, TOKENS), f32),
                pltpu.VMEM((width, CHUNK), bf16),
                pltpu.VMEM((width, CHUNK), bf16),
                pltpu.VMEM((width, CHUNK), bf16),
                pltpu.VMEM((width, CHUNK), f32),
                pltpu.VMEM((width, CHUNK), f32),
                pltpu.VMEM((width, CHUNK), f32),
            ],
        ),
        out_shape=[
            jax.ShapeDtypeStruct((width, TOKENS), bf16),
            jax.ShapeDtypeStruct((width, TOKENS), f32),
            jax.ShapeDtypeStruct((width, LANES), f32),
            jax.ShapeDtypeStruct((copies // 2, shards, 3, half, CHUNK), bf16),
            jax.ShapeDtypeStruct((copies // 2, shards, 3, half, CHUNK), bf16),
        ],
        compiler_params=pltpu.CompilerParams(
            vmem_limit_bytes=VMEM_LIMIT, dimension_semantics=("arbitrary",)
        ),
        cost_estimate=pl.CostEstimate(
            flops=int(6.2e9), bytes_accessed=14000000, transcendentals=1200000
        ),
        name="mlp",
    )(at, x2, ct, gains, gate, up, tall, mine, pair, mine, pair)


def attention_backward_kernel(
    shards, at_ref, x_ref, dx2_ref, row_ref, cos_ref, sin_ref, w_ref, gain_ref, q_ref,
    k_ref, v_ref, o_ref, lse_ref, gain_grad_ref,
    dx_ref, keep_ref, send_ref,
    bias_ref, do_ref, dq_ref, dk_ref, dv_ref, grad_ref,
):
    z, chip, core = at_ref[0], at_ref[1], at_ref[2]
    width = x_ref.shape[0]
    rows = width // shards
    half = rows // 2
    x = widen(x_ref[...])
    inverse = lax.rsqrt(jnp.mean(x * x, axis=0, keepdims=True) + EPSILON)
    u1 = x * inverse
    gain_attn = gain_ref[:, 0:1]
    h1t = narrow(u1 * gain_attn)
    gx = narrow(dx2_ref[...])
    cosine, sine = cos_ref[...], sin_ref[...]
    bias_ref[...] = mask_bias(row_ref[...])
    do = narrow(dot(w_ref[:, CHUNK : CHUNK + width], gx))
    for g in range(GROUPS):
        for r in range(SHARE):
            at = (g * SHARE + r) * HEAD_WIDTH
            do_ref[g, :, r * TOKENS : (r + 1) * TOKENS] = do[at : at + HEAD_WIDTH]

    def one_group(g, carry):
        bias = bias_ref[...]
        scores = dot(k_ref[g], q_ref[g], 0, 0) * HEAD_WIDTH ** (-0.5)
        scores = scores + jnp.concatenate([bias] * SHARE, axis=1)
        probs = jnp.exp(scores - lse_ref[g])
        do_g = do_ref[g]
        dv_ref[g] = jnp.transpose(dot(narrow(probs), do_g, 1, 1))
        delta = jnp.sum(widen(do_g) * widen(o_ref[g]), axis=0, keepdims=True)
        dp = dot(v_ref[g], do_g, 0, 0)
        ds = narrow(probs * (dp - delta) * HEAD_WIDTH ** (-0.5))
        dq_ref[g] = dot(k_ref[g], ds)
        dk_ref[g] = jnp.transpose(dot(ds, q_ref[g], 1, 1))
        return carry

    lax.fori_loop(0, GROUPS, one_group, 0)
    dkv = [narrow(turn(dk_ref[g], cosine, -sine)) for g in range(GROUPS)]
    dkv = jnp.concatenate(dkv + [narrow(dv_ref[g]) for g in range(GROUPS)], axis=0)
    dq = [
        narrow(turn(dq_ref[g, :, r * TOKENS : (r + 1) * TOKENS], cosine, -sine))
        for g in range(GROUPS)
        for r in range(SHARE)
    ]
    zeros = jnp.zeros((HEAD_WIDTH, TOKENS), jnp.bfloat16)
    dq_padded = jnp.concatenate([zeros] + dq, axis=0)
    dq = jnp.concatenate(dq, axis=0)
    dh1 = dot(w_ref[:, :CHUNK], dkv) + dot(w_ref[:, 896:], dq_padded)
    gain_grad = jnp.sum(dh1 * u1, axis=1, keepdims=True)
    lane = lax.broadcasted_iota(jnp.int32, gain_grad_ref.shape, 1)
    both = jnp.transpose(jnp.where(lane == 0, gain_grad, gain_grad_ref[...]))
    gain_grad, gain_mlp_grad = both[0:1], both[1:2]
    n1 = dh1 * gain_attn
    mean = jnp.mean(n1 * u1, axis=0, keepdims=True)
    dx_ref[...] = dx2_ref[...] + inverse * (n1 - u1 * mean)
    tail = width - CHUNK
    blank = jnp.zeros((1, CHUNK - tail), jnp.float32)
    extra = jnp.concatenate(
        [
            gain_grad[:, :CHUNK],
            jnp.concatenate([gain_grad[:, CHUNK:], blank], axis=1),
            gain_mlp_grad[:, :CHUNK],
            jnp.concatenate([gain_mlp_grad[:, CHUNK:], blank], axis=1),
            jnp.zeros((4, CHUNK), jnp.float32),
        ],
        axis=0,
    )
    o = joined_heads(o_ref)
    for c in range(4):
        if c == 0:
            grad = dot(h1t, dkv, 1, 1)
        elif c == 1:
            grad = dot(o, gx[:CHUNK], 1, 1)
        elif c == 2:
            grad = jnp.concatenate(
                [dot(o, gx[CHUNK:], 1, 1), dot(h1t, dq[: CHUNK - tail], 1, 1)], axis=1
            )
        else:
            grad = dot(h1t, dq[CHUNK - tail :], 1, 1)
        grad_ref[...] = grad
        to_chip = lax.bitwise_xor(chip, c)
        for rel, ref in ((0, keep_ref), (1, send_ref)):
            for k in range(shards):
                at = lax.rem(z + k, shards) * rows + lax.bitwise_xor(core, rel) * half
                at = pl.multiple_of(at, 8)
                ref[to_chip, k] = narrow(
                    jnp.concatenate([grad_ref[pl.ds(at, half), :], extra], axis=0)
                )


def attention_backward(at, args, shards, copies):
    x = args[0]
    width = x.shape[0]
    half = width // shards // 2
    cells = SHARE * TOKENS
    bf16, f32 = jnp.bfloat16, jnp.float32

    def kernel(*refs):
        attention_backward_kernel(shards, *refs)

    return pl.pallas_call(
        kernel,
        grid_spec=pltpu.PrefetchScalarGridSpec(
            num_scalar_prefetch=1,
            grid=(),
            in_specs=[pl.BlockSpec(memory_space=pltpu.VMEM)] * len(args),
            out_specs=[pl.BlockSpec(memory_space=pltpu.VMEM)] * 3,
            scratch_shapes=[
                pltpu.VMEM((TOKENS, TOKENS), f32),
                pltpu.VMEM((GROUPS, HEAD_WIDTH, cells), bf16),
                pltpu.VMEM((GROUPS, HEAD_WIDTH, cells), f32),
                pltpu.VMEM((GROUPS, HEAD_WIDTH, TOKENS), f32),
                pltpu.VMEM((GROUPS, HEAD_WIDTH, TOKENS), f32),
                pltpu.VMEM((width, CHUNK), f32),
            ],
        ),
        out_shape=[
            jax.ShapeDtypeStruct((width, TOKENS), f32),
            jax.ShapeDtypeStruct((copies // 2, shards, half + 8, CHUNK), bf16),
            jax.ShapeDtypeStruct((copies // 2, shards, half + 8, CHUNK), bf16),
        ],
        compiler_params=pltpu.CompilerParams(vmem_limit_bytes=VMEM_LIMIT),
        cost_estimate=pl.CostEstimate(
            flops=int(3e9), bytes_accessed=9000000, transcendentals=1400000
        ),
        name="attention_backward",
    )(at, *args)


def unpack_attn_kernel(piece_ref, q_ref, k_ref, v_ref, o_ref):
    half = piece_ref.shape[1]
    columns = []
    for c in range(piece_ref.shape[0] // 2):
        columns.append(
            jnp.concatenate([widen(piece_ref[2 * c]), widen(piece_ref[2 * c + 1])], axis=0)
        )
    full = jnp.concatenate(columns, axis=1)
    kvw, width = k_ref.shape[1], o_ref.shape[1]
    k_ref[...] = full[:, :kvw]
    v_ref[...] = full[:, kvw : 2 * kvw]
    o_ref[...] = full[:, 2 * kvw : 2 * kvw + width]
    q_ref[...] = full[:, 2 * kvw + width :]


def unpack_attn(pieces, shapes):
    return pl.pallas_call(
        unpack_attn_kernel,
        out_shape=[jax.ShapeDtypeStruct(shape, jnp.float32) for shape in shapes],
        name="unpack_attn",
    )(pieces)


def unpack_mlp_kernel(at_ref, mine_ref, pair_ref, gate_ref, up_ref, tall_ref):
    chip, core = at_ref[1], at_ref[2]
    half = mine_ref.shape[2]
    for c in range(mine_ref.shape[0]):
        to = lax.bitwise_xor(chip, c)
        for m in range(3):
            mine, pair = widen(mine_ref[to, m]), widen(pair_ref[to, m])
            upper = jnp.where(core == 0, mine, pair)
            lower = jnp.where(core == 0, pair, mine)
            if m < 2:
                ref = (gate_ref, up_ref)[m]
                ref[:half, c * CHUNK : (c + 1) * CHUNK] = upper
                ref[half:, c * CHUNK : (c + 1) * CHUNK] = lower
            else:
                tall_ref[2 * c * half : (2 * c + 1) * half, :] = upper
                tall_ref[(2 * c + 1) * half : (2 * c + 2) * half, :] = lower


def unpack_mlp(at, mine, pair, shapes):
    return pl.pallas_call(
        unpack_mlp_kernel,
        grid_spec=pltpu.PrefetchScalarGridSpec(
            num_scalar_prefetch=1,
            grid=(),
            in_specs=[pl.BlockSpec(memory_space=pltpu.VMEM)] * 2,
            out_specs=[pl.BlockSpec(memory_space=pltpu.VMEM)] * 3,
        ),
        out_shape=[jax.ShapeDtypeStruct(shape, jnp.float32) for shape in shapes],
        name="unpack_mlp",
    )(at, mine, pair)


def fits_kernels(block_input, query_weight, key_weight, gate_weight, down_weight):
    return (
        lax.axis_size("rep") == 8
        and lax.axis_size("shard") == 4
        and block_input.shape == (1, TOKENS, 576)
        and query_weight.shape == (144, 576)
        and key_weight.shape == (144, 192)
        and gate_weight.shape == (144, 1536)
        and down_weight.shape == (384, 576)
    )


def gain_rows(gain_attn, gain_mlp):
    both = jnp.zeros((2, 2 * CHUNK), jnp.bfloat16)
    at = lax.axis_index("shard") * gain_attn.shape[0]
    both = lax.dynamic_update_slice(both, jnp.stack([gain_attn, gain_mlp]), (0, at))
    return jnp.pad(both.reshape(4, CHUNK), ((0, 4), (0, 0)))


def swapped(values, bit):
    size = lax.axis_size("rep")
    return lax.ppermute(values, "rep", [(i, i ^ bit) for i in range(size)])


def plane_gather(own):
    from_x, from_y = swapped(own, 2), swapped(own, 4)
    mine = jnp.stack([own, from_x, from_y, swapped(from_y, 2)])
    return mine, swapped(mine, 1)


def plus(left, right):
    return narrow(widen(left) + widen(right))


def exchange_one(keep, came):
    tail = keep.shape[1:]
    mid = tail[0] // 2
    keep = keep.reshape((2, 2) + tail)
    came = came.reshape((2, 2) + tail)
    a_came = swapped(plus(keep[:, 1, :mid], came[:, 1, :mid]), 2)
    b_came = swapped(plus(keep[1, :, mid:], came[1, :, mid:]), 4)
    a_keep = plus(keep[:, 0, :mid], came[:, 0, :mid])
    b_keep = plus(keep[0, :, mid:], came[0, :, mid:])
    return a_keep, b_keep, a_came, b_came


def exchange_two(a_keep, b_keep, a_came, b_came):
    a_last = swapped(plus(a_keep[1], a_came[1]), 4)
    b_last = swapped(plus(b_keep[1], b_came[1]), 2)
    return a_last, b_last


def own_blocks(a_keep, b_keep, a_came, b_came, a_last, b_last):
    a = widen(a_keep[0]) + widen(a_came[0]) + widen(a_last)
    b = widen(b_keep[0]) + widen(b_came[0]) + widen(b_last)
    return [a[i] for i in range(a.shape[0])] + [b[i] for i in range(b.shape[0])]


def exchange_shards(blocks):
    return [shifted(narrow(blocks[k]), k) for k in range(1, len(blocks))]


def added(block, came):
    for value in came:
        block = block + widen(value)
    return block


def on_device(
    block_input,
    segment_ids,
    positions,
    query_weight,
    key_weight,
    value_weight,
    output_weight,
    gate_weight,
    up_weight,
    down_weight,
    gain_attn,
    gain_mlp,
    layer_output_cotangent,
):
    if not fits_kernels(block_input, query_weight, key_weight, gate_weight, down_weight):
        return on_device_generic(
            block_input,
            segment_ids,
            positions,
            query_weight,
            key_weight,
            value_weight,
            output_weight,
            gate_weight,
            up_weight,
            down_weight,
            gain_attn,
            gain_mlp,
            layer_output_cotangent,
        )
    shards, copies = lax.axis_size("shard"), lax.axis_size("rep")
    rank = lax.axis_index("rep")
    at = jnp.stack([lax.axis_index("shard"), rank // 2, rank % 2]).astype(jnp.int32)
    barrier = lax.optimization_barrier
    own = jnp.concatenate([key_weight, value_weight, output_weight, query_weight], axis=1)
    rows = own.shape[0]
    gains_own = gain_rows(gain_attn, gain_mlp)
    attn_piece = jnp.concatenate([piece_of(own), gains_own])
    attn_came = [shifted(attn_piece, k) for k in range(1, shards)]
    tall = jnp.transpose(down_weight)
    wide = jnp.stack([piece_of(gate_weight), piece_of(up_weight), row_piece_of(tall)])
    wide_came = [shifted(wide, k) for k in range(1, shards)]
    half_dim = HEAD_WIDTH // 2
    frequency = ROPE_BASE ** (-(jnp.arange(half_dim, dtype=jnp.float32) * 2.0 / HEAD_WIDTH))
    angles = frequency[:, None] * positions.astype(jnp.float32)
    cosine, sine = jnp.cos(angles), jnp.sin(angles)
    row = segment_ids
    x = jnp.transpose(block_input[0])
    ct = jnp.transpose(layer_output_cotangent[0])
    attn_own = jnp.stack(attn_came)
    attn_x, attn_y = swapped(attn_own, 2), swapped(attn_own, 4)
    mine = jnp.stack([attn_own, attn_x, attn_y, swapped(attn_y, 2)])
    mine, wide_came, cosine, sine, at = barrier((mine, wide_came, cosine, sine, at))
    pair = swapped(mine, 1)
    wide_own = jnp.concatenate(wide_came)
    wide_x, wide_y = swapped(wide_own, 2), swapped(wide_own, 4)

    w, gains, x2, q, k, v, o, lse = attention_forward(
        at, x, row, cosine, sine, own, gains_own, mine, pair, shards
    )
    wide_x, wide_y, x2 = barrier((wide_x, wide_y, x2))
    mid = wide_own.shape[0] // 2
    across = jnp.concatenate([swapped(wide_y[:mid], 2), swapped(wide_x[mid:], 4)])
    wide_mine = jnp.stack([wide_own, wide_x, wide_y, across])
    wide_pair = swapped(wide_mine, 1)
    blocks = (-1, shards - 1, 3) + wide.shape[1:]
    wide_mine, wide_pair = wide_mine.reshape(blocks), wide_pair.reshape(blocks)
    out, dx2, gain_mlp_grad, wide_keep, wide_send = mlp(
        at, x2, ct, gains, gate_weight, up_weight, tall, wide_mine, wide_pair, shards
    )
    wide_came = swapped(wide_send, 1)
    dx, attn_keep, attn_send = attention_backward(
        at,
        (x, dx2, row, cosine, sine, w, gains, q, k, v, o, lse, gain_mlp_grad),
        shards,
        copies,
    )
    wide_one = exchange_one(wide_keep, wide_came)
    wide_one, attn_send = barrier((wide_one, attn_send))
    attn_came = swapped(attn_send, 1)
    wide_two = exchange_two(*wide_one)
    wide_two, attn_came = barrier((wide_two, attn_came))
    wide_blocks = own_blocks(*wide_one, *wide_two)
    attn_one = exchange_one(attn_keep, attn_came)
    wide_last = exchange_shards(wide_blocks)
    wide_last, attn_one = barrier((wide_last, attn_one))
    wide_total = narrow(added(wide_blocks[0], wide_last))
    attn_two = exchange_two(*attn_one)
    attn_blocks = own_blocks(*attn_one, *attn_two)
    attn_total = added(attn_blocks[0], exchange_shards(attn_blocks))
    half = rows // 2
    total_mine, total_pair = plane_gather(wide_total)
    attn_pieces = lax.all_gather(narrow(attn_total[:half]), "rep")
    total_pair, attn_pieces = barrier((total_pair, attn_pieces))
    q_grad, k_grad, v_grad, o_grad = unpack_attn(
        attn_pieces,
        (query_weight.shape, key_weight.shape, value_weight.shape, output_weight.shape),
    )
    gate_grad, up_grad, tall_grad = unpack_mlp(
        at,
        total_mine,
        total_pair,
        (gate_weight.shape, up_weight.shape, tall.shape),
    )
    both = attn_total[half : half + 4].reshape(2, 2 * CHUNK)
    both = lax.dynamic_slice(both, (0, lax.axis_index("shard") * rows), (2, rows))
    return (
        jnp.transpose(out)[None],
        jnp.transpose(dx)[None],
        q_grad,
        k_grad,
        v_grad,
        o_grad,
        gate_grad,
        up_grad,
        jnp.transpose(tall_grad),
        both[0],
        both[1],
    )


def solution(mesh):
    placed = (
        P(("rep", "shard"), None, None),
        P(("rep", "shard"), None),
        P(("rep", "shard"), None),
        P("shard", None),
        P("shard", None),
        P("shard", None),
        P("shard", None),
        P("shard", None),
        P("shard", None),
        P("shard", None),
        P("shard"),
        P("shard"),
        P(("rep", "shard"), None, None),
    )
    return jax.shard_map(
        on_device,
        mesh=mesh,
        in_specs=placed,
        out_specs=(
            P(("rep", "shard"), None, None),
            P(("rep", "shard"), None, None),
            P("shard", None),
            P("shard", None),
            P("shard", None),
            P("shard", None),
            P("shard", None),
            P("shard", None),
            P("shard", None),
            P("shard"),
            P("shard"),
        ),
        check_vma=False,
    )
```

```python
import jax
import jax.numpy as jnp
from jax import lax
from jax.experimental import pallas as pl
from jax.experimental.pallas import tpu as pltpu
from jax.sharding import PartitionSpec as P

QUERY_HEADS = 9
KEY_VALUE_HEADS = 3
HEAD_WIDTH = 64


EPSILON = 1e-05
ROPE_BASE = 100000.0


def product_term(pattern, left_op, right_op):
    return jnp.einsum(pattern, left_op, right_op, preferred_element_type=jnp.float32)


def norm_stats(values):
    inverse = lax.rsqrt(jnp.mean(values * values, axis=-1, keepdims=True) + EPSILON)
    return (inverse, values * inverse)


def rope_tables(positions):
    half_dim = HEAD_WIDTH // 2
    frequency = ROPE_BASE ** (-(jnp.arange(half_dim, dtype=jnp.float32) * 2.0 / HEAD_WIDTH))
    angles = positions.astype(jnp.float32)[:, :, None] * frequency
    return (jnp.cos(angles)[:, :, None, :], jnp.sin(angles)[:, :, None, :])


def rotate(tensor, cosine_table, sine_table, direction):
    half_dim = HEAD_WIDTH // 2
    first_half = tensor[..., :half_dim]
    second_half = tensor[..., half_dim:]
    return jnp.concatenate(
        [
            first_half * cosine_table - direction * second_half * sine_table,
            second_half * cosine_table + direction * first_half * sine_table,
        ],
        axis=-1,
    )


def attention_mask(segment_ids):
    indices = jnp.arange(segment_ids.shape[1])
    causal = indices[:, None] >= indices[None, :]
    same_doc = segment_ids[:, :, None] == segment_ids[:, None, :]
    return (causal[None] & same_doc)[:, None, None]


def score_block(q_rot, k_rot, allowed):
    scores = product_term("sqgrh,skgh->sgrqk", q_rot, k_rot) * HEAD_WIDTH ** (-0.5)
    return jnp.where(allowed, scores, -1e30)


def forward_pass(weights, block_input, segment_ids, positions):
    (
        query_weight,
        key_weight,
        value_weight,
        output_weight,
        gate_weight,
        up_weight,
        down_weight,
        gain_attn,
        gain_mlp,
    ) = weights
    sequence_count, sequence_length, width = block_input.shape
    group_size = QUERY_HEADS // KEY_VALUE_HEADS
    q_width = QUERY_HEADS * HEAD_WIDTH
    residual_input = block_input.astype(jnp.float32)
    inv_attn, unit_attn = norm_stats(residual_input)
    attention_normalized = (unit_attn * gain_attn.astype(jnp.float32)).astype(jnp.bfloat16)
    cosine_table, sine_table = rope_tables(positions)
    query_projected = product_term("ifw,wq->ifq", attention_normalized, query_weight).reshape(
        sequence_count, sequence_length, QUERY_HEADS, HEAD_WIDTH
    )
    key_projected = product_term("ifw,wq->ifq", attention_normalized, key_weight).reshape(
        sequence_count, sequence_length, KEY_VALUE_HEADS, HEAD_WIDTH
    )
    value_projected = product_term("ifw,wq->ifq", attention_normalized, value_weight).reshape(
        sequence_count, sequence_length, KEY_VALUE_HEADS, HEAD_WIDTH
    )
    q_rot = rotate(query_projected, cosine_table, sine_table, 1.0).astype(jnp.bfloat16)
    q_rot = q_rot.reshape(sequence_count, sequence_length, KEY_VALUE_HEADS, group_size, HEAD_WIDTH)
    k_rot = rotate(key_projected, cosine_table, sine_table, 1.0).astype(jnp.bfloat16)
    value_b = value_projected.astype(jnp.bfloat16)
    allowed = attention_mask(segment_ids)
    scores = score_block(q_rot, k_rot, allowed)
    row_max = jnp.max(scores, axis=-1, keepdims=True)
    log_total = row_max + jnp.log(jnp.sum(jnp.exp(scores - row_max), axis=-1, keepdims=True))
    attn_probs = jnp.exp(scores - log_total).astype(jnp.bfloat16)
    attention_merged = (
        product_term("sgrqk,skgh->sqgrh", attn_probs, value_b)
        .reshape(sequence_count, sequence_length, q_width)
        .astype(jnp.bfloat16)
    )
    residual_middle = residual_input + product_term("gwb,ba->gwa", attention_merged, output_weight)
    inv_mlp, unit_mlp = norm_stats(residual_middle)
    feedforward_normalized = (unit_mlp * gain_mlp.astype(jnp.float32)).astype(jnp.bfloat16)
    gate_projected = product_term("qbg,gh->qbh", feedforward_normalized, gate_weight)
    up_projected = product_term("qbg,gh->qbh", feedforward_normalized, up_weight)
    hidden_state = (jax.nn.silu(gate_projected) * up_projected).astype(jnp.bfloat16)
    layer_result = residual_middle + product_term("jbw,wg->jbg", hidden_state, down_weight)
    stored = (
        inv_attn,
        unit_attn,
        attention_normalized,
        q_rot,
        k_rot,
        value_b,
        log_total,
        attention_merged,
        inv_mlp,
        unit_mlp,
        feedforward_normalized,
        gate_projected,
        up_projected,
        hidden_state,
    )
    return (layer_result, stored)


def backward_mlp(weights, layer_output_cotangent, stored):
    (
        query_weight,
        key_weight,
        value_weight,
        output_weight,
        gate_weight,
        up_weight,
        down_weight,
        gain_attn,
        gain_mlp,
    ) = weights
    inv_mlp, unit_mlp, feedforward_normalized, gate_projected, up_projected, hidden_state = stored[
        8:
    ]
    grad_out = layer_output_cotangent.astype(jnp.float32)
    activation_cotangent = product_term("zeo,ho->zeh", layer_output_cotangent, down_weight)
    down_weight_gradient = product_term("bux,bue->xe", layer_output_cotangent, hidden_state)
    gate_sigmoid = jax.nn.sigmoid(gate_projected)
    gate_cotangent = (
        activation_cotangent
        * up_projected
        * gate_sigmoid
        * (1.0 + gate_projected * (1.0 - gate_sigmoid))
    ).astype(jnp.bfloat16)
    up_cotangent = (activation_cotangent * gate_projected * gate_sigmoid).astype(jnp.bfloat16)
    gate_weight_gradient = product_term("avq,avc->qc", feedforward_normalized, gate_cotangent)
    up_weight_gradient = product_term("avq,avc->qc", feedforward_normalized, up_cotangent)
    normalized_cotangent = product_term("abo,mo->abm", gate_cotangent, gate_weight) + product_term(
        "abo,mo->abm", up_cotangent, up_weight
    )
    g_gain = jnp.sum(normalized_cotangent * unit_mlp, axis=(0, 1))
    d_unit = normalized_cotangent * gain_mlp.astype(jnp.float32)
    grad_mid = grad_out + inv_mlp * (
        d_unit - unit_mlp * jnp.mean(d_unit * unit_mlp, axis=-1, keepdims=True)
    )
    return (grad_mid, (gate_weight_gradient, up_weight_gradient, down_weight_gradient, g_gain))


def backward_attention(weights, segment_ids, positions, stored, grad_mid):
    (
        query_weight,
        key_weight,
        value_weight,
        output_weight,
        gate_weight,
        up_weight,
        down_weight,
        gain_attn,
        gain_mlp,
    ) = weights
    (
        inv_attn,
        unit_attn,
        attention_normalized,
        q_rot,
        k_rot,
        value_b,
        log_total,
        attention_merged,
    ) = stored[:8]
    sequence_count, sequence_length, width = grad_mid.shape
    group_size = QUERY_HEADS // KEY_VALUE_HEADS
    q_width = QUERY_HEADS * HEAD_WIDTH
    kv_width = KEY_VALUE_HEADS * HEAD_WIDTH
    block_gradient = grad_mid.astype(jnp.bfloat16)
    output_weight_gradient = product_term("uvc,uvn->cn", attention_merged, block_gradient)
    merged_cotangent = product_term("nuw,vw->nuv", block_gradient, output_weight).astype(
        jnp.bfloat16
    )
    merged_cotangent = merged_cotangent.reshape(
        sequence_count, sequence_length, KEY_VALUE_HEADS, group_size, HEAD_WIDTH
    )
    allowed = attention_mask(segment_ids)
    scores = score_block(q_rot, k_rot, allowed)
    attn_probs = jnp.exp(scores - log_total)
    d_value = product_term("sgrqk,sqgrh->skgh", attn_probs.astype(jnp.bfloat16), merged_cotangent)
    d_prob = product_term("sqgrh,skgh->sgrqk", merged_cotangent, value_b)
    mixed_heads = attention_merged.reshape(
        sequence_count, sequence_length, KEY_VALUE_HEADS, group_size, HEAD_WIDTH
    )
    row_delta = jnp.sum(
        merged_cotangent.astype(jnp.float32) * mixed_heads.astype(jnp.float32), axis=-1
    )
    row_delta = jnp.transpose(row_delta, (0, 2, 3, 1))[..., None]
    d_score = (attn_probs * (d_prob - row_delta) * HEAD_WIDTH ** (-0.5)).astype(jnp.bfloat16)
    d_query = product_term("sgrqk,skgh->sqgrh", d_score, k_rot).reshape(
        sequence_count, sequence_length, QUERY_HEADS, HEAD_WIDTH
    )
    d_key = product_term("sgrqk,sqgrh->skgh", d_score, q_rot)
    cosine_table, sine_table = rope_tables(positions)
    query_block_cotangent = (
        rotate(d_query, cosine_table, sine_table, -1.0)
        .astype(jnp.bfloat16)
        .reshape(sequence_count, sequence_length, q_width)
    )
    key_block_cotangent = (
        rotate(d_key, cosine_table, sine_table, -1.0)
        .astype(jnp.bfloat16)
        .reshape(sequence_count, sequence_length, kv_width)
    )
    value_block_cotangent = d_value.astype(jnp.bfloat16).reshape(
        sequence_count, sequence_length, kv_width
    )
    query_weight_gradient = product_term("uxj,uxc->jc", attention_normalized, query_block_cotangent)
    key_weight_gradient = product_term("uxj,uxc->jc", attention_normalized, key_block_cotangent)
    value_weight_gradient = product_term("uxj,uxc->jc", attention_normalized, value_block_cotangent)
    normalized_cotangent = (
        product_term("vcm,tm->vct", query_block_cotangent, query_weight)
        + product_term("vcm,tm->vct", key_block_cotangent, key_weight)
        + product_term("vcm,tm->vct", value_block_cotangent, value_weight)
    )
    g_gain = jnp.sum(normalized_cotangent * unit_attn, axis=(0, 1))
    d_unit = normalized_cotangent * gain_attn.astype(jnp.float32)
    grad_in = grad_mid + inv_attn * (
        d_unit - unit_attn * jnp.mean(d_unit * unit_attn, axis=-1, keepdims=True)
    )
    return (
        grad_in,
        (
            query_weight_gradient,
            key_weight_gradient,
            value_weight_gradient,
            output_weight_gradient,
            g_gain,
        ),
    )


def shifted(values, steps):
    size = lax.axis_size("shard")
    return lax.ppermute(values, "shard", [(i, (i + steps) % size) for i in range(size)])


def piece_of(block):
    copies = lax.axis_size("rep")
    me = lax.axis_index("rep")
    rows, columns = block.shape[0] // 2, block.shape[1] // (copies // 2)
    return lax.dynamic_slice(block, ((me % 2) * rows, (me // 2) * columns), (rows, columns))


def row_piece_of(block):
    copies = lax.axis_size("rep")
    rows = block.shape[0] // copies
    return lax.dynamic_slice_in_dim(block, lax.axis_index("rep") * rows, rows, 0)


def fetch_others(piece):
    size = lax.axis_size("shard")
    return jnp.stack([shifted(piece, k) for k in range(1, size)])


def place_blocks(own, others):
    size = lax.axis_size("shard")
    me = lax.axis_index("shard")
    full = jnp.zeros((size,) + own.shape, own.dtype)
    full = lax.dynamic_update_index_in_dim(full, own, me, 0)
    for k in range(1, size):
        full = lax.dynamic_update_index_in_dim(full, others[k - 1], (me - k) % size, 0)
    return full.reshape((size * own.shape[0],) + own.shape[1:])


def join_pieces(gathered):
    copies = gathered.shape[0]
    lead, rows, columns = gathered.shape[1:]
    parts = gathered.reshape(copies // 2, 2, lead, rows, columns)
    return jnp.transpose(parts, (2, 1, 3, 0, 4)).reshape(lead, 2 * rows, copies // 2 * columns)


def split_pieces(full):
    size = lax.axis_size("shard")
    copies = lax.axis_size("rep")
    rows, columns = full.shape[0] // size // 2, full.shape[1] // (copies // 2)
    parts = full.astype(jnp.bfloat16).reshape(size, 2, rows, copies // 2, columns)
    return jnp.transpose(parts, (3, 1, 0, 2, 4)).reshape(copies, size, rows, columns)


def sum_over_shard(parts):
    size = lax.axis_size("shard")
    me = lax.axis_index("shard")
    total = lax.dynamic_index_in_dim(parts, me, 0, keepdims=False).astype(jnp.float32)
    for k in range(1, size):
        block = lax.dynamic_index_in_dim(parts, (me + k) % size, 0, keepdims=False)
        total = total + shifted(block, k).astype(jnp.float32)
    return total


def gather_weights(q, k, v, o, gate, up, down, gain_attn, gain_mlp):
    rows = q.shape[0]
    attn = jnp.concatenate([q, k, v, o], axis=1)
    attn_piece = piece_of(attn)
    gains = jnp.stack([gain_attn, gain_mlp])
    gains_pad = jnp.pad(gains, ((0, 6), (0, attn_piece.shape[1] - rows)))
    attn_others = fetch_others(jnp.concatenate([attn_piece, gains_pad]))
    half = attn_piece.shape[0]
    gains_full = place_blocks(gains, attn_others[:, half : half + 2, :rows])
    size = lax.axis_size("shard")
    gains_full = jnp.transpose(gains_full.reshape(size, 2, rows), (1, 0, 2)).reshape(2, size * rows)
    attn_gathered = lax.all_gather(attn_others[:, :half], "rep")
    attn_full = place_blocks(attn, join_pieces(attn_gathered))
    gate_piece = piece_of(gate)
    tall = jnp.transpose(down)
    tall_piece = row_piece_of(tall).reshape(gate_piece.shape)
    wide = jnp.stack([gate_piece, piece_of(up), tall_piece])
    wide_gathered = lax.all_gather(fetch_others(wide), "rep")
    gate_full = place_blocks(gate, join_pieces(wide_gathered[:, :, 0]))
    up_full = place_blocks(up, join_pieces(wide_gathered[:, :, 1]))
    tall_rows = jnp.transpose(wide_gathered[:, :, 2], (1, 0, 2, 3)).reshape((-1,) + tall.shape)
    down_full = jnp.transpose(place_blocks(down, jnp.transpose(tall_rows, (0, 2, 1))), (0, 1))
    a, b, c = q.shape[1], k.shape[1], v.shape[1]
    return (
        attn_full[:, :a],
        attn_full[:, a : a + b],
        attn_full[:, a + b : a + b + c],
        attn_full[:, a + b + c :],
        gate_full,
        up_full,
        down_full,
        gains_full[0],
        gains_full[1],
    )


def spread_pieces(piece):
    gathered = lax.all_gather(piece.astype(jnp.bfloat16), "rep")
    return join_pieces(gathered[:, None])[0].astype(jnp.float32)


def reduce_mlp(gate, up, tall):
    size = lax.axis_size("shard")
    copies = lax.axis_size("rep")
    gate_parts = split_pieces(gate)
    tall_parts = tall.astype(jnp.bfloat16).reshape(copies, tall.shape[0] // copies, size, -1)
    tall_parts = jnp.transpose(tall_parts, (0, 2, 1, 3))
    rows, columns = tall_parts.shape[2:]
    wide = jnp.stack([gate_parts, split_pieces(up), tall_parts.reshape(gate_parts.shape)], axis=2)
    shape = wide.shape[1:]
    wide = lax.psum_scatter(wide.reshape(-1, columns), "rep", scatter_dimension=0, tiled=True)
    wide = wide.reshape(shape)
    wide = sum_over_shard(wide).astype(jnp.bfloat16)
    wide = lax.all_gather(wide, "rep").astype(jnp.float32)
    tall_total = wide[:, 2].reshape(copies * rows, columns)
    return (
        join_pieces(wide[:, None, 0])[0],
        join_pieces(wide[:, None, 1])[0],
        jnp.transpose(tall_total),
    )


def reduce_attn(q, k, v, o, gain_attn, gain_mlp):
    size = lax.axis_size("shard")
    copies = lax.axis_size("rep")
    parts = split_pieces(jnp.concatenate([q, k, v, o], axis=1))
    half, columns = parts.shape[2:]
    gains = jnp.stack([gain_attn, gain_mlp]).reshape(2, size, -1).astype(jnp.bfloat16)
    rows = gains.shape[2]
    gains = jnp.pad(jnp.transpose(gains, (1, 0, 2)), ((0, 0), (0, 6), (0, columns - rows)))
    gains = jnp.broadcast_to(gains[None], (copies,) + gains.shape)
    parts = lax.psum_scatter(jnp.concatenate([parts, gains], axis=2), "rep", scatter_dimension=0)
    total = sum_over_shard(parts)
    full = spread_pieces(total[:half])
    a, b, c = q.shape[1], k.shape[1], v.shape[1]
    return (
        full[:, :a],
        full[:, a : a + b],
        full[:, a + b : a + b + c],
        full[:, a + b + c :],
        total[half, :rows],
        total[half + 1, :rows],
    )


def on_device_generic(
    block_input,
    segment_ids,
    positions,
    query_weight,
    key_weight,
    value_weight,
    output_weight,
    gate_weight,
    up_weight,
    down_weight,
    gain_attn,
    gain_mlp,
    layer_output_cotangent,
):
    weights = gather_weights(
        query_weight,
        key_weight,
        value_weight,
        output_weight,
        gate_weight,
        up_weight,
        down_weight,
        gain_attn,
        gain_mlp,
    )
    layer_result, stored = forward_pass(weights, block_input, segment_ids, positions)
    grad_mid, mlp_grads = backward_mlp(weights, layer_output_cotangent, stored)
    gate_total, up_total, down_total = reduce_mlp(*mlp_grads[:3])
    grad_in, attn_grads = backward_attention(weights, segment_ids, positions, stored, grad_mid)
    q_total, k_total, v_total, o_total, gain_attn_total, gain_mlp_total = reduce_attn(
        *attn_grads, mlp_grads[3]
    )
    return (
        layer_result.astype(jnp.bfloat16),
        grad_in,
        q_total,
        k_total,
        v_total,
        o_total,
        gate_total,
        up_total,
        down_total,
        gain_attn_total,
        gain_mlp_total,
    )


TOKENS = 384
CHUNK = 384
LANES = 128
GROUPS = KEY_VALUE_HEADS
SHARE = QUERY_HEADS // KEY_VALUE_HEADS
VMEM_LIMIT = 56 * 1024 * 1024


def dot(left, right, left_dim=1, right_dim=0):
    return lax.dot_general(
        left, right, (((left_dim,), (right_dim,)), ((), ())), preferred_element_type=jnp.float32
    )


def widen(values):
    return values.astype(jnp.float32)


def narrow(values):
    return values.astype(jnp.bfloat16)


def mask_bias(seg_row):
    shape = (TOKENS, TOKENS)
    seg_col = jnp.transpose(jnp.broadcast_to(seg_row, (LANES, TOKENS)))[:, 0:1]
    key_at = lax.broadcasted_iota(jnp.int32, shape, 0)
    query_at = lax.broadcasted_iota(jnp.int32, shape, 1)
    allowed = (key_at <= query_at) & (seg_col == seg_row)
    return jnp.where(allowed, 0.0, -1e30)


def turn(values, cosine, sine):
    half = HEAD_WIDTH // 2
    first, second = values[:half], values[half:]
    return jnp.concatenate(
        [first * cosine - second * sine, second * cosine + first * sine], axis=0
    )


def in_core_order(core, mine, pair):
    mine, pair = widen(mine), widen(pair)
    upper = jnp.where(core == 0, mine, pair)
    lower = jnp.where(core == 0, pair, mine)
    return narrow(jnp.concatenate([upper, lower], axis=0))


def attention_forward_kernel(
    shards, at_ref, x_ref, row_ref, cos_ref, sin_ref, own_ref, gain_own_ref, mine_ref,
    pair_ref, w_ref, gain_ref, x2_ref, q_ref, k_ref, v_ref, o_ref, lse_ref, bias_ref,
):
    z = at_ref[0]
    rows = own_ref.shape[0]
    half = rows // 2
    width = x_ref.shape[0]
    own_at = pl.multiple_of(z * rows, 16)
    w_ref[pl.ds(own_at, rows), :] = own_ref[...]
    gains = widen(gain_own_ref[...])
    for k in range(1, shards):
        at = pl.multiple_of(lax.rem(z + shards - k, shards) * rows, 16)
        gains = gains + widen(mine_ref[0, k - 1, half:])
        for c in range(mine_ref.shape[0]):
            to = lax.bitwise_xor(at_ref[1], c)
            w_ref[pl.ds(at, rows), c * CHUNK : (c + 1) * CHUNK] = in_core_order(
                at_ref[2], mine_ref[to, k - 1, :half], pair_ref[to, k - 1, :half]
            )
    spare = 5 * LANES - CHUNK
    gains = jnp.concatenate(
        [
            jnp.concatenate([gains[0:1], gains[1:2, :spare]], axis=1),
            jnp.concatenate([gains[2:3], gains[3:4, :spare]], axis=1),
            jnp.zeros((6, 5 * LANES), jnp.float32),
        ],
        axis=0,
    )
    turned = jnp.transpose(jnp.concatenate([gains] * (LANES // 8), axis=0))
    gain_ref[...] = turned[:width]
    x = widen(x_ref[...])
    inverse = lax.rsqrt(jnp.mean(x * x, axis=0, keepdims=True) + EPSILON)
    h1 = narrow(x * inverse * turned[:width, 0:1])
    kv = dot(w_ref[:, :CHUNK], h1, 0, 0)
    q = dot(w_ref[:, 896:], h1, 0, 0)[HEAD_WIDTH:]
    cosine, sine = cos_ref[...], sin_ref[...]
    bias_ref[...] = mask_bias(row_ref[...])
    for g in range(GROUPS):
        at = g * HEAD_WIDTH
        k_ref[g] = narrow(turn(kv[at : at + HEAD_WIDTH], cosine, sine))
        at = (GROUPS + g) * HEAD_WIDTH
        v_ref[g] = narrow(kv[at : at + HEAD_WIDTH])
        for r in range(SHARE):
            at = (g * SHARE + r) * HEAD_WIDTH
            q_ref[g, :, r * TOKENS : (r + 1) * TOKENS] = narrow(
                turn(q[at : at + HEAD_WIDTH], cosine, sine)
            )

    def one_group(g, carry):
        scores = dot(k_ref[g], q_ref[g], 0, 0) * HEAD_WIDTH ** (-0.5)
        bias = bias_ref[...]
        scores = scores + jnp.concatenate([bias] * SHARE, axis=1)
        top = jnp.max(scores, axis=0, keepdims=True)
        weight = jnp.exp(scores - top)
        total = jnp.sum(weight, axis=0, keepdims=True)
        lse_ref[g] = top + jnp.log(total)
        probs = narrow(weight * (1.0 / total))
        o_ref[g] = narrow(dot(v_ref[g], probs))
        return carry

    lax.fori_loop(0, GROUPS, one_group, 0)
    x2_ref[...] = x + dot(w_ref[:, CHUNK : CHUNK + width], joined_heads(o_ref), 0, 0)


def joined_heads(ref):
    return jnp.concatenate(
        [
            ref[g, :, r * TOKENS : (r + 1) * TOKENS]
            for g in range(GROUPS)
            for r in range(SHARE)
        ],
        axis=0,
    )


def attention_forward(at, x, row, cosine, sine, own, gain_own, mine, pair, shards):
    width = x.shape[0]
    cells = SHARE * TOKENS
    bf16, f32 = jnp.bfloat16, jnp.float32

    def kernel(*refs):
        attention_forward_kernel(shards, *refs)

    return pl.pallas_call(
        kernel,
        grid_spec=pltpu.PrefetchScalarGridSpec(
            num_scalar_prefetch=1,
            grid=(),
            in_specs=[pl.BlockSpec(memory_space=pltpu.VMEM)] * 8,
            out_specs=[pl.BlockSpec(memory_space=pltpu.VMEM)] * 8,
            scratch_shapes=[pltpu.VMEM((TOKENS, TOKENS), f32)],
        ),
        out_shape=[
            jax.ShapeDtypeStruct((shards * own.shape[0], own.shape[1]), bf16),
            jax.ShapeDtypeStruct((width, LANES), f32),
            jax.ShapeDtypeStruct((width, TOKENS), f32),
            jax.ShapeDtypeStruct((GROUPS, HEAD_WIDTH, cells), bf16),
            jax.ShapeDtypeStruct((GROUPS, HEAD_WIDTH, TOKENS), bf16),
            jax.ShapeDtypeStruct((GROUPS, HEAD_WIDTH, TOKENS), bf16),
            jax.ShapeDtypeStruct((GROUPS, HEAD_WIDTH, cells), bf16),
            jax.ShapeDtypeStruct((GROUPS, 1, cells), f32),
        ],
        compiler_params=pltpu.CompilerParams(vmem_limit_bytes=VMEM_LIMIT),
        cost_estimate=pl.CostEstimate(
            flops=int(1.5e9), bytes_accessed=8000000, transcendentals=2000000
        ),
        name="attention_forward",
    )(at, x, row, cosine, sine, own, gain_own, mine, pair)


def mlp_kernel(
    shards, at_ref, x2_ref, ctt_ref, gain_ref, gate_ref, up_ref, tall_ref, mine_ref,
    pair_ref, tall_mine_ref, tall_pair_ref,
    out_ref, dx2_ref, gain_grad_ref, keep_ref, send_ref,
    h2_ref, h2t_ref, ct_ref, acc_ref, dh2_ref, wg_ref, wu_ref, wd_ref,
    gg_ref, gu_ref, gd_ref,
):
    z, chip, core = at_ref[0], at_ref[1], at_ref[2]
    j = pl.program_id(0)
    rows = gate_ref.shape[0]
    half = rows // 2

    @pl.when(j == 0)
    def _():
        x2 = x2_ref[...]
        inverse = lax.rsqrt(jnp.mean(x2 * x2, axis=0, keepdims=True) + EPSILON)
        h2t = x2 * inverse * gain_ref[:, 1:2]
        h2t_ref[...] = narrow(h2t)
        h2_ref[...] = narrow(jnp.transpose(h2t))
        ct_ref[...] = narrow(jnp.transpose(widen(ctt_ref[...])))
        acc_ref[...] = x2
        dh2_ref[...] = jnp.zeros_like(dh2_ref)

    own_at = pl.multiple_of(z * rows, 16)
    wg_ref[pl.ds(own_at, rows), :] = gate_ref[...]
    wu_ref[pl.ds(own_at, rows), :] = up_ref[...]
    for k in range(1, shards):
        at = pl.multiple_of(lax.rem(z + shards - k, shards) * rows, 16)
        for m, ref in ((0, wg_ref), (1, wu_ref)):
            ref[pl.ds(at, rows), :] = in_core_order(
                core, mine_ref[0, k - 1, m], pair_ref[0, k - 1, m]
            )

    @pl.when(j == z)
    def _():
        wd_ref[...] = tall_ref[...]

    @pl.when(j != z)
    def _():
        for c in range(tall_mine_ref.shape[0]):
            to = lax.bitwise_xor(chip, c)
            wd_ref[c * rows : (c + 1) * rows, :] = in_core_order(
                core, tall_mine_ref[to, 0, 0], tall_pair_ref[to, 0, 0]
            )

    h2, ct = h2_ref[...], ct_ref[...]
    wg, wu, wd = wg_ref[...], wu_ref[...], wd_ref[...]
    gate, up = dot(h2, wg), dot(h2, wu)
    da = dot(ct, wd)
    sigmoid = 1.0 / (1.0 + jnp.exp(-gate))
    silu = gate * sigmoid
    act = narrow(silu * up)
    dg = narrow(da * up * sigmoid * (1.0 + gate * (1.0 - sigmoid)))
    du = narrow(da * silu)
    acc_ref[...] += dot(wd, act, 1, 1)
    dh2_ref[...] += dot(wg, dg, 1, 1) + dot(wu, du, 1, 1)
    gg_ref[...] = dot(h2t_ref[...], dg)
    gu_ref[...] = dot(h2t_ref[...], du)
    gd_ref[...] = dot(ctt_ref[...], act)
    to_chip = lax.bitwise_xor(j, chip)
    to_shard = lax.rem(j + shards - z, shards)
    for rel, ref in ((0, keep_ref), (1, send_ref)):
        to_core = lax.bitwise_xor(core, rel)
        for k in range(shards):
            at = lax.rem(z + k, shards) * rows + to_core * half
            at = pl.multiple_of(at, 8)
            ref[to_chip, k, 0] = narrow(gg_ref[pl.ds(at, half), :])
            ref[to_chip, k, 1] = narrow(gu_ref[pl.ds(at, half), :])
        for c in range(4):
            at = (2 * lax.bitwise_xor(chip, c) + to_core) * half
            at = pl.multiple_of(at, 8)
            ref[c, to_shard, 2] = narrow(gd_ref[pl.ds(at, half), :])

    @pl.when(j == pl.num_programs(0) - 1)
    def _():
        out_ref[...] = narrow(acc_ref[...])
        dh2, x2 = dh2_ref[...], x2_ref[...]
        inverse = lax.rsqrt(jnp.mean(x2 * x2, axis=0, keepdims=True) + EPSILON)
        u2 = x2 * inverse
        gain_grad = jnp.sum(dh2 * u2, axis=1, keepdims=True)
        gain_grad_ref[...] = jnp.broadcast_to(gain_grad, gain_grad_ref.shape)
        n2 = dh2 * gain_ref[:, 1:2]
        mean = jnp.mean(n2 * u2, axis=0, keepdims=True)
        dx2_ref[...] = widen(ctt_ref[...]) + inverse * (n2 - u2 * mean)


def mlp(at, x2, ct, gains, gate, up, tall, mine, pair, shards):
    width = x2.shape[0]
    copies = 2 * mine.shape[0]
    rows, ff = gate.shape
    half = rows // 2
    bf16, f32 = jnp.bfloat16, jnp.float32

    def kernel(*refs):
        mlp_kernel(shards, *refs)

    def wide_block(j, at_ref):
        return (lax.bitwise_xor(j, at_ref[1]), 0, 0, 0, 0)

    def tall_block(j, at_ref):
        return (0, jnp.maximum(lax.rem(at_ref[0] + shards - j, shards) - 1, 0), 2, 0, 0)

    whole = lambda shape: pl.BlockSpec(shape, lambda j, at_ref: (0,) * len(shape))
    return pl.pallas_call(
        kernel,
        grid_spec=pltpu.PrefetchScalarGridSpec(
            num_scalar_prefetch=1,
            grid=(ff // CHUNK,),
            in_specs=[
                whole((width, TOKENS)),
                whole((width, TOKENS)),
                whole((width, LANES)),
                pl.BlockSpec((rows, CHUNK), lambda j, at_ref: (0, j)),
                pl.BlockSpec((rows, CHUNK), lambda j, at_ref: (0, j)),
                whole((width, CHUNK)),
                pl.BlockSpec((1, shards - 1, 2, half, CHUNK), wide_block),
                pl.BlockSpec((1, shards - 1, 2, half, CHUNK), wide_block),
                pl.BlockSpec((copies // 2, 1, 1, half, CHUNK), tall_block),
                pl.BlockSpec((copies // 2, 1, 1, half, CHUNK), tall_block),
            ],
            out_specs=[
                whole((width, TOKENS)),
                whole((width, TOKENS)),
                whole((width, LANES)),
                whole((copies // 2, shards, 3, half, CHUNK)),
                whole((copies // 2, shards, 3, half, CHUNK)),
            ],
            scratch_shapes=[
                pltpu.VMEM((TOKENS, width), bf16),
                pltpu.VMEM((width, TOKENS), bf16),
                pltpu.VMEM((TOKENS, width), bf16),
                pltpu.VMEM((width, TOKENS), f32),
                pltpu.VMEM((width, TOKENS), f32),
                pltpu.VMEM((width, CHUNK), bf16),
                pltpu.VMEM((width, CHUNK), bf16),
                pltpu.VMEM((width, CHUNK), bf16),
                pltpu.VMEM((width, CHUNK), f32),
                pltpu.VMEM((width, CHUNK), f32),
                pltpu.VMEM((width, CHUNK), f32),
            ],
        ),
        out_shape=[
            jax.ShapeDtypeStruct((width, TOKENS), bf16),
            jax.ShapeDtypeStruct((width, TOKENS), f32),
            jax.ShapeDtypeStruct((width, LANES), f32),
            jax.ShapeDtypeStruct((copies // 2, shards, 3, half, CHUNK), bf16),
            jax.ShapeDtypeStruct((copies // 2, shards, 3, half, CHUNK), bf16),
        ],
        compiler_params=pltpu.CompilerParams(
            vmem_limit_bytes=VMEM_LIMIT, dimension_semantics=("arbitrary",)
        ),
        cost_estimate=pl.CostEstimate(
            flops=int(6.2e9), bytes_accessed=14000000, transcendentals=1200000
        ),
        name="mlp",
    )(at, x2, ct, gains, gate, up, tall, mine, pair, mine, pair)


def attention_backward_kernel(
    shards, at_ref, x_ref, dx2_ref, row_ref, cos_ref, sin_ref, w_ref, gain_ref, q_ref,
    k_ref, v_ref, o_ref, lse_ref, gain_grad_ref,
    dx_ref, keep_ref, send_ref,
    bias_ref, do_ref, dq_ref, dk_ref, dv_ref, grad_ref,
):
    z, chip, core = at_ref[0], at_ref[1], at_ref[2]
    width = x_ref.shape[0]
    rows = width // shards
    half = rows // 2
    x = widen(x_ref[...])
    inverse = lax.rsqrt(jnp.mean(x * x, axis=0, keepdims=True) + EPSILON)
    u1 = x * inverse
    gain_attn = gain_ref[:, 0:1]
    h1t = narrow(u1 * gain_attn)
    gx = narrow(dx2_ref[...])
    cosine, sine = cos_ref[...], sin_ref[...]
    bias_ref[...] = mask_bias(row_ref[...])
    do = narrow(dot(w_ref[:, CHUNK : CHUNK + width], gx))
    for g in range(GROUPS):
        for r in range(SHARE):
            at = (g * SHARE + r) * HEAD_WIDTH
            do_ref[g, :, r * TOKENS : (r + 1) * TOKENS] = do[at : at + HEAD_WIDTH]

    def one_group(g, carry):
        bias = bias_ref[...]
        scores = dot(k_ref[g], q_ref[g], 0, 0) * HEAD_WIDTH ** (-0.5)
        scores = scores + jnp.concatenate([bias] * SHARE, axis=1)
        probs = jnp.exp(scores - lse_ref[g])
        do_g = do_ref[g]
        dv_ref[g] = jnp.transpose(dot(narrow(probs), do_g, 1, 1))
        delta = jnp.sum(widen(do_g) * widen(o_ref[g]), axis=0, keepdims=True)
        dp = dot(v_ref[g], do_g, 0, 0)
        ds = narrow(probs * (dp - delta) * HEAD_WIDTH ** (-0.5))
        dq_ref[g] = dot(k_ref[g], ds)
        dk_ref[g] = jnp.transpose(dot(ds, q_ref[g], 1, 1))
        return carry

    lax.fori_loop(0, GROUPS, one_group, 0)
    dkv = [narrow(turn(dk_ref[g], cosine, -sine)) for g in range(GROUPS)]
    dkv = jnp.concatenate(dkv + [narrow(dv_ref[g]) for g in range(GROUPS)], axis=0)
    dq = [
        narrow(turn(dq_ref[g, :, r * TOKENS : (r + 1) * TOKENS], cosine, -sine))
        for g in range(GROUPS)
        for r in range(SHARE)
    ]
    zeros = jnp.zeros((HEAD_WIDTH, TOKENS), jnp.bfloat16)
    dq_padded = jnp.concatenate([zeros] + dq, axis=0)
    dq = jnp.concatenate(dq, axis=0)
    dh1 = dot(w_ref[:, :CHUNK], dkv) + dot(w_ref[:, 896:], dq_padded)
    gain_grad = jnp.sum(dh1 * u1, axis=1, keepdims=True)
    lane = lax.broadcasted_iota(jnp.int32, gain_grad_ref.shape, 1)
    both = jnp.transpose(jnp.where(lane == 0, gain_grad, gain_grad_ref[...]))
    gain_grad, gain_mlp_grad = both[0:1], both[1:2]
    n1 = dh1 * gain_attn
    mean = jnp.mean(n1 * u1, axis=0, keepdims=True)
    dx_ref[...] = dx2_ref[...] + inverse * (n1 - u1 * mean)
    tail = width - CHUNK
    blank = jnp.zeros((1, CHUNK - tail), jnp.float32)
    extra = jnp.concatenate(
        [
            gain_grad[:, :CHUNK],
            jnp.concatenate([gain_grad[:, CHUNK:], blank], axis=1),
            gain_mlp_grad[:, :CHUNK],
            jnp.concatenate([gain_mlp_grad[:, CHUNK:], blank], axis=1),
            jnp.zeros((4, CHUNK), jnp.float32),
        ],
        axis=0,
    )
    o = joined_heads(o_ref)
    for c in range(4):
        if c == 0:
            grad = dot(h1t, dkv, 1, 1)
        elif c == 1:
            grad = dot(o, gx[:CHUNK], 1, 1)
        elif c == 2:
            grad = jnp.concatenate(
                [dot(o, gx[CHUNK:], 1, 1), dot(h1t, dq[: CHUNK - tail], 1, 1)], axis=1
            )
        else:
            grad = dot(h1t, dq[CHUNK - tail :], 1, 1)
        grad_ref[...] = grad
        to_chip = lax.bitwise_xor(chip, c)
        for rel, ref in ((0, keep_ref), (1, send_ref)):
            for k in range(shards):
                at = lax.rem(z + k, shards) * rows + lax.bitwise_xor(core, rel) * half
                at = pl.multiple_of(at, 8)
                ref[to_chip, k] = narrow(
                    jnp.concatenate([grad_ref[pl.ds(at, half), :], extra], axis=0)
                )


def attention_backward(at, args, shards, copies):
    x = args[0]
    width = x.shape[0]
    half = width // shards // 2
    cells = SHARE * TOKENS
    bf16, f32 = jnp.bfloat16, jnp.float32

    def kernel(*refs):
        attention_backward_kernel(shards, *refs)

    return pl.pallas_call(
        kernel,
        grid_spec=pltpu.PrefetchScalarGridSpec(
            num_scalar_prefetch=1,
            grid=(),
            in_specs=[pl.BlockSpec(memory_space=pltpu.VMEM)] * len(args),
            out_specs=[pl.BlockSpec(memory_space=pltpu.VMEM)] * 3,
            scratch_shapes=[
                pltpu.VMEM((TOKENS, TOKENS), f32),
                pltpu.VMEM((GROUPS, HEAD_WIDTH, cells), bf16),
                pltpu.VMEM((GROUPS, HEAD_WIDTH, cells), f32),
                pltpu.VMEM((GROUPS, HEAD_WIDTH, TOKENS), f32),
                pltpu.VMEM((GROUPS, HEAD_WIDTH, TOKENS), f32),
                pltpu.VMEM((width, CHUNK), f32),
            ],
        ),
        out_shape=[
            jax.ShapeDtypeStruct((width, TOKENS), f32),
            jax.ShapeDtypeStruct((copies // 2, shards, half + 8, CHUNK), bf16),
            jax.ShapeDtypeStruct((copies // 2, shards, half + 8, CHUNK), bf16),
        ],
        compiler_params=pltpu.CompilerParams(vmem_limit_bytes=VMEM_LIMIT),
        cost_estimate=pl.CostEstimate(
            flops=int(3e9), bytes_accessed=9000000, transcendentals=1400000
        ),
        name="attention_backward",
    )(at, *args)


def unpack_kernel(
    at_ref, mine_ref, pair_ref, gate_ref, up_ref, tall_ref, q_ref, k_ref, v_ref, o_ref
):
    chip, core = at_ref[1], at_ref[2]
    half = mine_ref.shape[2]
    columns = []
    for c in range(mine_ref.shape[0]):
        to = lax.bitwise_xor(chip, c)
        for m in range(4):
            mine, pair = widen(mine_ref[to, m]), widen(pair_ref[to, m])
            upper = jnp.where(core == 0, mine, pair)
            lower = jnp.where(core == 0, pair, mine)
            if m < 2:
                ref = (gate_ref, up_ref)[m]
                ref[:half, c * CHUNK : (c + 1) * CHUNK] = upper
                ref[half:, c * CHUNK : (c + 1) * CHUNK] = lower
            elif m == 2:
                tall_ref[2 * c * half : (2 * c + 1) * half, :] = upper
                tall_ref[(2 * c + 1) * half : (2 * c + 2) * half, :] = lower
            else:
                columns.append(jnp.concatenate([upper, lower], axis=0))
    full = jnp.concatenate(columns, axis=1)
    kvw, width = k_ref.shape[1], o_ref.shape[1]
    k_ref[...] = full[:, :kvw]
    v_ref[...] = full[:, kvw : 2 * kvw]
    o_ref[...] = full[:, 2 * kvw : 2 * kvw + width]
    q_ref[...] = full[:, 2 * kvw + width :]


def unpack(at, mine, pair, shapes):
    return pl.pallas_call(
        unpack_kernel,
        grid_spec=pltpu.PrefetchScalarGridSpec(
            num_scalar_prefetch=1,
            grid=(),
            in_specs=[pl.BlockSpec(memory_space=pltpu.VMEM)] * 2,
            out_specs=[pl.BlockSpec(memory_space=pltpu.VMEM)] * len(shapes),
        ),
        out_shape=[jax.ShapeDtypeStruct(shape, jnp.float32) for shape in shapes],
        name="unpack",
    )(at, mine, pair)


def fits_kernels(block_input, query_weight, key_weight, gate_weight, down_weight):
    return (
        lax.axis_size("rep") == 8
        and lax.axis_size("shard") == 4
        and block_input.shape == (1, TOKENS, 576)
        and query_weight.shape == (144, 576)
        and key_weight.shape == (144, 192)
        and gate_weight.shape == (144, 1536)
        and down_weight.shape == (384, 576)
    )


def gain_rows(gain_attn, gain_mlp):
    both = jnp.zeros((2, 2 * CHUNK), jnp.bfloat16)
    at = lax.axis_index("shard") * gain_attn.shape[0]
    both = lax.dynamic_update_slice(both, jnp.stack([gain_attn, gain_mlp]), (0, at))
    return jnp.pad(both.reshape(4, CHUNK), ((0, 4), (0, 0)))


def swapped(values, bit):
    size = lax.axis_size("rep")
    return lax.ppermute(values, "rep", [(i, i ^ bit) for i in range(size)])


def plane_gather(own):
    from_x, from_y = swapped(own, 2), swapped(own, 4)
    mid = own.shape[0] // 2
    across = jnp.concatenate([swapped(from_y[:mid], 2), swapped(from_x[mid:], 4)])
    mine = jnp.stack([own, from_x, from_y, across])
    return mine, swapped(mine, 1)


def plus(left, right):
    return narrow(widen(left) + widen(right))


def exchange_one(keep, came):
    tail = keep.shape[1:]
    mid = tail[0] // 2
    keep = keep.reshape((2, 2) + tail)
    came = came.reshape((2, 2) + tail)
    a_came = swapped(plus(keep[:, 1, :mid], came[:, 1, :mid]), 2)
    b_came = swapped(plus(keep[1, :, mid:], came[1, :, mid:]), 4)
    a_keep = plus(keep[:, 0, :mid], came[:, 0, :mid])
    b_keep = plus(keep[0, :, mid:], came[0, :, mid:])
    return a_keep, b_keep, a_came, b_came


def exchange_two(a_keep, b_keep, a_came, b_came):
    a_last = swapped(plus(a_keep[1], a_came[1]), 4)
    b_last = swapped(plus(b_keep[1], b_came[1]), 2)
    return a_last, b_last


def own_blocks(a_keep, b_keep, a_came, b_came, a_last, b_last):
    a = widen(a_keep[0]) + widen(a_came[0]) + widen(a_last)
    b = widen(b_keep[0]) + widen(b_came[0]) + widen(b_last)
    return [a[i] for i in range(a.shape[0])] + [b[i] for i in range(b.shape[0])]


def exchange_shards(blocks):
    return [shifted(narrow(blocks[k]), k) for k in range(1, len(blocks))]


def added(block, came):
    for value in came:
        block = block + widen(value)
    return block


def on_device(
    block_input,
    segment_ids,
    positions,
    query_weight,
    key_weight,
    value_weight,
    output_weight,
    gate_weight,
    up_weight,
    down_weight,
    gain_attn,
    gain_mlp,
    layer_output_cotangent,
):
    if not fits_kernels(block_input, query_weight, key_weight, gate_weight, down_weight):
        return on_device_generic(
            block_input,
            segment_ids,
            positions,
            query_weight,
            key_weight,
            value_weight,
            output_weight,
            gate_weight,
            up_weight,
            down_weight,
            gain_attn,
            gain_mlp,
            layer_output_cotangent,
        )
    shards, copies = lax.axis_size("shard"), lax.axis_size("rep")
    rank = lax.axis_index("rep")
    at = jnp.stack([lax.axis_index("shard"), rank // 2, rank % 2]).astype(jnp.int32)
    barrier = lax.optimization_barrier
    own = jnp.concatenate([key_weight, value_weight, output_weight, query_weight], axis=1)
    rows = own.shape[0]
    gains_own = gain_rows(gain_attn, gain_mlp)
    attn_piece = jnp.concatenate([piece_of(own), gains_own])
    attn_came = [shifted(attn_piece, k) for k in range(1, shards)]
    tall = jnp.transpose(down_weight)
    wide = jnp.stack([piece_of(gate_weight), piece_of(up_weight), row_piece_of(tall)])
    wide_came = [shifted(wide, k) for k in range(1, shards)]
    half_dim = HEAD_WIDTH // 2
    frequency = ROPE_BASE ** (-(jnp.arange(half_dim, dtype=jnp.float32) * 2.0 / HEAD_WIDTH))
    angles = frequency[:, None] * positions.astype(jnp.float32)
    cosine, sine = jnp.cos(angles), jnp.sin(angles)
    row = segment_ids
    x = jnp.transpose(block_input[0])
    ct = jnp.transpose(layer_output_cotangent[0])
    attn_own = jnp.stack(attn_came)
    attn_x, attn_y = swapped(attn_own, 2), swapped(attn_own, 4)
    mine = jnp.stack([attn_own, attn_x, attn_y, swapped(attn_y, 2)])
    mine, wide_came, cosine, sine, at = barrier((mine, wide_came, cosine, sine, at))
    pair = swapped(mine, 1)
    wide_own = jnp.concatenate(wide_came)
    wide_x, wide_y = swapped(wide_own, 2), swapped(wide_own, 4)

    w, gains, x2, q, k, v, o, lse = attention_forward(
        at, x, row, cosine, sine, own, gains_own, mine, pair, shards
    )
    wide_x, wide_y, x2 = barrier((wide_x, wide_y, x2))
    mid = wide_own.shape[0] // 2
    across = jnp.concatenate([swapped(wide_y[:mid], 2), swapped(wide_x[mid:], 4)])
    wide_mine = jnp.stack([wide_own, wide_x, wide_y, across])
    wide_pair = swapped(wide_mine, 1)
    blocks = (-1, shards - 1, 3) + wide.shape[1:]
    wide_mine, wide_pair = wide_mine.reshape(blocks), wide_pair.reshape(blocks)
    out, dx2, gain_mlp_grad, wide_keep, wide_send = mlp(
        at, x2, ct, gains, gate_weight, up_weight, tall, wide_mine, wide_pair, shards
    )
    wide_came = swapped(wide_send, 1)
    dx, attn_keep, attn_send = attention_backward(
        at,
        (x, dx2, row, cosine, sine, w, gains, q, k, v, o, lse, gain_mlp_grad),
        shards,
        copies,
    )
    wide_one = exchange_one(wide_keep, wide_came)
    wide_one, attn_send = barrier((wide_one, attn_send))
    attn_came = swapped(attn_send, 1)
    wide_two = exchange_two(*wide_one)
    wide_two, attn_came = barrier((wide_two, attn_came))
    wide_blocks = own_blocks(*wide_one, *wide_two)
    attn_one = exchange_one(attn_keep, attn_came)
    wide_last = exchange_shards(wide_blocks)
    wide_last, attn_one = barrier((wide_last, attn_one))
    wide_total = narrow(added(wide_blocks[0], wide_last))
    attn_two = exchange_two(*attn_one)
    attn_blocks = own_blocks(*attn_one, *attn_two)
    attn_total = added(attn_blocks[0], exchange_shards(attn_blocks))
    half = rows // 2
    totals = jnp.concatenate([wide_total, narrow(attn_total[:half])[None]])
    gate_grad, up_grad, tall_grad, q_grad, k_grad, v_grad, o_grad = unpack(
        at,
        *plane_gather(totals),
        (
            gate_weight.shape,
            up_weight.shape,
            tall.shape,
            query_weight.shape,
            key_weight.shape,
            value_weight.shape,
            output_weight.shape,
        ),
    )
    both = attn_total[half : half + 4].reshape(2, 2 * CHUNK)
    both = lax.dynamic_slice(both, (0, lax.axis_index("shard") * rows), (2, rows))
    return (
        jnp.transpose(out)[None],
        jnp.transpose(dx)[None],
        q_grad,
        k_grad,
        v_grad,
        o_grad,
        gate_grad,
        up_grad,
        jnp.transpose(tall_grad),
        both[0],
        both[1],
    )


def solution(mesh):
    placed = (
        P(("rep", "shard"), None, None),
        P(("rep", "shard"), None),
        P(("rep", "shard"), None),
        P("shard", None),
        P("shard", None),
        P("shard", None),
        P("shard", None),
        P("shard", None),
        P("shard", None),
        P("shard", None),
        P("shard"),
        P("shard"),
        P(("rep", "shard"), None, None),
    )
    return jax.shard_map(
        on_device,
        mesh=mesh,
        in_specs=placed,
        out_specs=(
            P(("rep", "shard"), None, None),
            P(("rep", "shard"), None, None),
            P("shard", None),
            P("shard", None),
            P("shard", None),
            P("shard", None),
            P("shard", None),
            P("shard", None),
            P("shard", None),
            P("shard"),
            P("shard"),
        ),
        check_vma=False,
    )
```

```python
import jax
import jax.numpy as jnp
from jax import lax
from jax.experimental import pallas as pl
from jax.experimental.pallas import tpu as pltpu
from jax.sharding import PartitionSpec as P

QUERY_HEADS = 9
KEY_VALUE_HEADS = 3
HEAD_WIDTH = 64


EPSILON = 1e-05
ROPE_BASE = 100000.0


def product_term(pattern, left_op, right_op):
    return jnp.einsum(pattern, left_op, right_op, preferred_element_type=jnp.float32)


def norm_stats(values):
    inverse = lax.rsqrt(jnp.mean(values * values, axis=-1, keepdims=True) + EPSILON)
    return (inverse, values * inverse)


def rope_tables(positions):
    half_dim = HEAD_WIDTH // 2
    frequency = ROPE_BASE ** (-(jnp.arange(half_dim, dtype=jnp.float32) * 2.0 / HEAD_WIDTH))
    angles = positions.astype(jnp.float32)[:, :, None] * frequency
    return (jnp.cos(angles)[:, :, None, :], jnp.sin(angles)[:, :, None, :])


def rotate(tensor, cosine_table, sine_table, direction):
    half_dim = HEAD_WIDTH // 2
    first_half = tensor[..., :half_dim]
    second_half = tensor[..., half_dim:]
    return jnp.concatenate(
        [
            first_half * cosine_table - direction * second_half * sine_table,
            second_half * cosine_table + direction * first_half * sine_table,
        ],
        axis=-1,
    )


def attention_mask(segment_ids):
    indices = jnp.arange(segment_ids.shape[1])
    causal = indices[:, None] >= indices[None, :]
    same_doc = segment_ids[:, :, None] == segment_ids[:, None, :]
    return (causal[None] & same_doc)[:, None, None]


def score_block(q_rot, k_rot, allowed):
    scores = product_term("sqgrh,skgh->sgrqk", q_rot, k_rot) * HEAD_WIDTH ** (-0.5)
    return jnp.where(allowed, scores, -1e30)


def forward_pass(weights, block_input, segment_ids, positions):
    (
        query_weight,
        key_weight,
        value_weight,
        output_weight,
        gate_weight,
        up_weight,
        down_weight,
        gain_attn,
        gain_mlp,
    ) = weights
    sequence_count, sequence_length, width = block_input.shape
    group_size = QUERY_HEADS // KEY_VALUE_HEADS
    q_width = QUERY_HEADS * HEAD_WIDTH
    residual_input = block_input.astype(jnp.float32)
    inv_attn, unit_attn = norm_stats(residual_input)
    attention_normalized = (unit_attn * gain_attn.astype(jnp.float32)).astype(jnp.bfloat16)
    cosine_table, sine_table = rope_tables(positions)
    query_projected = product_term("ifw,wq->ifq", attention_normalized, query_weight).reshape(
        sequence_count, sequence_length, QUERY_HEADS, HEAD_WIDTH
    )
    key_projected = product_term("ifw,wq->ifq", attention_normalized, key_weight).reshape(
        sequence_count, sequence_length, KEY_VALUE_HEADS, HEAD_WIDTH
    )
    value_projected = product_term("ifw,wq->ifq", attention_normalized, value_weight).reshape(
        sequence_count, sequence_length, KEY_VALUE_HEADS, HEAD_WIDTH
    )
    q_rot = rotate(query_projected, cosine_table, sine_table, 1.0).astype(jnp.bfloat16)
    q_rot = q_rot.reshape(sequence_count, sequence_length, KEY_VALUE_HEADS, group_size, HEAD_WIDTH)
    k_rot = rotate(key_projected, cosine_table, sine_table, 1.0).astype(jnp.bfloat16)
    value_b = value_projected.astype(jnp.bfloat16)
    allowed = attention_mask(segment_ids)
    scores = score_block(q_rot, k_rot, allowed)
    row_max = jnp.max(scores, axis=-1, keepdims=True)
    log_total = row_max + jnp.log(jnp.sum(jnp.exp(scores - row_max), axis=-1, keepdims=True))
    attn_probs = jnp.exp(scores - log_total).astype(jnp.bfloat16)
    attention_merged = (
        product_term("sgrqk,skgh->sqgrh", attn_probs, value_b)
        .reshape(sequence_count, sequence_length, q_width)
        .astype(jnp.bfloat16)
    )
    residual_middle = residual_input + product_term("gwb,ba->gwa", attention_merged, output_weight)
    inv_mlp, unit_mlp = norm_stats(residual_middle)
    feedforward_normalized = (unit_mlp * gain_mlp.astype(jnp.float32)).astype(jnp.bfloat16)
    gate_projected = product_term("qbg,gh->qbh", feedforward_normalized, gate_weight)
    up_projected = product_term("qbg,gh->qbh", feedforward_normalized, up_weight)
    hidden_state = (jax.nn.silu(gate_projected) * up_projected).astype(jnp.bfloat16)
    layer_result = residual_middle + product_term("jbw,wg->jbg", hidden_state, down_weight)
    stored = (
        inv_attn,
        unit_attn,
        attention_normalized,
        q_rot,
        k_rot,
        value_b,
        log_total,
        attention_merged,
        inv_mlp,
        unit_mlp,
        feedforward_normalized,
        gate_projected,
        up_projected,
        hidden_state,
    )
    return (layer_result, stored)


def backward_mlp(weights, layer_output_cotangent, stored):
    (
        query_weight,
        key_weight,
        value_weight,
        output_weight,
        gate_weight,
        up_weight,
        down_weight,
        gain_attn,
        gain_mlp,
    ) = weights
    inv_mlp, unit_mlp, feedforward_normalized, gate_projected, up_projected, hidden_state = stored[
        8:
    ]
    grad_out = layer_output_cotangent.astype(jnp.float32)
    activation_cotangent = product_term("zeo,ho->zeh", layer_output_cotangent, down_weight)
    down_weight_gradient = product_term("bux,bue->xe", layer_output_cotangent, hidden_state)
    gate_sigmoid = jax.nn.sigmoid(gate_projected)
    gate_cotangent = (
        activation_cotangent
        * up_projected
        * gate_sigmoid
        * (1.0 + gate_projected * (1.0 - gate_sigmoid))
    ).astype(jnp.bfloat16)
    up_cotangent = (activation_cotangent * gate_projected * gate_sigmoid).astype(jnp.bfloat16)
    gate_weight_gradient = product_term("avq,avc->qc", feedforward_normalized, gate_cotangent)
    up_weight_gradient = product_term("avq,avc->qc", feedforward_normalized, up_cotangent)
    normalized_cotangent = product_term("abo,mo->abm", gate_cotangent, gate_weight) + product_term(
        "abo,mo->abm", up_cotangent, up_weight
    )
    g_gain = jnp.sum(normalized_cotangent * unit_mlp, axis=(0, 1))
    d_unit = normalized_cotangent * gain_mlp.astype(jnp.float32)
    grad_mid = grad_out + inv_mlp * (
        d_unit - unit_mlp * jnp.mean(d_unit * unit_mlp, axis=-1, keepdims=True)
    )
    return (grad_mid, (gate_weight_gradient, up_weight_gradient, down_weight_gradient, g_gain))


def backward_attention(weights, segment_ids, positions, stored, grad_mid):
    (
        query_weight,
        key_weight,
        value_weight,
        output_weight,
        gate_weight,
        up_weight,
        down_weight,
        gain_attn,
        gain_mlp,
    ) = weights
    (
        inv_attn,
        unit_attn,
        attention_normalized,
        q_rot,
        k_rot,
        value_b,
        log_total,
        attention_merged,
    ) = stored[:8]
    sequence_count, sequence_length, width = grad_mid.shape
    group_size = QUERY_HEADS // KEY_VALUE_HEADS
    q_width = QUERY_HEADS * HEAD_WIDTH
    kv_width = KEY_VALUE_HEADS * HEAD_WIDTH
    block_gradient = grad_mid.astype(jnp.bfloat16)
    output_weight_gradient = product_term("uvc,uvn->cn", attention_merged, block_gradient)
    merged_cotangent = product_term("nuw,vw->nuv", block_gradient, output_weight).astype(
        jnp.bfloat16
    )
    merged_cotangent = merged_cotangent.reshape(
        sequence_count, sequence_length, KEY_VALUE_HEADS, group_size, HEAD_WIDTH
    )
    allowed = attention_mask(segment_ids)
    scores = score_block(q_rot, k_rot, allowed)
    attn_probs = jnp.exp(scores - log_total)
    d_value = product_term("sgrqk,sqgrh->skgh", attn_probs.astype(jnp.bfloat16), merged_cotangent)
    d_prob = product_term("sqgrh,skgh->sgrqk", merged_cotangent, value_b)
    mixed_heads = attention_merged.reshape(
        sequence_count, sequence_length, KEY_VALUE_HEADS, group_size, HEAD_WIDTH
    )
    row_delta = jnp.sum(
        merged_cotangent.astype(jnp.float32) * mixed_heads.astype(jnp.float32), axis=-1
    )
    row_delta = jnp.transpose(row_delta, (0, 2, 3, 1))[..., None]
    d_score = (attn_probs * (d_prob - row_delta) * HEAD_WIDTH ** (-0.5)).astype(jnp.bfloat16)
    d_query = product_term("sgrqk,skgh->sqgrh", d_score, k_rot).reshape(
        sequence_count, sequence_length, QUERY_HEADS, HEAD_WIDTH
    )
    d_key = product_term("sgrqk,sqgrh->skgh", d_score, q_rot)
    cosine_table, sine_table = rope_tables(positions)
    query_block_cotangent = (
        rotate(d_query, cosine_table, sine_table, -1.0)
        .astype(jnp.bfloat16)
        .reshape(sequence_count, sequence_length, q_width)
    )
    key_block_cotangent = (
        rotate(d_key, cosine_table, sine_table, -1.0)
        .astype(jnp.bfloat16)
        .reshape(sequence_count, sequence_length, kv_width)
    )
    value_block_cotangent = d_value.astype(jnp.bfloat16).reshape(
        sequence_count, sequence_length, kv_width
    )
    query_weight_gradient = product_term("uxj,uxc->jc", attention_normalized, query_block_cotangent)
    key_weight_gradient = product_term("uxj,uxc->jc", attention_normalized, key_block_cotangent)
    value_weight_gradient = product_term("uxj,uxc->jc", attention_normalized, value_block_cotangent)
    normalized_cotangent = (
        product_term("vcm,tm->vct", query_block_cotangent, query_weight)
        + product_term("vcm,tm->vct", key_block_cotangent, key_weight)
        + product_term("vcm,tm->vct", value_block_cotangent, value_weight)
    )
    g_gain = jnp.sum(normalized_cotangent * unit_attn, axis=(0, 1))
    d_unit = normalized_cotangent * gain_attn.astype(jnp.float32)
    grad_in = grad_mid + inv_attn * (
        d_unit - unit_attn * jnp.mean(d_unit * unit_attn, axis=-1, keepdims=True)
    )
    return (
        grad_in,
        (
            query_weight_gradient,
            key_weight_gradient,
            value_weight_gradient,
            output_weight_gradient,
            g_gain,
        ),
    )


def shifted(values, steps):
    size = lax.axis_size("shard")
    return lax.ppermute(values, "shard", [(i, (i + steps) % size) for i in range(size)])


def piece_of(block):
    copies = lax.axis_size("rep")
    me = lax.axis_index("rep")
    rows, columns = block.shape[0] // 2, block.shape[1] // (copies // 2)
    return lax.dynamic_slice(block, ((me % 2) * rows, (me // 2) * columns), (rows, columns))


def row_piece_of(block):
    copies = lax.axis_size("rep")
    rows = block.shape[0] // copies
    return lax.dynamic_slice_in_dim(block, lax.axis_index("rep") * rows, rows, 0)


def fetch_others(piece):
    size = lax.axis_size("shard")
    return jnp.stack([shifted(piece, k) for k in range(1, size)])


def place_blocks(own, others):
    size = lax.axis_size("shard")
    me = lax.axis_index("shard")
    full = jnp.zeros((size,) + own.shape, own.dtype)
    full = lax.dynamic_update_index_in_dim(full, own, me, 0)
    for k in range(1, size):
        full = lax.dynamic_update_index_in_dim(full, others[k - 1], (me - k) % size, 0)
    return full.reshape((size * own.shape[0],) + own.shape[1:])


def join_pieces(gathered):
    copies = gathered.shape[0]
    lead, rows, columns = gathered.shape[1:]
    parts = gathered.reshape(copies // 2, 2, lead, rows, columns)
    return jnp.transpose(parts, (2, 1, 3, 0, 4)).reshape(lead, 2 * rows, copies // 2 * columns)


def split_pieces(full):
    size = lax.axis_size("shard")
    copies = lax.axis_size("rep")
    rows, columns = full.shape[0] // size // 2, full.shape[1] // (copies // 2)
    parts = full.astype(jnp.bfloat16).reshape(size, 2, rows, copies // 2, columns)
    return jnp.transpose(parts, (3, 1, 0, 2, 4)).reshape(copies, size, rows, columns)


def sum_over_shard(parts):
    size = lax.axis_size("shard")
    me = lax.axis_index("shard")
    total = lax.dynamic_index_in_dim(parts, me, 0, keepdims=False).astype(jnp.float32)
    for k in range(1, size):
        block = lax.dynamic_index_in_dim(parts, (me + k) % size, 0, keepdims=False)
        total = total + shifted(block, k).astype(jnp.float32)
    return total


def gather_weights(q, k, v, o, gate, up, down, gain_attn, gain_mlp):
    rows = q.shape[0]
    attn = jnp.concatenate([q, k, v, o], axis=1)
    attn_piece = piece_of(attn)
    gains = jnp.stack([gain_attn, gain_mlp])
    gains_pad = jnp.pad(gains, ((0, 6), (0, attn_piece.shape[1] - rows)))
    attn_others = fetch_others(jnp.concatenate([attn_piece, gains_pad]))
    half = attn_piece.shape[0]
    gains_full = place_blocks(gains, attn_others[:, half : half + 2, :rows])
    size = lax.axis_size("shard")
    gains_full = jnp.transpose(gains_full.reshape(size, 2, rows), (1, 0, 2)).reshape(2, size * rows)
    attn_gathered = lax.all_gather(attn_others[:, :half], "rep")
    attn_full = place_blocks(attn, join_pieces(attn_gathered))
    gate_piece = piece_of(gate)
    tall = jnp.transpose(down)
    tall_piece = row_piece_of(tall).reshape(gate_piece.shape)
    wide = jnp.stack([gate_piece, piece_of(up), tall_piece])
    wide_gathered = lax.all_gather(fetch_others(wide), "rep")
    gate_full = place_blocks(gate, join_pieces(wide_gathered[:, :, 0]))
    up_full = place_blocks(up, join_pieces(wide_gathered[:, :, 1]))
    tall_rows = jnp.transpose(wide_gathered[:, :, 2], (1, 0, 2, 3)).reshape((-1,) + tall.shape)
    down_full = jnp.transpose(place_blocks(down, jnp.transpose(tall_rows, (0, 2, 1))), (0, 1))
    a, b, c = q.shape[1], k.shape[1], v.shape[1]
    return (
        attn_full[:, :a],
        attn_full[:, a : a + b],
        attn_full[:, a + b : a + b + c],
        attn_full[:, a + b + c :],
        gate_full,
        up_full,
        down_full,
        gains_full[0],
        gains_full[1],
    )


def spread_pieces(piece):
    gathered = lax.all_gather(piece.astype(jnp.bfloat16), "rep")
    return join_pieces(gathered[:, None])[0].astype(jnp.float32)


def reduce_mlp(gate, up, tall):
    size = lax.axis_size("shard")
    copies = lax.axis_size("rep")
    gate_parts = split_pieces(gate)
    tall_parts = tall.astype(jnp.bfloat16).reshape(copies, tall.shape[0] // copies, size, -1)
    tall_parts = jnp.transpose(tall_parts, (0, 2, 1, 3))
    rows, columns = tall_parts.shape[2:]
    wide = jnp.stack([gate_parts, split_pieces(up), tall_parts.reshape(gate_parts.shape)], axis=2)
    shape = wide.shape[1:]
    wide = lax.psum_scatter(wide.reshape(-1, columns), "rep", scatter_dimension=0, tiled=True)
    wide = wide.reshape(shape)
    wide = sum_over_shard(wide).astype(jnp.bfloat16)
    wide = lax.all_gather(wide, "rep").astype(jnp.float32)
    tall_total = wide[:, 2].reshape(copies * rows, columns)
    return (
        join_pieces(wide[:, None, 0])[0],
        join_pieces(wide[:, None, 1])[0],
        jnp.transpose(tall_total),
    )


def reduce_attn(q, k, v, o, gain_attn, gain_mlp):
    size = lax.axis_size("shard")
    copies = lax.axis_size("rep")
    parts = split_pieces(jnp.concatenate([q, k, v, o], axis=1))
    half, columns = parts.shape[2:]
    gains = jnp.stack([gain_attn, gain_mlp]).reshape(2, size, -1).astype(jnp.bfloat16)
    rows = gains.shape[2]
    gains = jnp.pad(jnp.transpose(gains, (1, 0, 2)), ((0, 0), (0, 6), (0, columns - rows)))
    gains = jnp.broadcast_to(gains[None], (copies,) + gains.shape)
    parts = lax.psum_scatter(jnp.concatenate([parts, gains], axis=2), "rep", scatter_dimension=0)
    total = sum_over_shard(parts)
    full = spread_pieces(total[:half])
    a, b, c = q.shape[1], k.shape[1], v.shape[1]
    return (
        full[:, :a],
        full[:, a : a + b],
        full[:, a + b : a + b + c],
        full[:, a + b + c :],
        total[half, :rows],
        total[half + 1, :rows],
    )


def on_device_generic(
    block_input,
    segment_ids,
    positions,
    query_weight,
    key_weight,
    value_weight,
    output_weight,
    gate_weight,
    up_weight,
    down_weight,
    gain_attn,
    gain_mlp,
    layer_output_cotangent,
):
    weights = gather_weights(
        query_weight,
        key_weight,
        value_weight,
        output_weight,
        gate_weight,
        up_weight,
        down_weight,
        gain_attn,
        gain_mlp,
    )
    layer_result, stored = forward_pass(weights, block_input, segment_ids, positions)
    grad_mid, mlp_grads = backward_mlp(weights, layer_output_cotangent, stored)
    gate_total, up_total, down_total = reduce_mlp(*mlp_grads[:3])
    grad_in, attn_grads = backward_attention(weights, segment_ids, positions, stored, grad_mid)
    q_total, k_total, v_total, o_total, gain_attn_total, gain_mlp_total = reduce_attn(
        *attn_grads, mlp_grads[3]
    )
    return (
        layer_result.astype(jnp.bfloat16),
        grad_in,
        q_total,
        k_total,
        v_total,
        o_total,
        gate_total,
        up_total,
        down_total,
        gain_attn_total,
        gain_mlp_total,
    )


TOKENS = 384
CHUNK = 384
LANES = 128
GROUPS = KEY_VALUE_HEADS
SHARE = QUERY_HEADS // KEY_VALUE_HEADS
VMEM_LIMIT = 56 * 1024 * 1024


def dot(left, right, left_dim=1, right_dim=0):
    return lax.dot_general(
        left, right, (((left_dim,), (right_dim,)), ((), ())), preferred_element_type=jnp.float32
    )


def widen(values):
    return values.astype(jnp.float32)


def narrow(values):
    return values.astype(jnp.bfloat16)


def mask_bias(seg_row):
    shape = (TOKENS, TOKENS)
    seg_col = jnp.transpose(jnp.broadcast_to(seg_row, (LANES, TOKENS)))[:, 0:1]
    key_at = lax.broadcasted_iota(jnp.int32, shape, 0)
    query_at = lax.broadcasted_iota(jnp.int32, shape, 1)
    allowed = (key_at <= query_at) & (seg_col == seg_row)
    return jnp.where(allowed, 0.0, -1e30)


def turn(values, cosine, sine):
    half = HEAD_WIDTH // 2
    first, second = values[:half], values[half:]
    return jnp.concatenate(
        [first * cosine - second * sine, second * cosine + first * sine], axis=0
    )


def in_core_order(core, mine, pair):
    mine, pair = widen(mine), widen(pair)
    upper = jnp.where(core == 0, mine, pair)
    lower = jnp.where(core == 0, pair, mine)
    return narrow(jnp.concatenate([upper, lower], axis=0))


def attention_forward_kernel(
    shards, at_ref, x_ref, row_ref, cos_ref, sin_ref, own_ref, gain_own_ref, mine_ref,
    pair_ref, w_ref, gain_ref, x2_ref, q_ref, k_ref, v_ref, o_ref, lse_ref, bias_ref,
):
    z = at_ref[0]
    rows = own_ref.shape[0]
    half = rows // 2
    width = x_ref.shape[0]
    own_at = pl.multiple_of(z * rows, 16)
    w_ref[pl.ds(own_at, rows), :] = own_ref[...]
    gains = widen(gain_own_ref[...])
    for k in range(1, shards):
        at = pl.multiple_of(lax.rem(z + shards - k, shards) * rows, 16)
        gains = gains + widen(mine_ref[0, k - 1, half:])
        for c in range(mine_ref.shape[0]):
            to = lax.bitwise_xor(at_ref[1], c)
            w_ref[pl.ds(at, rows), c * CHUNK : (c + 1) * CHUNK] = in_core_order(
                at_ref[2], mine_ref[to, k - 1, :half], pair_ref[to, k - 1, :half]
            )
    spare = 5 * LANES - CHUNK
    gains = jnp.concatenate(
        [
            jnp.concatenate([gains[0:1], gains[1:2, :spare]], axis=1),
            jnp.concatenate([gains[2:3], gains[3:4, :spare]], axis=1),
            jnp.zeros((6, 5 * LANES), jnp.float32),
        ],
        axis=0,
    )
    turned = jnp.transpose(jnp.concatenate([gains] * (LANES // 8), axis=0))
    gain_ref[...] = turned[:width]
    x = widen(x_ref[...])
    inverse = lax.rsqrt(jnp.mean(x * x, axis=0, keepdims=True) + EPSILON)
    h1 = narrow(x * inverse * turned[:width, 0:1])
    kv = dot(w_ref[:, :CHUNK], h1, 0, 0)
    q = dot(w_ref[:, 896:], h1, 0, 0)[HEAD_WIDTH:]
    cosine, sine = cos_ref[...], sin_ref[...]
    bias_ref[...] = mask_bias(row_ref[...])
    for g in range(GROUPS):
        at = g * HEAD_WIDTH
        k_ref[g] = narrow(turn(kv[at : at + HEAD_WIDTH], cosine, sine))
        at = (GROUPS + g) * HEAD_WIDTH
        v_ref[g] = narrow(kv[at : at + HEAD_WIDTH])
        for r in range(SHARE):
            at = (g * SHARE + r) * HEAD_WIDTH
            q_ref[g, :, r * TOKENS : (r + 1) * TOKENS] = narrow(
                turn(q[at : at + HEAD_WIDTH], cosine, sine)
            )

    def one_group(g, carry):
        scores = dot(k_ref[g], q_ref[g], 0, 0) * HEAD_WIDTH ** (-0.5)
        bias = bias_ref[...]
        scores = scores + jnp.concatenate([bias] * SHARE, axis=1)
        top = jnp.max(scores, axis=0, keepdims=True)
        weight = jnp.exp(scores - top)
        total = jnp.sum(weight, axis=0, keepdims=True)
        lse_ref[g] = top + jnp.log(total)
        probs = narrow(weight * (1.0 / total))
        o_ref[g] = narrow(dot(v_ref[g], probs))
        return carry

    lax.fori_loop(0, GROUPS, one_group, 0)
    x2_ref[...] = x + dot(w_ref[:, CHUNK : CHUNK + width], joined_heads(o_ref), 0, 0)


def joined_heads(ref):
    return jnp.concatenate(
        [
            ref[g, :, r * TOKENS : (r + 1) * TOKENS]
            for g in range(GROUPS)
            for r in range(SHARE)
        ],
        axis=0,
    )


def attention_forward(at, x, row, cosine, sine, own, gain_own, mine, pair, shards):
    width = x.shape[0]
    cells = SHARE * TOKENS
    bf16, f32 = jnp.bfloat16, jnp.float32

    def kernel(*refs):
        attention_forward_kernel(shards, *refs)

    return pl.pallas_call(
        kernel,
        grid_spec=pltpu.PrefetchScalarGridSpec(
            num_scalar_prefetch=1,
            grid=(),
            in_specs=[pl.BlockSpec(memory_space=pltpu.VMEM)] * 8,
            out_specs=[pl.BlockSpec(memory_space=pltpu.VMEM)] * 8,
            scratch_shapes=[pltpu.VMEM((TOKENS, TOKENS), f32)],
        ),
        out_shape=[
            jax.ShapeDtypeStruct((shards * own.shape[0], own.shape[1]), bf16),
            jax.ShapeDtypeStruct((width, LANES), f32),
            jax.ShapeDtypeStruct((width, TOKENS), f32),
            jax.ShapeDtypeStruct((GROUPS, HEAD_WIDTH, cells), bf16),
            jax.ShapeDtypeStruct((GROUPS, HEAD_WIDTH, TOKENS), bf16),
            jax.ShapeDtypeStruct((GROUPS, HEAD_WIDTH, TOKENS), bf16),
            jax.ShapeDtypeStruct((GROUPS, HEAD_WIDTH, cells), bf16),
            jax.ShapeDtypeStruct((GROUPS, 1, cells), f32),
        ],
        compiler_params=pltpu.CompilerParams(vmem_limit_bytes=VMEM_LIMIT),
        cost_estimate=pl.CostEstimate(
            flops=int(1.5e9), bytes_accessed=8000000, transcendentals=2000000
        ),
        name="attention_forward",
    )(at, x, row, cosine, sine, own, gain_own, mine, pair)


def mlp_kernel(
    shards, at_ref, x2_ref, ctt_ref, gain_ref, gate_ref, up_ref, tall_ref, mine_ref,
    pair_ref, tall_mine_ref, tall_pair_ref,
    out_ref, dx2_ref, gain_grad_ref, keep_ref, send_ref,
    h2_ref, h2t_ref, ct_ref, acc_ref, dh2_ref, wg_ref, wu_ref, wd_ref,
    gg_ref, gu_ref, gd_ref,
):
    z, chip, core = at_ref[0], at_ref[1], at_ref[2]
    j = pl.program_id(0)
    rows = gate_ref.shape[0]
    half = rows // 2

    @pl.when(j == 0)
    def _():
        x2 = x2_ref[...]
        inverse = lax.rsqrt(jnp.mean(x2 * x2, axis=0, keepdims=True) + EPSILON)
        h2t = x2 * inverse * gain_ref[:, 1:2]
        h2t_ref[...] = narrow(h2t)
        h2_ref[...] = narrow(jnp.transpose(h2t))
        ct_ref[...] = narrow(jnp.transpose(widen(ctt_ref[...])))
        acc_ref[...] = x2
        dh2_ref[...] = jnp.zeros_like(dh2_ref)

    own_at = pl.multiple_of(z * rows, 16)
    wg_ref[pl.ds(own_at, rows), :] = gate_ref[...]
    wu_ref[pl.ds(own_at, rows), :] = up_ref[...]
    for k in range(1, shards):
        at = pl.multiple_of(lax.rem(z + shards - k, shards) * rows, 16)
        for m, ref in ((0, wg_ref), (1, wu_ref)):
            ref[pl.ds(at, rows), :] = in_core_order(
                core, mine_ref[0, k - 1, m], pair_ref[0, k - 1, m]
            )

    @pl.when(j == z)
    def _():
        wd_ref[...] = tall_ref[...]

    @pl.when(j != z)
    def _():
        for c in range(tall_mine_ref.shape[0]):
            to = lax.bitwise_xor(chip, c)
            wd_ref[c * rows : (c + 1) * rows, :] = in_core_order(
                core, tall_mine_ref[to, 0, 0], tall_pair_ref[to, 0, 0]
            )

    h2, ct = h2_ref[...], ct_ref[...]
    wg, wu, wd = wg_ref[...], wu_ref[...], wd_ref[...]
    gate, up = dot(h2, wg), dot(h2, wu)
    da = dot(ct, wd)
    sigmoid = 1.0 / (1.0 + jnp.exp(-gate))
    silu = gate * sigmoid
    act = narrow(silu * up)
    dg = narrow(da * up * sigmoid * (1.0 + gate * (1.0 - sigmoid)))
    du = narrow(da * silu)
    acc_ref[...] += dot(wd, act, 1, 1)
    dh2_ref[...] += dot(wg, dg, 1, 1) + dot(wu, du, 1, 1)
    gg_ref[...] = dot(h2t_ref[...], dg)
    gu_ref[...] = dot(h2t_ref[...], du)
    gd_ref[...] = dot(ctt_ref[...], act)
    to_chip = lax.bitwise_xor(j, chip)
    to_shard = lax.rem(j + shards - z, shards)
    for rel, ref in ((0, keep_ref), (1, send_ref)):
        to_core = lax.bitwise_xor(core, rel)
        for k in range(shards):
            at = lax.rem(z + k, shards) * rows + to_core * half
            at = pl.multiple_of(at, 8)
            ref[to_chip, k, 0] = narrow(gg_ref[pl.ds(at, half), :])
            ref[to_chip, k, 1] = narrow(gu_ref[pl.ds(at, half), :])
        for c in range(4):
            at = (2 * lax.bitwise_xor(chip, c) + to_core) * half
            at = pl.multiple_of(at, 8)
            ref[c, to_shard, 2] = narrow(gd_ref[pl.ds(at, half), :])

    @pl.when(j == pl.num_programs(0) - 1)
    def _():
        out_ref[...] = narrow(acc_ref[...])
        dh2, x2 = dh2_ref[...], x2_ref[...]
        inverse = lax.rsqrt(jnp.mean(x2 * x2, axis=0, keepdims=True) + EPSILON)
        u2 = x2 * inverse
        gain_grad = jnp.sum(dh2 * u2, axis=1, keepdims=True)
        gain_grad_ref[...] = jnp.broadcast_to(gain_grad, gain_grad_ref.shape)
        n2 = dh2 * gain_ref[:, 1:2]
        mean = jnp.mean(n2 * u2, axis=0, keepdims=True)
        dx2_ref[...] = widen(ctt_ref[...]) + inverse * (n2 - u2 * mean)


def mlp(at, x2, ct, gains, gate, up, tall, mine, pair, shards):
    width = x2.shape[0]
    copies = 2 * mine.shape[0]
    rows, ff = gate.shape
    half = rows // 2
    bf16, f32 = jnp.bfloat16, jnp.float32

    def kernel(*refs):
        mlp_kernel(shards, *refs)

    def wide_block(j, at_ref):
        return (lax.bitwise_xor(j, at_ref[1]), 0, 0, 0, 0)

    def tall_block(j, at_ref):
        return (0, jnp.maximum(lax.rem(at_ref[0] + shards - j, shards) - 1, 0), 2, 0, 0)

    whole = lambda shape: pl.BlockSpec(shape, lambda j, at_ref: (0,) * len(shape))
    return pl.pallas_call(
        kernel,
        grid_spec=pltpu.PrefetchScalarGridSpec(
            num_scalar_prefetch=1,
            grid=(ff // CHUNK,),
            in_specs=[
                whole((width, TOKENS)),
                whole((width, TOKENS)),
                whole((width, LANES)),
                pl.BlockSpec((rows, CHUNK), lambda j, at_ref: (0, j)),
                pl.BlockSpec((rows, CHUNK), lambda j, at_ref: (0, j)),
                whole((width, CHUNK)),
                pl.BlockSpec((1, shards - 1, 2, half, CHUNK), wide_block),
                pl.BlockSpec((1, shards - 1, 2, half, CHUNK), wide_block),
                pl.BlockSpec((copies // 2, 1, 1, half, CHUNK), tall_block),
                pl.BlockSpec((copies // 2, 1, 1, half, CHUNK), tall_block),
            ],
            out_specs=[
                whole((width, TOKENS)),
                whole((width, TOKENS)),
                whole((width, LANES)),
                whole((copies // 2, shards, 3, half, CHUNK)),
                whole((copies // 2, shards, 3, half, CHUNK)),
            ],
            scratch_shapes=[
                pltpu.VMEM((TOKENS, width), bf16),
                pltpu.VMEM((width, TOKENS), bf16),
                pltpu.VMEM((TOKENS, width), bf16),
                pltpu.VMEM((width, TOKENS), f32),
                pltpu.VMEM((width, TOKENS), f32),
                pltpu.VMEM((width, CHUNK), bf16),
                pltpu.VMEM((width, CHUNK), bf16),
                pltpu.VMEM((width, CHUNK), bf16),
                pltpu.VMEM((width, CHUNK), f32),
                pltpu.VMEM((width, CHUNK), f32),
                pltpu.VMEM((width, CHUNK), f32),
            ],
        ),
        out_shape=[
            jax.ShapeDtypeStruct((width, TOKENS), bf16),
            jax.ShapeDtypeStruct((width, TOKENS), f32),
            jax.ShapeDtypeStruct((width, LANES), f32),
            jax.ShapeDtypeStruct((copies // 2, shards, 3, half, CHUNK), bf16),
            jax.ShapeDtypeStruct((copies // 2, shards, 3, half, CHUNK), bf16),
        ],
        compiler_params=pltpu.CompilerParams(
            vmem_limit_bytes=VMEM_LIMIT, dimension_semantics=("arbitrary",)
        ),
        cost_estimate=pl.CostEstimate(
            flops=int(6.2e9), bytes_accessed=14000000, transcendentals=1200000
        ),
        name="mlp",
    )(at, x2, ct, gains, gate, up, tall, mine, pair, mine, pair)


def attention_backward_kernel(
    shards, at_ref, x_ref, dx2_ref, row_ref, cos_ref, sin_ref, w_ref, gain_ref, q_ref,
    k_ref, v_ref, o_ref, lse_ref, gain_grad_ref,
    dx_ref, keep_ref, send_ref,
    bias_ref, do_ref, dq_ref, dk_ref, dv_ref, grad_ref,
):
    z, chip, core = at_ref[0], at_ref[1], at_ref[2]
    width = x_ref.shape[0]
    rows = width // shards
    half = rows // 2
    x = widen(x_ref[...])
    inverse = lax.rsqrt(jnp.mean(x * x, axis=0, keepdims=True) + EPSILON)
    u1 = x * inverse
    gain_attn = gain_ref[:, 0:1]
    h1t = narrow(u1 * gain_attn)
    gx = narrow(dx2_ref[...])
    cosine, sine = cos_ref[...], sin_ref[...]
    bias_ref[...] = mask_bias(row_ref[...])
    do = narrow(dot(w_ref[:, CHUNK : CHUNK + width], gx))
    for g in range(GROUPS):
        for r in range(SHARE):
            at = (g * SHARE + r) * HEAD_WIDTH
            do_ref[g, :, r * TOKENS : (r + 1) * TOKENS] = do[at : at + HEAD_WIDTH]

    def one_group(g, carry):
        bias = bias_ref[...]
        scores = dot(k_ref[g], q_ref[g], 0, 0) * HEAD_WIDTH ** (-0.5)
        scores = scores + jnp.concatenate([bias] * SHARE, axis=1)
        probs = jnp.exp(scores - lse_ref[g])
        do_g = do_ref[g]
        dv_ref[g] = jnp.transpose(dot(narrow(probs), do_g, 1, 1))
        delta = jnp.sum(widen(do_g) * widen(o_ref[g]), axis=0, keepdims=True)
        dp = dot(v_ref[g], do_g, 0, 0)
        ds = narrow(probs * (dp - delta) * HEAD_WIDTH ** (-0.5))
        dq_ref[g] = dot(k_ref[g], ds)
        dk_ref[g] = jnp.transpose(dot(ds, q_ref[g], 1, 1))
        return carry

    lax.fori_loop(0, GROUPS, one_group, 0)
    dkv = [narrow(turn(dk_ref[g], cosine, -sine)) for g in range(GROUPS)]
    dkv = jnp.concatenate(dkv + [narrow(dv_ref[g]) for g in range(GROUPS)], axis=0)
    dq = [
        narrow(turn(dq_ref[g, :, r * TOKENS : (r + 1) * TOKENS], cosine, -sine))
        for g in range(GROUPS)
        for r in range(SHARE)
    ]
    zeros = jnp.zeros((HEAD_WIDTH, TOKENS), jnp.bfloat16)
    dq_padded = jnp.concatenate([zeros] + dq, axis=0)
    dq = jnp.concatenate(dq, axis=0)
    dh1 = dot(w_ref[:, :CHUNK], dkv) + dot(w_ref[:, 896:], dq_padded)
    gain_grad = jnp.sum(dh1 * u1, axis=1, keepdims=True)
    lane = lax.broadcasted_iota(jnp.int32, gain_grad_ref.shape, 1)
    both = jnp.transpose(jnp.where(lane == 0, gain_grad, gain_grad_ref[...]))
    gain_grad, gain_mlp_grad = both[0:1], both[1:2]
    n1 = dh1 * gain_attn
    mean = jnp.mean(n1 * u1, axis=0, keepdims=True)
    dx_ref[...] = dx2_ref[...] + inverse * (n1 - u1 * mean)
    tail = width - CHUNK
    blank = jnp.zeros((1, CHUNK - tail), jnp.float32)
    extra = jnp.concatenate(
        [
            gain_grad[:, :CHUNK],
            jnp.concatenate([gain_grad[:, CHUNK:], blank], axis=1),
            gain_mlp_grad[:, :CHUNK],
            jnp.concatenate([gain_mlp_grad[:, CHUNK:], blank], axis=1),
            jnp.zeros((4, CHUNK), jnp.float32),
        ],
        axis=0,
    )
    o = joined_heads(o_ref)
    for c in range(4):
        if c == 0:
            grad = dot(h1t, dkv, 1, 1)
        elif c == 1:
            grad = dot(o, gx[:CHUNK], 1, 1)
        elif c == 2:
            grad = jnp.concatenate(
                [dot(o, gx[CHUNK:], 1, 1), dot(h1t, dq[: CHUNK - tail], 1, 1)], axis=1
            )
        else:
            grad = dot(h1t, dq[CHUNK - tail :], 1, 1)
        grad_ref[...] = grad
        to_chip = lax.bitwise_xor(chip, c)
        for rel, ref in ((0, keep_ref), (1, send_ref)):
            for k in range(shards):
                at = lax.rem(z + k, shards) * rows + lax.bitwise_xor(core, rel) * half
                at = pl.multiple_of(at, 8)
                ref[to_chip, k] = narrow(
                    jnp.concatenate([grad_ref[pl.ds(at, half), :], extra], axis=0)
                )


def attention_backward(at, args, shards, copies):
    x = args[0]
    width = x.shape[0]
    half = width // shards // 2
    cells = SHARE * TOKENS
    bf16, f32 = jnp.bfloat16, jnp.float32

    def kernel(*refs):
        attention_backward_kernel(shards, *refs)

    return pl.pallas_call(
        kernel,
        grid_spec=pltpu.PrefetchScalarGridSpec(
            num_scalar_prefetch=1,
            grid=(),
            in_specs=[pl.BlockSpec(memory_space=pltpu.VMEM)] * len(args),
            out_specs=[pl.BlockSpec(memory_space=pltpu.VMEM)] * 3,
            scratch_shapes=[
                pltpu.VMEM((TOKENS, TOKENS), f32),
                pltpu.VMEM((GROUPS, HEAD_WIDTH, cells), bf16),
                pltpu.VMEM((GROUPS, HEAD_WIDTH, cells), f32),
                pltpu.VMEM((GROUPS, HEAD_WIDTH, TOKENS), f32),
                pltpu.VMEM((GROUPS, HEAD_WIDTH, TOKENS), f32),
                pltpu.VMEM((width, CHUNK), f32),
            ],
        ),
        out_shape=[
            jax.ShapeDtypeStruct((width, TOKENS), f32),
            jax.ShapeDtypeStruct((copies // 2, shards, half + 8, CHUNK), bf16),
            jax.ShapeDtypeStruct((copies // 2, shards, half + 8, CHUNK), bf16),
        ],
        compiler_params=pltpu.CompilerParams(vmem_limit_bytes=VMEM_LIMIT),
        cost_estimate=pl.CostEstimate(
            flops=int(3e9), bytes_accessed=9000000, transcendentals=1400000
        ),
        name="attention_backward",
    )(at, *args)


def unpack_kernel(
    at_ref, mine_ref, pair_ref, gate_ref, up_ref, tall_ref, q_ref, k_ref, v_ref, o_ref
):
    chip, core = at_ref[1], at_ref[2]
    half = mine_ref.shape[2]
    columns = []
    for c in range(mine_ref.shape[0]):
        to = lax.bitwise_xor(chip, c)
        for m in range(4):
            mine, pair = widen(mine_ref[to, m]), widen(pair_ref[to, m])
            upper = jnp.where(core == 0, mine, pair)
            lower = jnp.where(core == 0, pair, mine)
            if m < 2:
                ref = (gate_ref, up_ref)[m]
                ref[:half, c * CHUNK : (c + 1) * CHUNK] = upper
                ref[half:, c * CHUNK : (c + 1) * CHUNK] = lower
            elif m == 2:
                tall_ref[2 * c * half : (2 * c + 1) * half, :] = upper
                tall_ref[(2 * c + 1) * half : (2 * c + 2) * half, :] = lower
            else:
                columns.append(jnp.concatenate([upper, lower], axis=0))
    full = jnp.concatenate(columns, axis=1)
    kvw, width = k_ref.shape[1], o_ref.shape[1]
    k_ref[...] = full[:, :kvw]
    v_ref[...] = full[:, kvw : 2 * kvw]
    o_ref[...] = full[:, 2 * kvw : 2 * kvw + width]
    q_ref[...] = full[:, 2 * kvw + width :]


def unpack(at, mine, pair, shapes):
    return pl.pallas_call(
        unpack_kernel,
        grid_spec=pltpu.PrefetchScalarGridSpec(
            num_scalar_prefetch=1,
            grid=(),
            in_specs=[pl.BlockSpec(memory_space=pltpu.VMEM)] * 2,
            out_specs=[pl.BlockSpec(memory_space=pltpu.VMEM)] * len(shapes),
        ),
        out_shape=[jax.ShapeDtypeStruct(shape, jnp.float32) for shape in shapes],
        name="unpack",
    )(at, mine, pair)


def fits_kernels(block_input, query_weight, key_weight, gate_weight, down_weight):
    return (
        lax.axis_size("rep") == 8
        and lax.axis_size("shard") == 4
        and block_input.shape == (1, TOKENS, 576)
        and query_weight.shape == (144, 576)
        and key_weight.shape == (144, 192)
        and gate_weight.shape == (144, 1536)
        and down_weight.shape == (384, 576)
    )


def gain_rows(gain_attn, gain_mlp):
    both = jnp.zeros((2, 2 * CHUNK), jnp.bfloat16)
    at = lax.axis_index("shard") * gain_attn.shape[0]
    both = lax.dynamic_update_slice(both, jnp.stack([gain_attn, gain_mlp]), (0, at))
    return jnp.pad(both.reshape(4, CHUNK), ((0, 4), (0, 0)))


def swapped(values, bit):
    size = lax.axis_size("rep")
    return lax.ppermute(values, "rep", [(i, i ^ bit) for i in range(size)])


def plane_gather(own):
    from_x, from_y = swapped(own, 2), swapped(own, 4)
    mid = own.shape[0] // 2
    across = jnp.concatenate([swapped(from_y[:mid], 2), swapped(from_x[mid:], 4)])
    mine = jnp.stack([own, from_x, from_y, across])
    return mine, swapped(mine, 1)


def plus(left, right):
    return narrow(widen(left) + widen(right))


def exchange_one(keep, came):
    tail = keep.shape[1:]
    mid = tail[0] // 2
    keep = keep.reshape((2, 2) + tail)
    came = came.reshape((2, 2) + tail)
    a_came = swapped(plus(keep[:, 1, :mid], came[:, 1, :mid]), 2)
    b_came = swapped(plus(keep[1, :, mid:], came[1, :, mid:]), 4)
    a_keep = plus(keep[:, 0, :mid], came[:, 0, :mid])
    b_keep = plus(keep[0, :, mid:], came[0, :, mid:])
    return a_keep, b_keep, a_came, b_came


def exchange_two(a_keep, b_keep, a_came, b_came):
    a_last = swapped(plus(a_keep[1], a_came[1]), 4)
    b_last = swapped(plus(b_keep[1], b_came[1]), 2)
    return a_last, b_last


def own_blocks(a_keep, b_keep, a_came, b_came, a_last, b_last):
    a = widen(a_keep[0]) + widen(a_came[0]) + widen(a_last)
    b = widen(b_keep[0]) + widen(b_came[0]) + widen(b_last)
    return [a[i] for i in range(a.shape[0])] + [b[i] for i in range(b.shape[0])]


def exchange_shards(blocks):
    return [shifted(narrow(blocks[k]), k) for k in range(1, len(blocks))]


def added(block, came):
    for value in came:
        block = block + widen(value)
    return block


def on_device(
    block_input,
    segment_ids,
    positions,
    query_weight,
    key_weight,
    value_weight,
    output_weight,
    gate_weight,
    up_weight,
    down_weight,
    gain_attn,
    gain_mlp,
    layer_output_cotangent,
):
    if not fits_kernels(block_input, query_weight, key_weight, gate_weight, down_weight):
        return on_device_generic(
            block_input,
            segment_ids,
            positions,
            query_weight,
            key_weight,
            value_weight,
            output_weight,
            gate_weight,
            up_weight,
            down_weight,
            gain_attn,
            gain_mlp,
            layer_output_cotangent,
        )
    shards, copies = lax.axis_size("shard"), lax.axis_size("rep")
    rank = lax.axis_index("rep")
    at = jnp.stack([lax.axis_index("shard"), rank // 2, rank % 2]).astype(jnp.int32)
    barrier = lax.optimization_barrier
    own = jnp.concatenate([key_weight, value_weight, output_weight, query_weight], axis=1)
    rows = own.shape[0]
    gains_own = gain_rows(gain_attn, gain_mlp)
    attn_piece = jnp.concatenate([piece_of(own), gains_own])
    attn_came = [shifted(attn_piece, k) for k in range(1, shards)]
    tall = jnp.transpose(down_weight)
    wide = jnp.stack([piece_of(gate_weight), piece_of(up_weight), row_piece_of(tall)])
    wide_came = [shifted(wide, k) for k in range(1, shards)]
    half_dim = HEAD_WIDTH // 2
    frequency = ROPE_BASE ** (-(jnp.arange(half_dim, dtype=jnp.float32) * 2.0 / HEAD_WIDTH))
    angles = frequency[:, None] * positions.astype(jnp.float32)
    cosine, sine = jnp.cos(angles), jnp.sin(angles)
    row = segment_ids
    x = jnp.transpose(block_input[0])
    ct = jnp.transpose(layer_output_cotangent[0])
    attn_own = jnp.stack(attn_came)
    attn_x, attn_y = swapped(attn_own, 2), swapped(attn_own, 4)
    mine = jnp.stack([attn_own, attn_x, attn_y, swapped(attn_y, 2)])
    mine, wide_came, cosine, sine, at = barrier((mine, wide_came, cosine, sine, at))
    pair = swapped(mine, 1)
    wide_own = jnp.concatenate(wide_came)
    wide_x, wide_y = swapped(wide_own, 2), swapped(wide_own, 4)

    w, gains, x2, q, k, v, o, lse = attention_forward(
        at, x, row, cosine, sine, own, gains_own, mine, pair, shards
    )
    wide_x, wide_y, x2 = barrier((wide_x, wide_y, x2))
    mid = wide_own.shape[0] // 2
    across = jnp.concatenate([swapped(wide_y[:mid], 2), swapped(wide_x[mid:], 4)])
    wide_mine = jnp.stack([wide_own, wide_x, wide_y, across])
    wide_pair = swapped(wide_mine, 1)
    blocks = (-1, shards - 1, 3) + wide.shape[1:]
    wide_mine, wide_pair = wide_mine.reshape(blocks), wide_pair.reshape(blocks)
    out, dx2, gain_mlp_grad, wide_keep, wide_send = mlp(
        at, x2, ct, gains, gate_weight, up_weight, tall, wide_mine, wide_pair, shards
    )
    wide_came = swapped(wide_send, 1)
    dx, attn_keep, attn_send = attention_backward(
        at,
        (x, dx2, row, cosine, sine, w, gains, q, k, v, o, lse, gain_mlp_grad),
        shards,
        copies,
    )
    wide_one = exchange_one(wide_keep, wide_came)
    wide_one, attn_send = barrier((wide_one, attn_send))
    attn_came = swapped(attn_send, 1)
    wide_two = exchange_two(*wide_one)
    wide_two, attn_came = barrier((wide_two, attn_came))
    wide_blocks = own_blocks(*wide_one, *wide_two)
    attn_one = exchange_one(attn_keep, attn_came)
    wide_last = exchange_shards(wide_blocks)
    wide_total = narrow(added(wide_blocks[0], wide_last))
    attn_two = exchange_two(*attn_one)
    attn_blocks = own_blocks(*attn_one, *attn_two)
    attn_total = added(attn_blocks[0], exchange_shards(attn_blocks))
    half = rows // 2
    totals = jnp.concatenate([wide_total, narrow(attn_total[:half])[None]])
    gate_grad, up_grad, tall_grad, q_grad, k_grad, v_grad, o_grad = unpack(
        at,
        *plane_gather(totals),
        (
            gate_weight.shape,
            up_weight.shape,
            tall.shape,
            query_weight.shape,
            key_weight.shape,
            value_weight.shape,
            output_weight.shape,
        ),
    )
    both = attn_total[half : half + 4].reshape(2, 2 * CHUNK)
    both = lax.dynamic_slice(both, (0, lax.axis_index("shard") * rows), (2, rows))
    return (
        jnp.transpose(out)[None],
        jnp.transpose(dx)[None],
        q_grad,
        k_grad,
        v_grad,
        o_grad,
        gate_grad,
        up_grad,
        jnp.transpose(tall_grad),
        both[0],
        both[1],
    )


def solution(mesh):
    placed = (
        P(("rep", "shard"), None, None),
        P(("rep", "shard"), None),
        P(("rep", "shard"), None),
        P("shard", None),
        P("shard", None),
        P("shard", None),
        P("shard", None),
        P("shard", None),
        P("shard", None),
        P("shard", None),
        P("shard"),
        P("shard"),
        P(("rep", "shard"), None, None),
    )
    return jax.shard_map(
        on_device,
        mesh=mesh,
        in_specs=placed,
        out_specs=(
            P(("rep", "shard"), None, None),
            P(("rep", "shard"), None, None),
            P("shard", None),
            P("shard", None),
            P("shard", None),
            P("shard", None),
            P("shard", None),
            P("shard", None),
            P("shard", None),
            P("shard"),
            P("shard"),
        ),
        check_vma=False,
    )
```
